32 devices in a mesh: seq: 8 (over z, x), ch: 4 (over y, core).
Axes of the slice: x: 2, y: 2, z: 4, core: 2. Of those that a mesh axis runs over, the one named last changes fastest.
Arguments:
- stream: bfloat16 [2048, 2048], P('seq', 'ch'), may hold values from -6 to 6
- norm_gain: float32 [2048], replicated, may hold values from 0.1 to 1.9
- w_in: bfloat16 [2, 2, 2048, 4096], P(None, None, 'seq', 'ch'), may hold values from -0.125 to 0.125
- conv_w: float32 [4, 4096], P(None, 'ch'), may hold values from -3 to 3
- conv_b: float32 [4096], P('ch'), may hold values from -3 to 3
- w_xdt: bfloat16 [2, 128, 4096], P(None, 'seq', 'ch'), may hold values from -0.09375 to 0.09375
- w_xbc: bfloat16 [2, 32, 4096], P(None, None, 'ch'), may hold values from -0.25 to 0.25
- w_dt: bfloat16 [2, 128, 4096], P(None, 'seq', 'ch'), may hold values from -0.5 to 0.5
- dt_bias: float32 [2, 4096], P(None, 'ch'), may hold values from -12 to -1
- a_log: float32 [16, 4096], P(None, 'ch'), may hold values from 0 to 2.77
- d_skip: float32 [4096], P('ch'), may hold values from 0.5 to 1.5
- w_out: bfloat16 [2, 4096, 2048], P(None, 'ch', 'seq'), may hold values from -0.25 to 0.25
- cotangent: bfloat16 [2048, 2048], P('seq', 'ch'), may hold values from -6 to 6
- seg_ids: int32 [2048], replicated, may hold values from 0 to 1, as said below
- modality: int32 [2048], P('seq'), may hold values from 0 to 1, as said below
Outputs:
- output: bfloat16 [2048, 2048], P('seq', 'ch')
- grad_stream: float32 [2048, 2048], P('seq', 'ch')
- grad_gain: float32 [2048], replicated
- grad_w_in: float32 [2, 2, 2048, 4096], P(None, None, 'seq', 'ch')
- grad_conv_w: float32 [4, 4096], P(None, 'ch')
- grad_conv_b: float32 [4096], P('ch')
- grad_w_xdt: float32 [2, 128, 4096], P(None, 'seq', 'ch')
- grad_w_xbc: float32 [2, 32, 4096], P(None, None, 'ch')
- grad_w_dt: float32 [2, 128, 4096], P(None, 'seq', 'ch')
- grad_dt_bias: float32 [2, 4096], P(None, 'ch')
- grad_a_log: float32 [16, 4096], P(None, 'ch')
- grad_d_skip: float32 [4096], P('ch')
- grad_w_out: float32 [2, 4096, 2048], P(None, 'ch', 'seq')
- stats: float32 [3], replicated
The draws below stay inside these ranges and needn't reach their ends.
Inputs may be any that keep to these rules, and one draw needn't show every extreme that they name: `seg_ids`: ids never fall and both are used; one of the two sequences, which one drawn from the seed, holds fewer than 256 tokens; no sequence but the first begins at the first token of a device. `modality`: 0 marks text and 1 image tokens; every run of image tokens holds 256 tokens or more.
All inputs are finite; a program needn't handle non-finite values.
Results may differ from the reference program's by a relative error of at most 0.011.
The reference program's roundings to bfloat16 on the way count: a program that leaves them out, or rounds other values in their place, can miss the bound.
Values may be sent and summed in bfloat16 or wider, within the bound.
A program may use at most 256 MiB of HBM per device.

```python
import math
from functools import partial
import jax
import jax.numpy as jnp
from jax import lax

D = 2048
INNER = 4096
STATE = 16
CONV = 4
RANK = 128
MODS = 2
IMG = 256
BLK = 64
TOK_DEV = 256
TOKENS = 2048


def draw_seg_ids(key, part):
    key_side, key_len = jax.random.split(jax.random.fold_in(key, 11))
    side = jax.random.randint(key_side, (), 0, 2)
    short_len = jax.random.randint(key_len, (), 1, TOK_DEV)
    bound = jnp.where(side == 0, short_len, TOKENS - short_len).astype(jnp.int32)
    positions = jnp.arange(TOKENS, dtype=jnp.int32)
    return (positions >= bound).astype(jnp.int32)


def draw_modality(key, part):
    window = 8 * IMG
    groups = (TOKENS + window - 1) // window
    key_size, key_start = jax.random.split(jax.random.fold_in(key, 7))
    sizes = IMG * (1 + 3 * jax.random.randint(key_size, (groups,), 0, 2))
    offsets = jax.random.randint(key_start, (groups,), 0, window - sizes + 1)
    starts = jnp.minimum(jnp.arange(groups, dtype=jnp.int32) * window + offsets, TOKENS - sizes)
    positions = jnp.arange(TOKENS, dtype=jnp.int32)
    inside = jnp.logical_and(positions[:, None] >= starts[None, :], positions[:, None] < (starts + sizes)[None, :])
    return jnp.any(inside, axis=1).astype(jnp.int32)


def block_levels(rng, shape, shards, least, top_value):
    level, own = 1.0, jax.random.fold_in(rng, 6)
    for position, blocks in shards:
        steps = jnp.exp(jax.random.uniform(jax.random.fold_in(own, position), (blocks,), jnp.float32, least / len(shards), top_value / len(shards)))
        level = level * jnp.repeat(steps, shape[position] // blocks).reshape([-1 if axis == position else 1 for axis in range(len(shape))])
    return level


def noise(own_key, dims, spread, most, pieces=(), held_as=jnp.bfloat16):
    factor_of = block_levels(own_key, dims, pieces, -0.22, 0.18) if pieces else 1.0
    result = jax.random.normal(own_key, dims, jnp.float32) * spread * factor_of
    return jnp.minimum(jnp.maximum(result, -most), most).astype(held_as)


def setup_inputs(seed: int = 0) -> dict:
    seeds = jax.random.split(jax.random.key(seed), 16)
    return {
        "stream": noise(seeds[0], (TOKENS, D), 1.0, 6.0, ((0, 8), (1, 4))),
        "norm_gain": jnp.clip(1.0 + 0.18 * jax.random.normal(seeds[1], (D,), jnp.float32), 0.1, 1.9),
        "w_in": noise(seeds[2], (MODS, 2, D, INNER), D ** -0.5, 0.125, ((2, 8), (3, 4))),
        "conv_w": noise(seeds[3], (CONV, INNER), CONV ** -0.5, 3.0, ((1, 4),), jnp.float32),
        "conv_b": noise(seeds[4], (INNER,), 0.5, 3.0, ((0, 4),), jnp.float32),
        "w_xdt": noise(seeds[5], (MODS, RANK, INNER), INNER ** -0.5, 0.09375, ((1, 8), (2, 4))),
        "w_xbc": noise(seeds[6], (MODS, 2 * STATE, INNER), (INNER // 8) ** -0.5, 0.25, ((2, 4),)),
        "w_dt": noise(seeds[7], (MODS, RANK, INNER), RANK ** -0.5, 0.5, ((1, 8), (2, 4))),
        "dt_bias": jnp.clip(-12.0 + 11.0 * jax.random.uniform(seeds[8], (MODS, INNER), jnp.float32) ** block_levels(seeds[8], (MODS, INNER), ((1, 4),), -0.2, 0.2), -12.0, -1.0),
        "a_log": jnp.clip(2.77 * jax.random.uniform(seeds[9], (STATE, INNER), jnp.float32) ** block_levels(seeds[9], (STATE, INNER), ((1, 4),), -0.2, 0.2), 0.0, 2.77),
        "d_skip": jnp.clip(0.5 + 1.0 * jax.random.uniform(seeds[10], (INNER,), jnp.float32) ** block_levels(seeds[10], (INNER,), ((0, 4),), -0.2, 0.2), 0.5, 1.5),
        "w_out": noise(seeds[11], (MODS, INNER, D), (INNER // 8) ** -0.5, 0.25, ((1, 4), (2, 8))),
        "cotangent": noise(seeds[12], (TOKENS, D), 1.0, 6.0, ((0, 8), (1, 4))),
        "seg_ids": draw_seg_ids(jax.random.fold_in(seeds[15], 71), 0),
        "modality": draw_modality(jax.random.fold_in(seeds[15], 71), 0),
    }


EPSILON = 1e-05
PRECISE = lax.Precision.HIGHEST

@jax.custom_vjp
def low(v):
    return lax.optimization_barrier(v.astype(jnp.bfloat16)).astype(jnp.float32)

@jax.custom_vjp
def low_back(v):
    return v

def low_keep(v):
    return (low(v), None)

def low_pass(kept, grad):
    return (grad,)

def back_keep(v):
    return (v, None)

def back_low(kept, grad):
    return (low(grad),)
low.defvjp(low_keep, low_pass)
low_back.defvjp(back_keep, back_low)

def silu(value):
    return value * jax.nn.sigmoid(value)

def ssm_block(neg_a, state_in, blk_rows):

    def token_step(state_now, row):
        dt_row, u_row, b_row, c_row, keep_row = row
        state_now = keep_row * jnp.exp(dt_row[None, :] * neg_a) * state_now + b_row[:, None] * (dt_row * u_row)[None, :]
        return (state_now, lax.optimization_barrier(jnp.sum(c_row[:, None] * state_now, axis=0)))
    return lax.scan(token_step, state_in, blk_rows)

def layer_block(params, carried, blk_rows):
    norm_gain, w_in, conv_w, conv_b, w_xdt, w_xbc, w_dt, dt_bias, a_log, d_skip, w_out = params
    state_in, tail_rows, tail_seg = carried
    stream_blk, mod_blk, seg_blk = blk_rows
    length = stream_blk.shape[0]
    rim_len = CONV - 1
    sel = (mod_blk[None, :] == jnp.arange(MODS, dtype=jnp.int32)[:, None]).astype(jnp.float32)
    inv_rms = lax.rsqrt(lax.optimization_barrier(jnp.mean(stream_blk * stream_blk, axis=1, keepdims=True)) + EPSILON)
    normed = low(stream_blk * inv_rms * norm_gain[None, :])
    projected = low_back(jnp.einsum('mtd,mkde->tke', sel[:, :, None] * normed[None], w_in, precision=PRECISE))
    x_pre = low(projected[:, 0])
    gate_in = projected[:, 1]
    extended = jnp.concatenate([tail_rows, x_pre], 0)
    seg_ext = jnp.concatenate([tail_seg, seg_blk], 0)
    conv_out = conv_b[None, :] + sum((conv_w[offset][None, :] * extended[offset:offset + length] * (seg_ext[offset:offset + length] == seg_blk).astype(jnp.float32)[:, None] for offset in range(CONV)))
    u_val = low(silu(conv_out))
    u_split = sel[:, :, None] * u_val[None]
    x_dbl = low_back(jnp.concatenate([jnp.einsum('mte,mre->tr', u_split, w_xdt, precision=PRECISE), jnp.einsum('mte,mne->tn', u_split, w_xbc, precision=PRECISE)], 1))
    dt_low = low(x_dbl[:, :RANK])
    b_in = x_dbl[:, RANK:RANK + STATE]
    c_out = x_dbl[:, RANK + STATE:]
    dt_raw = low_back(jnp.einsum('mtr,mre->te', sel[:, :, None] * dt_low[None], w_dt, precision=PRECISE) + jnp.dot(sel.T, dt_bias, precision=PRECISE))
    dt_val = jax.nn.softplus(dt_raw)
    keep_mask = (seg_blk == jnp.concatenate([tail_seg[rim_len - 1:], seg_blk[:-1]])).astype(jnp.float32)
    neg_a = -jnp.exp(a_log)
    block_count = length // BLK
    scan_rows = tuple((value.reshape((block_count, BLK) + value.shape[1:]) for value in (dt_val, u_val, b_in, c_out, keep_mask)))
    state_out, y_ssm = lax.scan(jax.checkpoint(partial(ssm_block, neg_a)), state_in, scan_rows)
    y_val = y_ssm.reshape(length, INNER) + d_skip[None, :] * u_val
    gated = low(y_val * silu(gate_in))
    branch = jnp.einsum('mte,med->td', sel[:, :, None] * gated[None], w_out, precision=PRECISE)
    new_carry = (state_out, x_pre[length - rim_len:], seg_blk[length - rim_len:])
    return (new_carry, (stream_blk + branch, jnp.sum(branch * branch)))

def reference(stream, norm_gain, w_in, conv_w, conv_b, w_xdt, w_xbc, w_dt, dt_bias, a_log, d_skip, w_out, cotangent, seg_ids, modality):
    row_block = math.gcd(TOKENS, 4096)
    block_count = TOKENS // row_block

    def forward(stream_f, *params):
        start_carry = (jnp.zeros((STATE, INNER), jnp.float32), jnp.zeros((CONV - 1, INNER), jnp.float32), jnp.full((CONV - 1,), -1, jnp.int32))
        blk_rows = (stream_f.reshape(block_count, row_block, D), modality.reshape(block_count, row_block), seg_ids.reshape(block_count, row_block))
        step_fn = jax.checkpoint(lambda carried, rows_now: layer_block(params, carried, rows_now))
        _, (mixed_rows, squares) = lax.scan(step_fn, start_carry, blk_rows)
        return (mixed_rows.reshape(TOKENS, D), jnp.sum(squares))
    stream_f = stream.astype(jnp.float32)
    params = (norm_gain, w_in.astype(jnp.float32), conv_w, conv_b, w_xdt.astype(jnp.float32), w_xbc.astype(jnp.float32), w_dt.astype(jnp.float32), dt_bias, a_log, d_skip, w_out.astype(jnp.float32))
    mixed, back_fn, branch_sq = jax.vjp(forward, stream_f, *params, has_aux=True)
    grads = back_fn(cotangent.astype(jnp.float32))
    scale = float(TOKENS * D)
    stats = jnp.stack([jnp.sqrt(jnp.sum(stream_f * stream_f) / scale), jnp.sqrt(branch_sq / scale), jnp.sqrt(jnp.sum(mixed * mixed) / scale)])
    return (mixed.astype(jnp.bfloat16), grads[0], grads[1], grads[2], grads[3], grads[4], grads[5], grads[6], grads[7], grads[8], grads[9], grads[10], grads[11], stats)
```

```python
import jax
import jax.numpy as jnp
from jax import lax
from jax.experimental import pallas as pl
from jax.experimental.pallas import tpu as pltpu
from jax.sharding import PartitionSpec as P

INNER = 4096
STATE = 16
CONV = 4
BLK = 64
RANK = 128


EPSILON = 1e-05
PRECISE = lax.Precision.HIGHEST


def passed_along(value, axis, steps):
    count = lax.axis_size(axis)
    initial, last = (max(0, -steps), min(count, count - steps))
    return lax.ppermute(value, axis, [(source, source + steps) for source in range(initial, last)])


def entering(part, axis, combine, identity, reverse):
    count = lax.axis_size(axis)
    place = lax.axis_index(axis)
    ahead = count - 1 - place if reverse else place
    gathered = jax.tree.map(lambda a: lax.all_gather(a, axis), part)
    state = jax.tree.map(lambda a, e: jnp.zeros_like(a) + jnp.asarray(e, a.dtype), part, identity)

    def one(step, state):
        source = count - 1 - step if reverse else step
        return combine(
            state, jax.tree.map(lambda a: lax.dynamic_index_in_dim(a, source, 0, False), gathered)
        )

    return lax.fori_loop(0, ahead, one, state)


def silu_grad(value):
    sigma = jax.nn.sigmoid(value)
    return sigma * (1.0 + value * (1.0 - sigma))


def chain_link(earlier, latter):
    return (earlier[0] * latter[0], latter[0] * earlier[1] + latter[1])


def decay_terms(dt_blk, keep_blk, neg_a):
    return keep_blk[:, None, None] * jnp.exp(dt_blk[:, None, :] * neg_a[None])


def drive_terms(b_blk, dtu_blk):
    return b_blk[:, :, None] * dtu_blk[:, None, :]


def to_blocks(values):
    block_count = values[0].shape[0] // BLK
    return tuple((value.reshape((block_count, BLK) + value.shape[1:]) for value in values))


def run_forward(state_in, dt_val, dt_u, b_in, c_out, keep_mask, neg_a):

    def block_step(state_now, blk_rows):
        dt_blk, dtu_blk, b_blk, c_blk, keep_blk = blk_rows
        cum_a, cum_b = lax.associative_scan(
            chain_link, (decay_terms(dt_blk, keep_blk, neg_a), drive_terms(b_blk, dtu_blk))
        )
        states = cum_a * state_now[None] + cum_b
        y_blk = jnp.einsum("tn,tne->te", c_blk, states, precision=PRECISE)
        return (states[-1], (state_now, y_blk))

    state_end, (starts, y_ssm) = lax.scan(
        block_step, state_in, to_blocks((dt_val, dt_u, b_in, c_out, keep_mask))
    )
    return (state_end, starts, y_ssm.reshape(dt_val.shape))


def adjoint_states(decay, c_blk, dy_blk, incoming):
    source = c_blk[:, :, None] * dy_blk[:, None, :]
    shifted = jnp.concatenate([decay[1:], jnp.ones_like(decay[:1])], 0)
    prod_a, acc_g = lax.associative_scan(chain_link, (shifted, source), reverse=True)
    return prod_a * incoming[None] + acc_g


def local_adjoint(dt_val, c_out, keep_mask, d_y, neg_a):

    def block_step(incoming, blk_rows):
        dt_blk, c_blk, keep_blk, dy_blk = blk_rows
        decay = decay_terms(dt_blk, keep_blk, neg_a)
        adjoint = adjoint_states(decay, c_blk, dy_blk, incoming)
        return (decay[0] * adjoint[0], None)

    outgoing, _ = lax.scan(
        block_step, jnp.zeros_like(neg_a), to_blocks((dt_val, c_out, keep_mask, d_y)), reverse=True
    )
    return outgoing


def run_adjoint(incoming, starts, dt_val, dt_u, b_in, c_out, keep_mask, d_y, neg_a):

    def block_step(carried, blk_rows):
        later_in, d_neg = carried
        state_in, dt_blk, dtu_blk, b_blk, c_blk, keep_blk, dy_blk = blk_rows
        decay = decay_terms(dt_blk, keep_blk, neg_a)
        adjoint = adjoint_states(decay, c_blk, dy_blk, later_in)
        cum_a, cum_b = lax.associative_scan(chain_link, (decay, drive_terms(b_blk, dtu_blk)))
        states = cum_a * state_in[None] + cum_b
        before = jnp.concatenate([state_in[None], states[:-1]], 0)
        flow = adjoint * before * decay
        d_dt_blk = jnp.sum(flow * neg_a[None], axis=1)
        d_neg = d_neg + jnp.einsum("tne,te->ne", flow, dt_blk, precision=PRECISE)
        d_dtu_blk = jnp.einsum("tne,tn->te", adjoint, b_blk, precision=PRECISE)
        d_b_blk = jnp.einsum("tne,te->tn", adjoint, dtu_blk, precision=PRECISE)
        d_c_blk = jnp.einsum("tne,te->tn", states, dy_blk, precision=PRECISE)
        return ((decay[0] * adjoint[0], d_neg), (d_dt_blk, d_dtu_blk, d_b_blk, d_c_blk))

    blk_rows = (starts,) + to_blocks((dt_val, dt_u, b_in, c_out, keep_mask, d_y))
    (_, d_neg), outs = lax.scan(
        block_step, (incoming, jnp.zeros_like(neg_a)), blk_rows, reverse=True
    )
    length = dt_val.shape[0]
    return (d_neg,) + tuple((value.reshape((length,) + value.shape[2:]) for value in outs))


F32 = jnp.float32
BF16 = jnp.bfloat16
LANES = 128
ROWS = 256
CHUNK = 128
GROUP = 16
LOG2E = 1.4426950408889634
CUT = 1e4


def dot(a, b, da, db):
    return lax.dot_general(a, b, (((da,), (db,)), ((), ())), preferred_element_type=F32)


def column(row):
    return jnp.transpose(jnp.broadcast_to(row, (LANES, row.shape[1])))


def silu_slope(value, sigma):
    return sigma * (1.0 + value * (1.0 - sigma))


def front_kernel(
    info, x_ref, gain_ref, w_ref, cw_ref, cb_ref, wx_ref, mod_ref,
    normed_ref, xpre_ref, gate_ref, conv_ref, u_ref, part_ref, ext,
):
    i = pl.program_id(0)
    bound = info[1]

    @pl.when(i == 0)
    def _():
        ext[0:8] = jnp.zeros((8, LANES), F32)

    x = jnp.concatenate([x_ref[c] for c in range(x_ref.shape[0])], axis=1).astype(F32)
    inv = lax.rsqrt(jnp.mean(x * x, axis=1, keepdims=True) + EPSILON)
    normed = (x * inv * gain_ref[...]).astype(BF16)
    normed_ref[...] = normed
    row = mod_ref[...]
    image = column(row) > 0.5
    proj = [jnp.where(image, dot(normed, w_ref[1, k], 1, 0), dot(normed, w_ref[0, k], 1, 0)) for k in range(2)]
    x_pre = proj[0].astype(BF16)
    xpre_ref[...] = x_pre
    gate_ref[...] = proj[1]
    ext[8:] = x_pre.astype(F32)
    t = i * ROWS + lax.broadcasted_iota(jnp.int32, (ROWS, LANES), 0)
    conv = None
    for j in range(CONV):
        lag = CONV - 1 - j
        term = cw_ref[j : j + 1] * ext[8 - lag : 8 - lag + ROWS]
        if lag:
            out = (t < lag) | ((t >= bound) & (t - lag < bound))
            term = jnp.where(out, 0.0, term)
        conv = term if conv is None else conv + term
    conv = cb_ref[...] + conv
    conv_ref[...] = conv
    ext[0:8] = ext[ROWS : ROWS + 8]
    u = (conv * jax.nn.sigmoid(conv)).astype(BF16)
    u_ref[...] = u
    part_ref[...] = jnp.where(row > 0.5, dot(wx_ref[1], u, 1, 1), dot(wx_ref[0], u, 1, 1))


def forward_kernel(
    info, xt_ref, u_ref, gate_ref, mod_ref, wdt_ref, bias_ref, alog_ref, skip_ref, cot_ref, wo_ref,
    hs_ref, gated_ref, dgate_ref, dy_ref, dt_ref, sig_ref, dskip_ref,
    h_s, dta_s, dtu_s, p_s,
):
    i = pl.program_id(0)
    bound = info[1]

    @pl.when(i == 0)
    def _():
        h_s[...] = jnp.zeros_like(h_s)
        dskip_ref[...] = jnp.zeros_like(dskip_ref)

    image = column(mod_ref[...]) > 0.5
    low = xt_ref[0:RANK].astype(BF16)
    raw = jnp.where(
        image,
        dot(low, wdt_ref[1], 0, 0) + bias_ref[1:2],
        dot(low, wdt_ref[0], 0, 0) + bias_ref[0:1],
    )
    dt = jnp.maximum(raw, 0.0) + jnp.log1p(jnp.exp(-jnp.abs(raw)))
    u = u_ref[...].astype(F32)
    t = i * CHUNK + lax.broadcasted_iota(jnp.int32, (CHUNK, LANES), 0)
    dt_ref[...] = dt
    sig_ref[...] = jax.nn.sigmoid(raw)
    dta_s[...] = jnp.where((t == 0) | (t == bound), CUT, dt)
    dtu_s[...] = dt * u
    rate = -jnp.exp(alog_ref[...]) * LOG2E
    b_all = xt_ref[RANK : RANK + STATE]
    c_all = xt_ref[RANK + STATE : RANK + 2 * STATE]

    def group(g, h):
        turn = lax.rem(CHUNK - GROUP * g, CHUNK)
        b_now = pltpu.roll(b_all, turn, 1)
        c_now = pltpu.roll(c_all, turn, 1)
        base = pl.multiple_of(g * GROUP, GROUP)
        for k in range(GROUP):
            decay = jnp.exp2(dta_s[pl.ds(base + k, 1)] * rate)
            h = decay * h + b_now[:, k : k + 1] * dtu_s[pl.ds(base + k, 1)]
            hs_ref[base + k] = h
            made = c_now[:, k : k + 1] * h
            p_s[base + k] = made[0:8] + made[8:16]
        return h

    h_s[...] = lax.fori_loop(0, CHUNK // GROUP, group, h_s[...])
    y = jnp.sum(p_s[...], axis=1) + skip_ref[...] * u
    gate = gate_ref[...]
    sigma = jax.nn.sigmoid(gate)
    gated_ref[...] = (y * (gate * sigma)).astype(BF16)
    cot = jnp.concatenate([cot_ref[c] for c in range(cot_ref.shape[0])], axis=1)
    d_gated = jnp.where(image, dot(cot, wo_ref[1], 1, 1), dot(cot, wo_ref[0], 1, 1))
    d_y = d_gated * gate * sigma
    dy_ref[...] = d_y
    dgate_ref[...] = (d_gated * y * silu_slope(gate, sigma)).astype(BF16)
    dskip_ref[...] += jnp.sum(d_y * u, axis=0, keepdims=True)


def adjoint_kernel(
    info, xt_ref, hs_ref, hp_ref, u_ref, dy_ref, dt_ref, sig_ref, mod_ref, wdt_ref, alog_ref, skip_ref,
    part_ref, du_ref, dwdt_ref, dbias_ref, dalog_ref,
    ga_s, dn_s, dta_s, dtu_s, pu_s, pd_s,
):
    j = pl.program_id(0)
    i = pl.num_programs(0) - 1 - j
    bound = info[1]

    @pl.when(j == 0)
    def _():
        ga_s[...] = jnp.zeros_like(ga_s)
        dn_s[...] = jnp.zeros_like(dn_s)
        dwdt_ref[...] = jnp.zeros_like(dwdt_ref)
        dbias_ref[...] = jnp.zeros_like(dbias_ref)

    dt = dt_ref[...]
    u = u_ref[...].astype(F32)
    t = i * CHUNK + lax.broadcasted_iota(jnp.int32, (CHUNK, LANES), 0)
    dta_s[...] = jnp.where((t == 0) | (t == bound), CUT, dt)
    dtu_s[...] = dt * u
    neg_a = -jnp.exp(alog_ref[...])
    rate = neg_a * LOG2E
    b_all = xt_ref[RANK : RANK + STATE]
    c_all = xt_ref[RANK + STATE : RANK + 2 * STATE]
    lane = lax.broadcasted_iota(jnp.int32, (STATE, LANES), 1)
    h_first = hp_ref[0]
    zero = jnp.zeros((STATE, LANES), F32)

    def group(step, carried):
        h, ga, dn, db_all, dc_all = carried
        g = CHUNK // GROUP - 1 - step
        turn = lax.rem(CHUNK - GROUP * g, CHUNK)
        b_now = pltpu.roll(b_all, turn, 1)
        c_now = pltpu.roll(c_all, turn, 1)
        base = pl.multiple_of(g * GROUP, GROUP)
        db, dc = zero, zero
        for k in reversed(range(GROUP)):
            if k:
                before = hs_ref[base + k - 1]
            else:
                before = jnp.where(g == 0, h_first, hs_ref[jnp.maximum(base - 1, 0)])
            decay = jnp.exp2(dta_s[pl.ds(base + k, 1)] * rate)
            d_y = dy_ref[pl.ds(base + k, 1)]
            adjoint = c_now[:, k : k + 1] * d_y + ga
            dc = jnp.where(lane == k, jnp.sum(d_y * h, axis=1, keepdims=True), dc)
            db = jnp.where(lane == k, jnp.sum(adjoint * dtu_s[pl.ds(base + k, 1)], axis=1, keepdims=True), db)
            drive = adjoint * b_now[:, k : k + 1]
            pu_s[base + k] = drive[0:8] + drive[8:16]
            ga = decay * adjoint
            flow = ga * before
            slow = flow * neg_a
            pd_s[base + k] = slow[0:8] + slow[8:16]
            dn = dn + flow * dt_ref[pl.ds(base + k, 1)]
            h = before
        back = GROUP * g
        return (h, ga, dn, db_all + pltpu.roll(db, back, 1), dc_all + pltpu.roll(dc, back, 1))

    _, ga, dn, db_all, dc_all = lax.fori_loop(
        0, CHUNK // GROUP, group, (hs_ref[CHUNK - 1], ga_s[...], dn_s[...], zero, zero)
    )
    ga_s[...] = ga
    dn_s[...] = dn
    d_dtu = jnp.sum(pu_s[...], axis=1)
    d_dt = jnp.sum(pd_s[...], axis=1) + d_dtu * u
    du_ref[...] = dy_ref[...] * skip_ref[...] + d_dtu * dt
    d_raw = (d_dt * sig_ref[...]).astype(BF16)
    row = mod_ref[...]
    image = column(row) > 0.5
    low = xt_ref[0:RANK].astype(BF16)
    part_ref[0:RANK] = jnp.where(row > 0.5, dot(wdt_ref[1], d_raw, 1, 1), dot(wdt_ref[0], d_raw, 1, 1))
    part_ref[RANK : RANK + STATE] = db_all
    part_ref[RANK + STATE : RANK + 2 * STATE] = dc_all
    raw_f = d_raw.astype(F32)
    for m in range(2):
        own = jnp.where(image == (m == 1), raw_f, 0.0)
        dwdt_ref[m] += dot(low, own.astype(BF16), 1, 0)
        dbias_ref[m : m + 1] += jnp.sum(own, axis=0, keepdims=True)

    @pl.when(j == pl.num_programs(0) - 1)
    def _():
        dalog_ref[...] = neg_a * dn


def rear_kernel(
    info, dx_ref, du_ref, u_ref, conv_ref, xpre_ref, tail_ref, mod_ref, wx_ref, cw_ref,
    dpre_ref, dwx_ref, dconv_ref, ext, ahead,
):
    j = pl.program_id(0)
    i = pl.num_programs(0) - 1 - j
    bound = info[1]

    @pl.when(j == 0)
    def _():
        ahead[...] = jnp.zeros_like(ahead)
        dwx_ref[...] = jnp.zeros_like(dwx_ref)
        dconv_ref[...] = jnp.zeros_like(dconv_ref)

    row = mod_ref[...]
    image = column(row) > 0.5
    dx = dx_ref[...].astype(BF16)
    u = u_ref[...]
    d_u = du_ref[...] + jnp.where(image, dot(dx, wx_ref[1], 0, 0), dot(dx, wx_ref[0], 0, 0))
    u_f = u.astype(F32)
    for m in range(2):
        own = jnp.where(image == (m == 1), u_f, 0.0).astype(BF16)
        dwx_ref[m] += dot(dx, own, 1, 0)
    conv = conv_ref[...]
    d_conv = d_u * silu_slope(conv, jax.nn.sigmoid(conv))
    ext[0:8] = tail_ref[...].astype(F32)[-8:]
    ext[8:] = xpre_ref[...].astype(F32)
    ahead[ROWS : ROWS + 8] = ahead[0:8]
    ahead[0:ROWS] = d_conv
    t = i * ROWS + lax.broadcasted_iota(jnp.int32, (ROWS, LANES), 0)
    d_pre = None
    for tap in range(CONV):
        lag = CONV - 1 - tap
        seen = ext[8 - lag : 8 - lag + ROWS] * d_conv
        term = cw_ref[tap : tap + 1] * ahead[lag : lag + ROWS]
        if lag:
            seen = jnp.where((t < lag) | ((t >= bound) & (t - lag < bound)), 0.0, seen)
            term = jnp.where((t < bound) & (t + lag >= bound), 0.0, term)
        dconv_ref[tap : tap + 1] += jnp.sum(seen, axis=0, keepdims=True)
        d_pre = term if d_pre is None else d_pre + term
    dconv_ref[CONV : CONV + 1] += jnp.sum(d_conv, axis=0, keepdims=True)
    dpre_ref[...] = d_pre.astype(BF16)


def out_kernel(info, gated_ref, cot_ref, mod_ref, wo_ref, branch_ref, dwo_ref):
    i = pl.program_id(0)

    @pl.when(i == 0)
    def _():
        dwo_ref[...] = jnp.zeros_like(dwo_ref)

    gated = gated_ref[...]
    cot = cot_ref[0].astype(F32)
    image = column(mod_ref[...]) > 0.5
    image = jnp.concatenate([image] * (cot.shape[1] // LANES), axis=1)
    branch_ref[...] = jnp.where(image, dot(gated, wo_ref[1], 1, 0), dot(gated, wo_ref[0], 1, 0))
    for m in range(2):
        own = jnp.where(image == (m == 1), cot, 0.0).astype(BF16)
        dwo_ref[m] += dot(gated, own, 0, 0)


def in_grad_kernel(info, normed_ref, dz_ref, mod_ref, wi_ref, *rest):
    added_ref = rest[0] if len(rest) == 3 else None
    dnorm_ref, dwi_ref = rest[-2:]
    i = pl.program_id(0)

    @pl.when(i == 0)
    def _():
        dwi_ref[...] = jnp.zeros_like(dwi_ref)

    dz = dz_ref[...]
    normed = normed_ref[...].astype(F32)
    image = column(mod_ref[...]) > 0.5
    image = jnp.concatenate([image] * (normed.shape[1] // LANES), axis=1)
    total = jnp.where(image, dot(dz, wi_ref[1, 0], 1, 1), dot(dz, wi_ref[0, 0], 1, 1))
    dnorm_ref[...] = total if added_ref is None else added_ref[...] + total
    for m in range(2):
        own = jnp.where(image == (m == 1), normed, 0.0).astype(BF16)
        dwi_ref[m, 0] += dot(own, dz, 0, 0)


def call(kernel, info, grid, ins, outs, scratch, name, flops, moved):
    specs = [spec for _, spec in ins]
    return pl.pallas_call(
        kernel,
        out_shape=[jax.ShapeDtypeStruct(shape, dtype) for shape, dtype, _ in outs],
        grid_spec=pltpu.PrefetchScalarGridSpec(
            num_scalar_prefetch=1,
            grid=(grid,),
            in_specs=specs,
            out_specs=[spec for _, _, spec in outs],
            scratch_shapes=scratch,
        ),
        compiler_params=pltpu.CompilerParams(
            dimension_semantics=("arbitrary",), vmem_limit_bytes=56 * 2**20
        ),
        cost_estimate=pl.CostEstimate(flops=flops, bytes_accessed=moved, transcendentals=0),
        name=name,
    )(info, *[array for array, _ in ins])


def fixed(*block):
    zeros = (0,) * len(block)
    return pl.BlockSpec(block, lambda i, info: zeros)


def per_device(
    stream, norm_gain, w_in, conv_w, conv_b, w_xdt, w_xbc, w_dt, dt_bias, a_log, d_skip, w_out,
    cotangent, seg_ids, modality,
):
    seqs, chs = lax.axis_size("seq"), lax.axis_size("ch")
    s = lax.axis_index("seq")
    rows, cols = stream.shape
    tokens, width = seg_ids.shape[0], norm_gain.shape[0]
    channels = conv_b.shape[0]
    own = channels // seqs
    part = width // seqs
    folds = seqs // chs
    n_rows, n_chunks = tokens // ROWS, tokens // CHUNK
    info = jnp.stack([s, jnp.sum(seg_ids == 0)]).astype(jnp.int32)

    x_all = lax.all_gather(stream, ("seq", "ch"))
    cot_all = lax.all_gather(cotangent, ("seq", "ch"))
    wi = lax.all_to_all(w_in, "seq", 3, 2, tiled=True)
    wo = lax.all_to_all(w_out, "seq", 1, 2, tiled=True)
    wdt = lax.all_to_all(w_dt, "seq", 2, 1, tiled=True)
    wxdt = lax.all_to_all(w_xdt, "seq", 2, 1, tiled=True)
    wx = jnp.concatenate([wxdt, lax.dynamic_slice_in_dim(w_xbc, s * own, own, 2)], 1)
    mod = lax.all_gather(modality, "seq", tiled=True).astype(F32)[None]

    def mine(*lead):
        zeros = (0,) * len(lead)
        return pl.BlockSpec(lead + (own,), lambda i, info: zeros + (info[0],))

    def down(block, *lead):
        zeros = (0,) * len(lead)
        return pl.BlockSpec(lead + (block,), lambda i, info: zeros + (i,))

    def over(block, last, flip=None):
        if flip is None:
            return pl.BlockSpec((block, last), lambda i, info: (i, 0))
        return pl.BlockSpec((block, last), lambda i, info: (flip - 1 - i, 0))

    tall = jax.ShapeDtypeStruct
    half = ROWS // CHUNK
    normed, x_pre, gate, conv, u, xt = call(
        front_kernel, info, n_rows,
        [
            (x_all, pl.BlockSpec((chs, rows, cols), lambda i, info: (i, 0, 0))),
            (norm_gain[None], fixed(1, width)),
            (wi, fixed(2, 2, width, own)),
            (conv_w, mine(CONV)),
            (conv_b[None], mine(1)),
            (wx, fixed(2, RANK + 2 * STATE, own)),
            (mod, down(ROWS, 1)),
        ],
        [
            ((tokens, width), BF16, over(ROWS, width)),
            ((tokens, own), BF16, over(ROWS, own)),
            ((tokens, own), F32, over(ROWS, own)),
            ((tokens, own), F32, over(ROWS, own)),
            ((tokens, own), BF16, over(ROWS, own)),
            ((RANK + 2 * STATE, tokens), F32, down(ROWS, RANK + 2 * STATE)),
        ],
        [pltpu.VMEM((ROWS + 8, own), F32)],
        "front", 8 * tokens * width * own, 24 << 20,
    )
    xt = lax.psum(xt, ("seq", "ch"))
    hs, gated, d_gate, d_y, dt, sig, d_skip_own = call(
        forward_kernel, info, n_chunks,
        [
            (xt, down(CHUNK, RANK + 2 * STATE)),
            (u, over(CHUNK, own)),
            (gate, over(CHUNK, own)),
            (mod, down(CHUNK, 1)),
            (wdt, fixed(2, RANK, own)),
            (dt_bias, mine(2)),
            (a_log, mine(STATE)),
            (d_skip[None], mine(1)),
            (cot_all, pl.BlockSpec((chs, CHUNK, cols), lambda i, info: (i // half, i % half, 0))),
            (wo, fixed(2, own, width)),
        ],
        [
            ((tokens, STATE, own), F32, pl.BlockSpec((CHUNK, STATE, own), lambda i, info: (i, 0, 0))),
            ((tokens, own), BF16, over(CHUNK, own)),
            ((tokens, own), BF16, over(CHUNK, own)),
            ((tokens, own), F32, over(CHUNK, own)),
            ((tokens, own), F32, over(CHUNK, own)),
            ((tokens, own), F32, over(CHUNK, own)),
            ((1, own), F32, fixed(1, own)),
        ],
        [
            pltpu.VMEM((STATE, own), F32),
            pltpu.VMEM((CHUNK, own), F32),
            pltpu.VMEM((CHUNK, own), F32),
            pltpu.VMEM((CHUNK, 8, own), F32),
        ],
        "forward", 4 * tokens * width * own, 32 << 20,
    )
    gated_all = lax.all_gather(gated, "seq", axis=1, tiled=True)
    d_gate_all = lax.all_gather(d_gate, "seq", axis=1, tiled=True)

    last = n_chunks - 1

    def back(block, *lead):
        zeros = (0,) * len(lead)
        return pl.BlockSpec(lead + (block,), lambda i, info: zeros + (tokens // block - 1 - i,))

    flip = n_chunks
    dxt, d_u, d_w_dt, d_bias, d_a_log = call(
        adjoint_kernel, info, n_chunks,
        [
            (xt, back(CHUNK, RANK + 2 * STATE)),
            (hs, pl.BlockSpec((CHUNK, STATE, own), lambda i, info: (last - i, 0, 0))),
            (hs, pl.BlockSpec((1, STATE, own), lambda i, info: (jnp.maximum((last - i) * CHUNK - 1, 0), 0, 0))),
            (u, over(CHUNK, own, flip)),
            (d_y, over(CHUNK, own, flip)),
            (dt, over(CHUNK, own, flip)),
            (sig, over(CHUNK, own, flip)),
            (mod, back(CHUNK, 1)),
            (wdt, fixed(2, RANK, own)),
            (a_log, mine(STATE)),
            (d_skip[None], mine(1)),
        ],
        [
            ((RANK + 2 * STATE, tokens), F32, back(CHUNK, RANK + 2 * STATE)),
            ((tokens, own), F32, over(CHUNK, own, flip)),
            ((2, RANK, own), F32, fixed(2, RANK, own)),
            ((2, own), F32, fixed(2, own)),
            ((STATE, own), F32, fixed(STATE, own)),
        ],
        [
            pltpu.VMEM((STATE, own), F32),
            pltpu.VMEM((STATE, own), F32),
            pltpu.VMEM((CHUNK, own), F32),
            pltpu.VMEM((CHUNK, own), F32),
            pltpu.VMEM((CHUNK, 8, own), F32),
            pltpu.VMEM((CHUNK, 8, own), F32),
        ],
        "adjoint", 8 * tokens * RANK * own, 32 << 20,
    )
    dxt = lax.psum(dxt, ("seq", "ch"))
    top = n_rows - 1
    d_pre, d_wx, d_conv = call(
        rear_kernel, info, n_rows,
        [
            (dxt, back(ROWS, RANK + 2 * STATE)),
            (d_u, over(ROWS, own, n_rows)),
            (u, over(ROWS, own, n_rows)),
            (conv, over(ROWS, own, n_rows)),
            (x_pre, over(ROWS, own, n_rows)),
            (x_pre, pl.BlockSpec((16, own), lambda i, info: (jnp.maximum((top - i) * (ROWS // 16) - 1, 0), 0))),
            (mod, back(ROWS, 1)),
            (wx, fixed(2, RANK + 2 * STATE, own)),
            (conv_w, mine(CONV)),
        ],
        [
            ((tokens, own), BF16, over(ROWS, own, n_rows)),
            ((2, RANK + 2 * STATE, own), F32, fixed(2, RANK + 2 * STATE, own)),
            ((8, own), F32, fixed(8, own)),
        ],
        [pltpu.VMEM((ROWS + 8, own), F32), pltpu.VMEM((ROWS + 8, own), F32)],
        "rear", 16 * tokens * RANK * own, 8 << 20,
    )
    d_pre_all = lax.all_gather(d_pre, "seq", axis=1, tiled=True)

    cot_slice = pl.BlockSpec((1, rows, part), lambda i, info: (i * chs + info[0] // folds, 0, info[0] % folds))
    branch_part, own_w_out = call(
        out_kernel, info, n_rows,
        [
            (gated_all, over(ROWS, channels)),
            (cot_all, cot_slice),
            (mod, down(ROWS, 1)),
            (w_out, fixed(2, channels, part)),
        ],
        [
            ((tokens, part), F32, over(ROWS, part)),
            ((2, channels, part), F32, fixed(2, channels, part)),
        ],
        [], "out", 8 * tokens * channels * part, 12 << 20,
    )

    def in_grad(k, dz, *more):
        outs = [
            jax.ShapeDtypeStruct((tokens, part), F32),
            jax.ShapeDtypeStruct(w_in.shape, F32),
        ]
        ins = [
            (normed, pl.BlockSpec((ROWS, part), lambda i, info: (i, info[0]))),
            (dz, over(ROWS, channels)),
            (mod, down(ROWS, 1)),
            (w_in, pl.BlockSpec((2, 1, part, channels), lambda i, info: (0, k, 0, 0))),
        ]
        kernel, alias = in_grad_kernel, {}
        if more:
            ins += [(more[0], over(ROWS, part)), (more[1], pl.BlockSpec(memory_space=pl.ANY))]
            alias = {6: 1}

            def kernel(info, a, b, c, d, added, held, *rest):
                in_grad_kernel(info, a, b, c, d, added, *rest)

        return pl.pallas_call(
            kernel,
            out_shape=outs,
            grid_spec=pltpu.PrefetchScalarGridSpec(
                num_scalar_prefetch=1,
                grid=(n_rows,),
                in_specs=[spec for _, spec in ins],
                out_specs=[over(ROWS, part), pl.BlockSpec((2, 1, part, channels), lambda i, info: (0, k, 0, 0))],
            ),
            input_output_aliases=alias,
            compiler_params=pltpu.CompilerParams(
                dimension_semantics=("arbitrary",), vmem_limit_bytes=56 * 2**20
            ),
            cost_estimate=pl.CostEstimate(
                flops=8 * tokens * channels * part, bytes_accessed=12 << 20, transcendentals=0
            ),
            name="in_grad",
        )(info, *[array for array, _ in ins])

    first = in_grad(1, d_gate_all)
    d_norm_part, own_w_in = in_grad(0, d_pre_all, *first)

    def regroup(value):
        value = lax.all_to_all(value, "seq", 0, 1, tiled=True)
        return lax.psum_scatter(value, "ch", scatter_dimension=1, tiled=True)

    branch = regroup(branch_part)
    d_norm = regroup(d_norm_part)
    x_own = stream.astype(F32)
    col = lax.axis_index("ch") * cols
    mixed = x_own + branch
    output = mixed.astype(BF16)
    squares = lax.psum(jnp.sum(x_own * x_own, axis=1), "ch")
    inv_rms = lax.rsqrt(squares / width + EPSILON)[:, None]
    x_hat = x_own * inv_rms
    d_hat = d_norm * lax.dynamic_slice_in_dim(norm_gain, col, cols)[None]
    inner = lax.psum(jnp.sum(d_hat * x_hat, axis=1), "ch")[:, None] / width
    grad_stream = cotangent.astype(F32) + inv_rms * (d_hat - x_hat * inner)
    gain_part = lax.dynamic_update_slice_in_dim(
        jnp.zeros((width,), F32), jnp.sum(d_norm * x_hat, axis=0), col, 0
    )
    stats_part = jnp.stack([jnp.sum(x_own * x_own), jnp.sum(branch * branch), jnp.sum(mixed * mixed)])
    gain, stats = lax.psum((gain_part, stats_part), ("seq", "ch"))
    small = jnp.concatenate(
        [d_conv, d_bias, d_a_log, d_skip_own, jnp.zeros((5, own), F32), d_wx[0, RANK:], d_wx[1, RANK:]], 0
    )
    small = lax.all_gather(small, "seq", axis=1, tiled=True)
    split = lax.all_to_all(jnp.stack([d_wx[:, :RANK], d_w_dt]), "seq", 2, 3, tiled=True)
    return (
        output,
        grad_stream,
        gain,
        own_w_in,
        small[:CONV],
        small[CONV],
        split[0],
        small[32:].reshape(w_xbc.shape),
        split[1],
        small[8:10],
        small[10:26],
        small[26],
        own_w_out,
        jnp.sqrt(stats / float(tokens * width)),
    )


def per_device_by_token(
    stream,
    norm_gain,
    w_in,
    conv_w,
    conv_b,
    w_xdt,
    w_xbc,
    w_dt,
    dt_bias,
    a_log,
    d_skip,
    w_out,
    cotangent,
    seg_ids,
    modality,
):
    length = stream.shape[0]
    channels = conv_b.shape[0]
    model_width = norm_gain.shape[0]
    mod_count = w_in.shape[0]
    rim_len = CONV - 1
    ch_start = lax.axis_index("ch") * channels
    col_start = lax.axis_index("ch") * stream.shape[1]
    x_full, grad_full = (
        lax.all_gather(stream, "ch", axis=1, tiled=True),
        lax.all_gather(cotangent, "ch", axis=1, tiled=True),
    )
    w_in_full, w_xdt_full, w_dt_full, w_out_full = (
        lax.all_gather(w_in, "seq", axis=2, tiled=True),
        lax.all_gather(w_xdt, "seq", axis=1, tiled=True),
        lax.all_gather(w_dt, "seq", axis=1, tiled=True),
        lax.all_gather(w_out, "seq", axis=2, tiled=True),
    )
    mod_mask = modality[None, :] == jnp.arange(mod_count, dtype=jnp.int32)[:, None]
    mod_float = mod_mask.astype(jnp.float32)

    def by_mod(value):
        chosen = mod_mask.reshape(mod_mask.shape + (1,) * (value.ndim - 1))
        return jnp.where(chosen, value[None], jnp.zeros((), value.dtype))

    stream_f = x_full.astype(jnp.float32)
    inv_rms = lax.rsqrt(jnp.mean(stream_f * stream_f, axis=1, keepdims=True) + EPSILON)
    x_hat = stream_f * inv_rms
    normed = (x_hat * norm_gain[None, :]).astype(jnp.bfloat16)
    normed_split = by_mod(normed)
    projected = jnp.einsum(
        "mtd,mkde->tke", normed_split, w_in_full, preferred_element_type=jnp.float32
    )
    x_pre = projected[:, 0].astype(jnp.bfloat16)
    gate_in = projected[:, 1]
    rim_rows = passed_along(x_pre[length - rim_len :], "seq", 1)
    padded_seg = jnp.concatenate([jnp.full((rim_len,), -1, jnp.int32), seg_ids])
    seg_win = lax.dynamic_slice_in_dim(padded_seg, lax.axis_index("seq") * length, length + rim_len)
    seg_now = seg_win[rim_len:]
    extended = jnp.concatenate([rim_rows, x_pre], 0).astype(jnp.float32)
    tap_mask = [
        (seg_win[offset : offset + length] == seg_now).astype(jnp.float32)[:, None]
        for offset in range(CONV)
    ]
    conv_out = conv_b[None, :] + sum(
        (
            conv_w[offset][None, :] * extended[offset : offset + length] * tap_mask[offset]
            for offset in range(CONV)
        )
    )
    u_val = (conv_out * jax.nn.sigmoid(conv_out)).astype(jnp.bfloat16)
    u_split = by_mod(u_val)
    dt_part = jnp.einsum("mte,mre->tr", u_split, w_xdt_full, preferred_element_type=jnp.float32)
    bc_part = jnp.einsum("mte,mne->tn", u_split, w_xbc, preferred_element_type=jnp.float32)
    dt_sum, bc_sum = lax.psum((dt_part, bc_part), "ch")
    dt_low = dt_sum.astype(jnp.bfloat16)
    b_in = bc_sum[:, :STATE]
    c_out = bc_sum[:, STATE:]
    low_split = by_mod(dt_low)
    dt_raw = jnp.einsum(
        "mtr,mre->te", low_split, w_dt_full, preferred_element_type=jnp.float32
    ) + jnp.dot(mod_float.T, dt_bias, precision=PRECISE)
    dt_val = jax.nn.softplus(dt_raw)
    u_float = u_val.astype(jnp.float32)
    dt_u = dt_val * u_float
    neg_a = -jnp.exp(a_log)
    keep_mask = (seg_now == seg_win[rim_len - 1 : rim_len - 1 + length]).astype(jnp.float32)
    decay_all = jnp.exp(neg_a * jnp.sum(dt_val, axis=0)[None, :]) * jnp.prod(keep_mask)
    zero_state = jnp.zeros_like(neg_a)
    local_end, _, _ = run_forward(zero_state, dt_val, dt_u, b_in, c_out, keep_mask, neg_a)
    _, start_state = entering(
        (decay_all, local_end), "seq", chain_link, (jnp.ones_like(neg_a), zero_state), False
    )
    _, starts, y_ssm = run_forward(start_state, dt_val, dt_u, b_in, c_out, keep_mask, neg_a)
    y_val = y_ssm + d_skip[None, :] * u_float
    sig_gate = jax.nn.sigmoid(gate_in)
    gated = (y_val * (gate_in * sig_gate)).astype(jnp.bfloat16)
    gated_split = by_mod(gated)
    branch = lax.psum_scatter(
        jnp.einsum("mte,med->dt", gated_split, w_out_full, preferred_element_type=jnp.float32),
        "ch",
        scatter_dimension=0,
        tiled=True,
    ).T
    x_own = stream.astype(jnp.float32)
    mixed = x_own + branch
    output = mixed.astype(jnp.bfloat16)
    stats_part = jnp.stack(
        [jnp.sum(x_own * x_own), jnp.sum(branch * branch), jnp.sum(mixed * mixed)]
    )
    grad_split = by_mod(grad_full)
    d_gated = jnp.einsum("mtd,med->te", grad_split, w_out_full, preferred_element_type=jnp.float32)
    d_w_out = jnp.einsum("mte,td->med", gated_split, grad_full, preferred_element_type=jnp.float32)
    d_y = d_gated * gate_in * sig_gate
    d_gate = d_gated * y_val * silu_grad(gate_in)
    d_skip_part = jnp.sum(d_y * u_float, axis=0)
    local_back = local_adjoint(dt_val, c_out, keep_mask, d_y, neg_a)
    _, incoming = entering(
        (decay_all, local_back), "seq", chain_link, (jnp.ones_like(neg_a), zero_state), True
    )
    d_neg, d_dt_ssm, d_dtu, d_b, d_c = run_adjoint(
        incoming, starts, dt_val, dt_u, b_in, c_out, keep_mask, d_y, neg_a
    )
    d_a_log = d_neg * neg_a
    d_dt = d_dt_ssm + d_dtu * u_float
    d_u = d_y * d_skip[None, :] + d_dtu * dt_val
    d_raw = (d_dt * jax.nn.sigmoid(dt_raw)).astype(jnp.bfloat16)
    d_w_dt = jnp.einsum("mtr,te->mre", low_split, d_raw, preferred_element_type=jnp.float32)
    d_dt_bias = jnp.dot(mod_float, d_raw.astype(jnp.float32), precision=PRECISE)
    d_low_part = jnp.einsum(
        "mte,mre->tr", by_mod(d_raw), w_dt_full, preferred_element_type=jnp.float32
    )
    d_bc_part = jnp.concatenate([d_b, d_c], 1)
    d_low_sum, d_bc_sum = lax.psum((d_low_part, d_bc_part), "ch")
    d_low = d_low_sum.astype(jnp.bfloat16)
    d_bc = d_bc_sum.astype(jnp.bfloat16)
    d_w_xdt = jnp.einsum("mte,tr->mre", u_split, d_low, preferred_element_type=jnp.float32)
    d_w_xbc = jnp.einsum("mte,tn->mne", u_split, d_bc, preferred_element_type=jnp.float32)
    d_u = d_u + jnp.einsum(
        "mtr,mre->te", by_mod(d_low), w_xdt_full, preferred_element_type=jnp.float32
    )
    d_u = d_u + jnp.einsum("mtn,mne->te", by_mod(d_bc), w_xbc, preferred_element_type=jnp.float32)
    d_conv = d_u * silu_grad(conv_out)
    d_conv_b = jnp.sum(d_conv, axis=0)
    d_conv_w = jnp.stack(
        [
            jnp.sum(d_conv * extended[offset : offset + length] * tap_mask[offset], axis=0)
            for offset in range(CONV)
        ]
    )
    d_ext = sum(
        (
            jnp.pad(
                conv_w[offset][None, :] * d_conv * tap_mask[offset],
                ((offset, rim_len - offset), (0, 0)),
            )
            for offset in range(CONV)
        )
    )
    back_rim = passed_along(d_ext[:rim_len], "seq", -1)
    d_pre = d_ext[rim_len:] + jnp.pad(back_rim, ((length - rim_len, 0), (0, 0)))
    d_xz = jnp.stack([d_pre, d_gate], 1).astype(jnp.bfloat16)
    d_w_in = jnp.einsum("mtd,tke->mkde", normed_split, d_xz, preferred_element_type=jnp.float32)
    d_norm_part = jnp.einsum(
        "mtke,mkde->dt", by_mod(d_xz), w_in_full, preferred_element_type=jnp.float32
    )
    d_gain_part = jnp.einsum("dt,td->d", d_norm_part, x_hat, precision=PRECISE)
    d_norm = lax.psum(d_norm_part, "ch").T
    d_hat = d_norm * norm_gain[None, :]
    inner_dot = jnp.mean(d_hat * x_hat, axis=1, keepdims=True)
    d_x_full = inv_rms * (d_hat - x_hat * inner_dot)
    grad_stream = lax.dynamic_slice_in_dim(
        d_x_full, col_start, stream.shape[1], 1
    ) + cotangent.astype(jnp.float32)
    own_w_in, own_w_xdt, own_w_dt, own_w_out = (
        lax.psum_scatter(d_w_in, "seq", scatter_dimension=2, tiled=True),
        lax.psum_scatter(d_w_xdt, "seq", scatter_dimension=1, tiled=True),
        lax.psum_scatter(d_w_dt, "seq", scatter_dimension=1, tiled=True),
        lax.psum_scatter(d_w_out, "seq", scatter_dimension=2, tiled=True),
    )

    def spread(value):
        full_shape = value.shape[:-1] + (INNER,)
        return lax.dynamic_update_slice_in_dim(
            jnp.zeros(full_shape, jnp.float32), value, ch_start, value.ndim - 1
        )

    def own_slice(value):
        return lax.dynamic_slice_in_dim(value, ch_start, channels, value.ndim - 1)

    summed = lax.psum(
        (
            spread(d_conv_w),
            spread(d_conv_b),
            spread(d_w_xbc),
            spread(d_dt_bias),
            spread(d_a_log),
            spread(d_skip_part),
            d_gain_part,
            stats_part,
        ),
        ("seq", "ch"),
    )
    stats = jnp.sqrt(summed[7] / float(length * lax.axis_size("seq") * model_width))
    return (
        output,
        grad_stream,
        summed[6],
        own_w_in,
        own_slice(summed[0]),
        own_slice(summed[1]),
        own_w_xdt,
        own_slice(summed[2]),
        own_w_dt,
        own_slice(summed[3]),
        own_slice(summed[4]),
        own_slice(summed[5]),
        own_w_out,
        stats,
    )


def solution(mesh):
    in_specs = (
        P("seq", "ch"),
        P(),
        P(None, None, "seq", "ch"),
        P(None, "ch"),
        P("ch"),
        P(None, "seq", "ch"),
        P(None, None, "ch"),
        P(None, "seq", "ch"),
        P(None, "ch"),
        P(None, "ch"),
        P("ch"),
        P(None, "ch", "seq"),
        P("seq", "ch"),
        P(),
        P("seq"),
    )
    out_specs = (
        P("seq", "ch"),
        P("seq", "ch"),
        P(),
        P(None, None, "seq", "ch"),
        P(None, "ch"),
        P("ch"),
        P(None, "seq", "ch"),
        P(None, None, "ch"),
        P(None, "seq", "ch"),
        P(None, "ch"),
        P(None, "ch"),
        P("ch"),
        P(None, "ch", "seq"),
        P(),
    )
    seqs, chs = mesh.shape["seq"], mesh.shape["ch"]
    whole_lanes = INNER % (seqs * chs * LANES) == 0 and seqs % chs == 0
    return jax.shard_map(
        per_device if whole_lanes else per_device_by_token, mesh=mesh, in_specs=in_specs, out_specs=out_specs, check_vma=False
    )
```

```python
from functools import partial

import jax
import jax.numpy as jnp
from jax import lax
from jax.experimental import pallas as pl
from jax.experimental.pallas import tpu as pltpu
from jax.sharding import PartitionSpec as P

INNER = 4096
STATE = 16
CONV = 4
BLK = 64
RANK = 128


EPSILON = 1e-05
PRECISE = lax.Precision.HIGHEST


def passed_along(value, axis, steps):
    count = lax.axis_size(axis)
    initial, last = (max(0, -steps), min(count, count - steps))
    return lax.ppermute(value, axis, [(source, source + steps) for source in range(initial, last)])


def entering(part, axis, combine, identity, reverse):
    count = lax.axis_size(axis)
    place = lax.axis_index(axis)
    ahead = count - 1 - place if reverse else place
    gathered = jax.tree.map(lambda a: lax.all_gather(a, axis), part)
    state = jax.tree.map(lambda a, e: jnp.zeros_like(a) + jnp.asarray(e, a.dtype), part, identity)

    def one(step, state):
        source = count - 1 - step if reverse else step
        return combine(
            state, jax.tree.map(lambda a: lax.dynamic_index_in_dim(a, source, 0, False), gathered)
        )

    return lax.fori_loop(0, ahead, one, state)


def silu_grad(value):
    sigma = jax.nn.sigmoid(value)
    return sigma * (1.0 + value * (1.0 - sigma))


def chain_link(earlier, latter):
    return (earlier[0] * latter[0], latter[0] * earlier[1] + latter[1])


def decay_terms(dt_blk, keep_blk, neg_a):
    return keep_blk[:, None, None] * jnp.exp(dt_blk[:, None, :] * neg_a[None])


def drive_terms(b_blk, dtu_blk):
    return b_blk[:, :, None] * dtu_blk[:, None, :]


def to_blocks(values):
    block_count = values[0].shape[0] // BLK
    return tuple((value.reshape((block_count, BLK) + value.shape[1:]) for value in values))


def run_forward(state_in, dt_val, dt_u, b_in, c_out, keep_mask, neg_a):

    def block_step(state_now, blk_rows):
        dt_blk, dtu_blk, b_blk, c_blk, keep_blk = blk_rows
        cum_a, cum_b = lax.associative_scan(
            chain_link, (decay_terms(dt_blk, keep_blk, neg_a), drive_terms(b_blk, dtu_blk))
        )
        states = cum_a * state_now[None] + cum_b
        y_blk = jnp.einsum("tn,tne->te", c_blk, states, precision=PRECISE)
        return (states[-1], (state_now, y_blk))

    state_end, (starts, y_ssm) = lax.scan(
        block_step, state_in, to_blocks((dt_val, dt_u, b_in, c_out, keep_mask))
    )
    return (state_end, starts, y_ssm.reshape(dt_val.shape))


def adjoint_states(decay, c_blk, dy_blk, incoming):
    source = c_blk[:, :, None] * dy_blk[:, None, :]
    shifted = jnp.concatenate([decay[1:], jnp.ones_like(decay[:1])], 0)
    prod_a, acc_g = lax.associative_scan(chain_link, (shifted, source), reverse=True)
    return prod_a * incoming[None] + acc_g


def local_adjoint(dt_val, c_out, keep_mask, d_y, neg_a):

    def block_step(incoming, blk_rows):
        dt_blk, c_blk, keep_blk, dy_blk = blk_rows
        decay = decay_terms(dt_blk, keep_blk, neg_a)
        adjoint = adjoint_states(decay, c_blk, dy_blk, incoming)
        return (decay[0] * adjoint[0], None)

    outgoing, _ = lax.scan(
        block_step, jnp.zeros_like(neg_a), to_blocks((dt_val, c_out, keep_mask, d_y)), reverse=True
    )
    return outgoing


def run_adjoint(incoming, starts, dt_val, dt_u, b_in, c_out, keep_mask, d_y, neg_a):

    def block_step(carried, blk_rows):
        later_in, d_neg = carried
        state_in, dt_blk, dtu_blk, b_blk, c_blk, keep_blk, dy_blk = blk_rows
        decay = decay_terms(dt_blk, keep_blk, neg_a)
        adjoint = adjoint_states(decay, c_blk, dy_blk, later_in)
        cum_a, cum_b = lax.associative_scan(chain_link, (decay, drive_terms(b_blk, dtu_blk)))
        states = cum_a * state_in[None] + cum_b
        before = jnp.concatenate([state_in[None], states[:-1]], 0)
        flow = adjoint * before * decay
        d_dt_blk = jnp.sum(flow * neg_a[None], axis=1)
        d_neg = d_neg + jnp.einsum("tne,te->ne", flow, dt_blk, precision=PRECISE)
        d_dtu_blk = jnp.einsum("tne,tn->te", adjoint, b_blk, precision=PRECISE)
        d_b_blk = jnp.einsum("tne,te->tn", adjoint, dtu_blk, precision=PRECISE)
        d_c_blk = jnp.einsum("tne,te->tn", states, dy_blk, precision=PRECISE)
        return ((decay[0] * adjoint[0], d_neg), (d_dt_blk, d_dtu_blk, d_b_blk, d_c_blk))

    blk_rows = (starts,) + to_blocks((dt_val, dt_u, b_in, c_out, keep_mask, d_y))
    (_, d_neg), outs = lax.scan(
        block_step, (incoming, jnp.zeros_like(neg_a)), blk_rows, reverse=True
    )
    length = dt_val.shape[0]
    return (d_neg,) + tuple((value.reshape((length,) + value.shape[2:]) for value in outs))


F32 = jnp.float32
BF16 = jnp.bfloat16
LANES = 128
ROWS = 256
CHUNK = 128
GROUP = 16
LOG2E = 1.4426950408889634
CUT = 1e4
CUTS = 4
SKIP, CONV_B, CONV_W, BIAS = STATE, STATE + 1, STATE + 2, STATE + 2 + CONV


def dot(a, b, da, db):
    return lax.dot_general(a, b, (((da,), (db,)), ((), ())), preferred_element_type=F32)


def column(row):
    return jnp.transpose(jnp.broadcast_to(row, (LANES, row.shape[1])))


def silu_slope(value, sigma):
    return sigma * (1.0 + value * (1.0 - sigma))


def flat_mask(rows):
    t = lax.broadcasted_iota(jnp.int32, (rows, LANES), 0)
    lane = lax.broadcasted_iota(jnp.int32, (rows, LANES), 1)
    return lax.rem(t, 8) == lane // STATE


def two_parts(value):
    high = value.astype(BF16).astype(F32)
    return high, value - high


def stacked(value):
    return jnp.concatenate(two_parts(value), axis=0).astype(BF16)


def outer(flat, value, out):
    mask = flat_mask(8)
    for r in range(CHUNK // 8):
        bh, bl = two_parts(jnp.where(mask, flat[r : r + 1], 0.0))
        vh, vl = two_parts(value[8 * r : 8 * r + 8])
        left = jnp.concatenate([bh, bh, bl, bl], axis=0).astype(BF16)
        right = jnp.concatenate([vh, vl, vh, vl], axis=0).astype(BF16)
        out[8 * r : 8 * r + 8] = dot(left, right, 0, 0).reshape(8, STATE, LANES)


def block_at(i, size):
    return pl.ds(pl.multiple_of(i * size, size), size)


def token_at(i, size):
    return i * size + lax.broadcasted_iota(jnp.int32, (size, LANES), 0)


def decay_step(i, bound, dt):
    t = token_at(i, CHUNK)
    return jnp.where((t == 0) | (t == bound), CUT, dt)


class Front:
    def __init__(self, bound, x_all, gain, wi, rows, wx, wbc, mod, own, outs, scratch):
        self.bound, self.x_all, self.gain, self.wi, self.rows, self.wx, self.wbc = bound, x_all, gain, wi, rows, wx, wbc
        self.mod, self.own = mod, own
        self.normed, self.inv, self.xpre, self.conv, self.u, self.gate = outs
        self.ext, self.wide = scratch
        self.ext[0:8] = jnp.zeros((8, LANES), F32)

    def block(self, at, i):
        chs, part = at.chs, self.normed.shape[1]
        tokens = self.u.shape[0]
        span = block_at(i, ROWS)
        x = jnp.concatenate([self.x_all[i * chs + c] for c in range(chs)], axis=1).astype(F32)
        inv = lax.rsqrt(jnp.mean(x * x, axis=1, keepdims=True) + EPSILON)
        normed = (x * inv * self.gain[...]).astype(BF16)
        self.inv[span] = jnp.broadcast_to(inv, (ROWS, LANES))
        self.wide[...] = normed
        self.normed[span] = self.wide[:, lanes_at(at.s, part)]
        image = column(self.mod[i, 0:1]) > 0.5
        both = [dot(normed, jnp.concatenate([self.wi[m, 0], self.wi[m, 1]], axis=1), 1, 0) for m in range(2)]
        x_pre = jnp.where(image, both[1][:, :LANES], both[0][:, :LANES]).astype(BF16)
        self.gate[span] = jnp.where(image, both[1][:, LANES:], both[0][:, LANES:])
        self.xpre[span] = x_pre
        ext = self.ext
        ext[8:] = x_pre.astype(F32)
        t = token_at(i, ROWS)
        conv = None
        for j in range(CONV):
            lag = CONV - 1 - j
            term = self.rows[CONV_W + j : CONV_W + j + 1] * ext[8 - lag : 8 - lag + ROWS]
            if lag:
                term = jnp.where((t < lag) | ((t >= self.bound) & (t - lag < self.bound)), 0.0, term)
            conv = term if conv is None else conv + term
        conv = self.rows[CONV_B : CONV_B + 1] + conv
        self.conv[span] = conv
        ext[0:8] = ext[ROWS : ROWS + 8]
        u = (conv * jax.nn.sigmoid(conv)).astype(BF16)
        self.u[span] = u
        self.own[span] = jnp.where(image, dot(u, self.wx[1], 1, 1), dot(u, self.wx[0], 1, 1))
        mask = flat_mask(ROWS)
        few = ROWS // 8
        for n in range(2):
            tiled = [
                jnp.concatenate([self.wbc[m, n * STATE : (n + 1) * STATE, lanes_at(at.s, LANES)]] * 8, axis=0)
                for m in range(2)
            ]
            wide = jnp.where(mask, jnp.where(image, dot(u, tiled[1], 1, 1), dot(u, tiled[0], 1, 1)), 0.0)
            start = pl.multiple_of(tokens + n * (tokens // 8) + i * few, few)
            self.own[pl.ds(start, few)] = jnp.sum(wide.reshape(few, 8, LANES), axis=1)


def chunk_image(mod, i):
    fold = ROWS // CHUNK
    return column(mod[i // fold, 0:1, lanes_at(lax.rem(i, fold), CHUNK)]) > 0.5


def flats_at(xdbl, i, n):
    tokens = xdbl.shape[0] // 5 * 4
    few = CHUNK // 8
    return xdbl[pl.ds(pl.multiple_of(tokens + n * (tokens // 8) + i * few, few), few)]


def forward_kernel(
    seqs, chs, bound_ref, x_ref, cot_ref, wi_ref, wo_ref, wx_ref, wdt_ref, mod_ref, gain_ref, wbc_ref, rows_ref,
    xdbl, u_all, conv_all, xpre_all, dy_all, dt_all, sig_all, gated_all, dgate_all, hs_out, normed_s, cot_s, inv_all,
    wx, wdt, mod, dskip, *rest,
):
    totals, spread1, spread2, trades, rest = split(rest, 10, 3, 3, 15, 13)
    x_all, cot_all, wi, wo, gate_all, y_all, ext, wide, h_s, dta_s, x_s, hbuf, sems = rest
    at = Place(seqs, chs)
    bound = bound_ref[0]
    own, part, low = LANES, wi_ref.shape[2], wx_ref.shape[1]
    tokens = u_all.shape[0]
    total = Total(at, xdbl, *totals)
    stream = Spread(at, x_ref, x_all, *spread1)
    cot = Spread(at, cot_ref, cot_all, *spread2)
    lows = pl.ds(pl.multiple_of(at.s * low, 16), low)
    plans = [
        (lambda t: wi_ref.at[:, :, :, lanes_at(t, own)], wi.at[:, :, rows_at(at.s, part)]),
        (lambda t: wx_ref.at[:, :, lanes_at(t, own)], wx.at[:, lows]),
        (lambda t: mod_ref, mod.at[at.s]),
        (lambda t: wdt_ref.at[:, :, lanes_at(t, own)], wdt.at[:, lows]),
        (lambda t: wo_ref.at[:, rows_at(t, own)], wo.at[:, :, lanes_at(at.s, part)]),
    ]
    trades = [Trade(at, src, dst, *trades[3 * n : 3 * n + 3]) for n, (src, dst) in enumerate(plans)]
    at.greet(at.others + [at.side, at.across])
    stream.start()
    for trade in trades[:4]:
        trade.start()
    for level in range(3):
        stream.relay(level)
    cot.start()
    trades[4].start()
    stream.finish()
    for trade in trades[:4]:
        trade.finish()
    front = Front(
        bound, x_all, gain_ref, wi, rows_ref, wx, wbc_ref, mod, total.own,
        (normed_s, inv_all, xpre_all, conv_all, u_all, gate_all), (ext, wide),
    )

    def front_step(i, carry):
        front.block(at, i)
        return carry

    lax.fori_loop(0, tokens // ROWS, front_step, 0)
    cot.relay(0)
    total.halve(0)
    total.halve(1)
    cot.relay(1)
    total.halve(2)
    total.meet()
    total.double(2)
    cot.relay(2)
    total.double(1)
    total.double(0)
    rate = -jnp.exp(rows_ref[0:STATE]) * LOG2E
    h_s[...] = jnp.zeros_like(h_s)
    first = pltpu.make_async_copy(h_s, hs_out.at[0], sems.at[2])
    first.start()
    first.wait()

    def out_copy(i, slot):
        start = i * CHUNK + 1
        return pltpu.make_async_copy(hbuf.at[slot], hs_out.at[pl.ds(start, CHUNK)], sems.at[slot])

    def scan_step(i, carry):
        slot = lax.rem(i, 2)
        span = block_at(i, CHUNK)
        image = chunk_image(mod, i)
        low = xdbl[span].astype(BF16)
        raw = jnp.where(
            image,
            dot(low, wdt[1], 1, 0) + rows_ref[BIAS + 1 : BIAS + 2],
            dot(low, wdt[0], 1, 0) + rows_ref[BIAS : BIAS + 1],
        )
        dt = jnp.maximum(raw, 0.0) + jnp.log1p(jnp.exp(-jnp.abs(raw)))
        u = u_all[span].astype(F32)
        dt_all[span] = dt
        sig_all[span] = jax.nn.sigmoid(raw)
        dta_s[...] = decay_step(i, bound, dt)
        outer(flats_at(xdbl, i, 0), dt * u, x_s)

        @pl.when(i >= 2)
        def _():
            out_copy(i - 2, slot).wait()

        def group(g, h):
            base = pl.multiple_of(g * GROUP, GROUP)
            for k in range(GROUP):
                h = jnp.exp2(dta_s[pl.ds(base + k, 1)] * rate) * h + x_s[base + k]
                hbuf[slot, base + k] = h
            return h

        h_s[...] = lax.fori_loop(0, CHUNK // GROUP, group, h_s[...])
        out_copy(i, slot).start()
        c_all = flats_at(xdbl, i, 1)
        mask = flat_mask(8)
        parts = []
        for r in range(CHUNK // 8):
            left = stacked(jnp.where(mask, c_all[r : r + 1], 0.0))
            made = dot(left, hbuf[slot, 8 * r : 8 * r + 8].reshape(8 * STATE, LANES).astype(BF16), 1, 0)
            parts.append(made[0:8] + made[8:16])
        y = jnp.concatenate(parts, axis=0) + rows_ref[SKIP : SKIP + 1] * u
        y_all[span] = y
        gate = gate_all[span]
        gated_all[span] = (y * (gate * jax.nn.sigmoid(gate))).astype(BF16)
        return carry

    chunks = tokens // CHUNK
    lax.fori_loop(0, chunks, scan_step, 0)
    cot.finish()
    trades[4].finish()
    folds = seqs // chs
    slices = []
    for n in range(seqs):
        src = cot_all.at[n * chs + at.s // folds, :, lanes_at(lax.rem(at.s, folds), part)]
        slices.append(pltpu.make_async_copy(src, cot_s.at[pl.ds(n * ROWS, ROWS)], sems.at[3 + n]))
        slices[-1].start()
    dskip[...] = jnp.zeros_like(dskip)

    def gate_step(i, carry):
        span = block_at(i, ROWS)
        image = column(mod[i, 0:1]) > 0.5
        cots = jnp.concatenate([cot_all[i * chs + c] for c in range(chs)], axis=1)
        d_gated = jnp.where(image, dot(cots, wo[1], 1, 1), dot(cots, wo[0], 1, 1))
        gate = gate_all[span]
        sigma = jax.nn.sigmoid(gate)
        d_y = d_gated * gate * sigma
        dy_all[span] = d_y
        dgate_all[span] = (d_gated * y_all[span] * silu_slope(gate, sigma)).astype(BF16)
        dskip[...] += jnp.sum(d_y * u_all[span].astype(F32), axis=0, keepdims=True)
        return carry

    lax.fori_loop(0, tokens // ROWS, gate_step, 0)
    for i in (chunks - 2, chunks - 1):
        out_copy(i, i % 2).wait()
    for copy in slices:
        copy.wait()
    total.finish()


def adjoint_chunk(bound, i, state, xdbl, u_all, dy_all, dt_all, sig_all, mod, wdt, rows_ref, own, du_all, grads, scratch):
    ga_s, dn_s, dta_s, x_s, g_s, f_s = scratch
    dwdt, dbias = grads
    tokens = u_all.shape[0]
    span = block_at(i, CHUNK)
    dt = dt_all[span]
    u = u_all[span].astype(F32)
    d_y = dy_all[span]
    dta_s[...] = decay_step(i, bound, dt)
    neg_a = -jnp.exp(rows_ref[0:STATE])
    rate = neg_a * LOG2E
    outer(flats_at(xdbl, i, 1), d_y, x_s)
    start = pl.multiple_of(i * CHUNK, CHUNK)

    def group(step, carried):
        ga, dn = carried
        base = pl.multiple_of((CHUNK // GROUP - 1 - step) * GROUP, GROUP)
        for k in reversed(range(GROUP)):
            adjoint = x_s[base + k] + ga
            ga = jnp.exp2(dta_s[pl.ds(base + k, 1)] * rate) * adjoint
            slow = ga * state[base + k] * neg_a
            dn = dn + slow * dt_all[pl.ds(start + base + k, 1)]
            g_s[base + k] = adjoint.astype(BF16)
            f_s[base + k] = slow.astype(BF16)
        return ga, dn

    ga, dn = lax.fori_loop(0, CHUNK // GROUP, group, (ga_s[...], dn_s[...]))
    ga_s[...] = ga
    dn_s[...] = dn
    dtu = dt * u
    b_all = flats_at(xdbl, i, 0)
    mask = flat_mask(8)
    ones = jnp.where(flat_mask(16), 1.0, 0.0).astype(BF16)
    pu, pd, db, dc = [], [], [], []
    for r in range(CHUNK // 8):
        few = slice(8 * r, 8 * r + 8)
        adjoint = g_s[few].reshape(8 * STATE, LANES)
        slow = f_s[few].reshape(8 * STATE, LANES)
        h = state[8 * r + 1 : 8 * r + 9].reshape(8 * STATE, LANES).astype(BF16)
        made = dot(stacked(jnp.where(mask, b_all[r : r + 1], 0.0)), adjoint, 1, 0)
        pu.append(made[0:8] + made[8:16])
        pd.append(dot(ones, slow, 1, 0)[0:8])
        for out, value, other in ((db, dtu, adjoint), (dc, d_y, h)):
            made = dot(stacked(value[few]), other, 1, 1)
            out.append(jnp.sum(jnp.where(mask, made[0:8] + made[8:16], 0.0), axis=0, keepdims=True))
    d_dtu = jnp.concatenate(pu, axis=0)
    d_dt = jnp.concatenate(pd, axis=0) + d_dtu * u
    few = CHUNK // 8
    for n, part in enumerate((db, dc)):
        first = pl.multiple_of(tokens + n * (tokens // 8) + i * few, few)
        own[pl.ds(first, few)] = jnp.concatenate(part, axis=0)
    du_all[span] = d_y * rows_ref[SKIP : SKIP + 1] + d_dtu * dt
    d_raw = (d_dt * sig_all[span]).astype(BF16)
    image = chunk_image(mod, i)
    low = xdbl[span].astype(BF16)
    own[span] = jnp.where(image, dot(d_raw, wdt[1], 1, 1), dot(d_raw, wdt[0], 1, 1))
    raw_f = d_raw.astype(F32)
    for m in range(2):
        mine = jnp.where(image == (m == 1), raw_f, 0.0)
        dwdt[m] += dot(low, mine.astype(BF16), 0, 0)
        dbias[m : m + 1] += jnp.sum(mine, axis=0, keepdims=True)


def rear_block(bound, i, at, dx, du_all, u_all, conv_all, xpre_all, mod, wx, wbc, rows_ref, dpre_all, grads, scratch):
    dwx, dwbc, dconv = grads
    ext, ahead = scratch
    tokens = u_all.shape[0]
    span = block_at(i, ROWS)
    few = ROWS // 8
    image = column(mod[i, 0:1]) > 0.5
    low = dx[span].astype(BF16)
    mask = flat_mask(ROWS)
    lane = lax.broadcasted_iota(jnp.int32, (LANES, 2 * STATE), 0)
    state = lax.broadcasted_iota(jnp.int32, (LANES, 2 * STATE), 1)
    d_bc = None
    for n in range(2):
        fold = jnp.where(lax.rem(lane, STATE) + n * STATE == state, 1.0, 0.0).astype(BF16)
        flat = dx[pl.ds(pl.multiple_of(tokens + n * (tokens // 8) + i * few, few), few)]
        wide = jnp.broadcast_to(flat[:, None, :], (few, 8, LANES)).reshape(ROWS, LANES)
        part = dot(jnp.where(mask, wide, 0.0).astype(BF16), fold, 1, 0)
        d_bc = part if d_bc is None else d_bc + part
    d_bc = d_bc.astype(BF16)
    u = u_all[span]
    extra = [dot(low, wx[m], 1, 0) + dot(d_bc, wbc[m, :, lanes_at(at.s, LANES)], 1, 0) for m in range(2)]
    d_u = du_all[span] + jnp.where(image, extra[1], extra[0])
    u_f = u.astype(F32)
    for m in range(2):
        mine = jnp.where(image == (m == 1), u_f, 0.0).astype(BF16)
        dwx[m] += dot(low, mine, 0, 0)
        dwbc[m] += dot(d_bc, mine, 0, 0)
    conv = conv_all[span]
    d_conv = d_u * silu_slope(conv, jax.nn.sigmoid(conv))
    before = lax.rem(i * ROWS + tokens - 16, tokens)
    ext[0:8] = xpre_all[pl.ds(pl.multiple_of(before, 16), 16)].astype(F32)[8:16]
    ext[8:] = xpre_all[span].astype(F32)
    ahead[ROWS : ROWS + 8] = ahead[0:8]
    ahead[0:ROWS] = d_conv
    t = token_at(i, ROWS)
    d_pre = None
    for tap in range(CONV):
        lag = CONV - 1 - tap
        seen = ext[8 - lag : 8 - lag + ROWS] * d_conv
        term = rows_ref[CONV_W + tap : CONV_W + tap + 1] * ahead[lag : lag + ROWS]
        if lag:
            seen = jnp.where((t < lag) | ((t >= bound) & (t - lag < bound)), 0.0, seen)
            term = jnp.where((t < bound) & (t + lag >= bound), 0.0, term)
        dconv[tap : tap + 1] += jnp.sum(seen, axis=0, keepdims=True)
        d_pre = term if d_pre is None else d_pre + term
    dconv[CONV : CONV + 1] += jnp.sum(d_conv, axis=0, keepdims=True)
    dpre_all[span] = d_pre.astype(BF16)


def grown(image, width):
    return jnp.concatenate([image] * (width // LANES), axis=1)


def out_block(i, gated, cot_s, mod, wo, branch, dwo):
    span = block_at(i, ROWS)
    wide = jnp.concatenate([gated[n, span] for n in range(gated.shape[0])], axis=1)
    cot = cot_s[span].astype(F32)
    image = grown(column(mod[i, 0:1]) > 0.5, cot.shape[1])
    branch[span] = jnp.where(image, dot(wide, wo[1], 1, 0), dot(wide, wo[0], 1, 0))
    for m in range(2):
        dwo[m] += dot(wide, jnp.where(image == (m == 1), cot, 0.0).astype(BF16), 0, 0)


def in_block(i, k, first, dz_all, normed_s, mod, wi, d_norm, dwi):
    span = block_at(i, ROWS)
    dz = jnp.concatenate([dz_all[n, span] for n in range(dz_all.shape[0])], axis=1)
    normed = normed_s[span].astype(F32)
    image = grown(column(mod[i, 0:1]) > 0.5, normed.shape[1])
    total = jnp.where(image, dot(dz, wi[1, k], 1, 1), dot(dz, wi[0, k], 1, 1))
    d_norm[span] = total if first else d_norm[span] + total
    for m in range(2):
        dwi[m, k] += dot(jnp.where(image == (m == 1), normed, 0.0).astype(BF16), dz, 0, 0)


def backward_kernel(
    seqs, chs, bound_ref, xdbl, u_all, conv_hbm, xpre_hbm, dy_all, dt_all, sig_all, gated_own, dgate_own, hs,
    normed_hbm, cot_hbm, inv_hbm, wx, wdt, mod, dskip, wbc, rows_ref, wi_hbm, wo_hbm, gain_ref, x_ref, own_cot,
    out_ref, grad_ref, sums_ref, dwi, dwo, small_ref, parts_ref, *rest,
):
    totals, branches, norms, shares, trades, rest = split(rest, 10, 10, 10, 15, 6, len(rest) - 51)
    (
        dx, du_all, dpre_own, gated_all, dgate_all, dpre_all, conv_all, xpre_all, normed_s, cot_s, wi, wo, inv,
        branch, d_norm, hbuf, ga_s, dn_s, dta_s, x_s, g_s, f_s, ext, ahead, dwdx, dwbc, dbias, dconv,
        small_own, small_all, dots, r3, pay, r4, hsem, lsem, dsend, drecv, gsend, grecv, psend, precv,
    ) = rest
    at = Place(seqs, chs)
    bound = bound_ref[0]
    tokens, own, rows = u_all.shape[0], LANES, x_ref.shape[0]
    chunks, blocks = tokens // CHUNK, tokens // ROWS

    def state_copy(i, slot):
        return pltpu.make_async_copy(hs.at[pl.ds(i * CHUNK, CHUNK + 1)], hbuf.at[slot], hsem.at[slot])

    state_copy(chunks - 1, 0).start()
    late = [
        (conv_hbm, conv_all), (xpre_hbm, xpre_all), (normed_hbm, normed_s), (cot_hbm, cot_s), (wi_hbm, wi),
        (wo_hbm, wo), (inv_hbm.at[block_at(at.s, rows)], inv),
    ]
    late = [pltpu.make_async_copy(src, dst, lsem.at[n]) for n, (src, dst) in enumerate(late)]
    for copy in late:
        copy.start()
    total = Total(at, dx, *totals)
    gated = Share(at, gated_own, gated_all, CUTS, *shares[0:5])
    d_gate = Share(at, dgate_own, dgate_all, CUTS, *shares[5:10])
    d_pre = Share(at, dpre_own, dpre_all, CUTS, *shares[10:15])
    at.greet(at.mates + at.others + Regroup.sources(at))
    gated.start()
    d_gate.start()
    for ref in (ga_s, dn_s, dwdx, dwbc, dbias, dconv, ahead, dwi, dwo):
        ref[...] = jnp.zeros_like(ref)

    def adjoint_step(j, carry):
        i = chunks - 1 - j
        slot = lax.rem(j, 2)
        state_copy(i, slot).wait()

        @pl.when(j < chunks - 1)
        def _():
            state_copy(i - 1, 1 - slot).start()

        adjoint_chunk(
            bound, i, hbuf.at[slot], xdbl, u_all, dy_all, dt_all, sig_all, mod, wdt, rows_ref, total.own, du_all,
            (dwdx.at[1], dbias), (ga_s, dn_s, dta_s, x_s, g_s, f_s),
        )
        for cut in range(2):

            @pl.when(j == 7 + 5 * cut)
            def _():
                gated.relay(cut)

        return carry

    lax.fori_loop(0, chunks, adjoint_step, 0)
    total.halve(0)
    gated.relay(2)
    total.halve(1)
    gated.relay(3)
    total.halve(2)
    total.meet()
    total.double(2)
    d_gate.relay(0)
    total.double(1)
    d_gate.relay(1)
    total.double(0)
    for copy in late:
        copy.wait()

    def rear_step(j, carry):
        rear_block(
            bound, blocks - 1 - j, at, dx, du_all, u_all, conv_all, xpre_all, mod, wx, wbc, rows_ref, dpre_own,
            (dwdx.at[0], dwbc, dconv), (ext, ahead),
        )
        return carry

    lax.fori_loop(0, blocks, rear_step, 0)
    d_gate.relay(2)
    d_gate.relay(3)
    d_pre.start()
    small_own[...] = jnp.concatenate(
        [dn_s[...], dconv[...], dbias[...], dskip[...], jnp.zeros((5, own), F32), dwbc[0], dwbc[1]], axis=0
    )
    small = Trade(at, lambda t: small_own, small_all.at[at.s], *trades[0:3])
    low = parts_ref.shape[2]
    parts = Trade(
        at, lambda t: dwdx.at[:, :, rows_at(t, low)], parts_ref.at[:, :, :, lanes_at(at.s, own)], *trades[3:6]
    )
    small.start()
    parts.start()
    gated.finish()

    def out_step(i, carry):
        out_block(i, gated_all, cot_s, mod, wo, branch, dwo)
        return carry

    lax.fori_loop(0, blocks, out_step, 0)
    branch_sum = Regroup(at, branch, *branches)
    branch_sum.one()
    d_gate.finish()
    d_pre.relay(0)

    def first_step(i, carry):
        in_block(i, 1, True, dgate_all, normed_s, mod, wi, d_norm, dwi)
        return carry

    lax.fori_loop(0, blocks // 2, first_step, 0)
    branch_sum.two()
    d_pre.relay(1)
    lax.fori_loop(blocks // 2, blocks, first_step, 0)
    branch_sum.three()
    d_pre.relay(2)
    d_pre.relay(3)
    added = branch_sum.result()
    xs = x_ref[...].astype(F32)
    mixed = xs + added
    out_ref[...] = mixed.astype(BF16)
    d_pre.finish()
    norm_sum = Regroup(at, d_norm, *norms)

    def second_step(n, carry):
        i = lax.rem((1 - at.o) * (blocks // 2) + n, blocks)
        in_block(i, 0, False, dpre_all, normed_s, mod, wi, d_norm, dwi)
        return carry

    lax.fori_loop(0, blocks // 2, second_step, 0)
    norm_sum.one()
    lax.fori_loop(blocks // 2, blocks, second_step, 0)
    norm_sum.two()
    small.finish()
    parts.finish()
    for n in range(seqs):
        small_ref[:, n * own : (n + 1) * own] = small_all[n]
    norm_sum.three()
    inv_own = inv[...][:, 0:1]
    x_hat = xs * inv_own
    width = chs * x_ref.shape[1]
    gain = gain_ref[:, lanes_at(at.c, x_ref.shape[1])]
    total_norm = norm_sum.result()
    d_hat = total_norm * gain
    dot_part = jnp.sum(d_hat * x_hat, axis=1, keepdims=True)
    dots[...] = jnp.transpose(jnp.broadcast_to(dot_part, (rows, LANES)))[0:8]
    third = [remote(dots, r3.at[k], dsend.at[k], drecv.at[k], mate) for k, mate in enumerate(at.mates)]
    for copy in third:
        copy.start()
    rows_of = [total_norm * x_hat, xs * xs, added * added, mixed * mixed]
    pay[...] = jnp.concatenate(
        [jnp.sum(v, axis=0, keepdims=True) for v in rows_of] + [jnp.zeros((4, x_ref.shape[1]), F32)], axis=0
    )
    fourth = [remote(pay, r4.at[k], gsend.at[k], grecv.at[k], other) for k, other in enumerate(at.others)]
    for copy in fourth:
        copy.start()
    dot_sum = dots[...]
    for k, copy in enumerate(third):
        copy.wait_recv()
        dot_sum = dot_sum + r3[k]
    inner = column(dot_sum[0:1])[:, 0:1] / width
    grad_ref[...] = own_cot[...].astype(F32) + inv_own * (d_hat - x_hat * inner)
    joint = pay[...]
    for k, copy in enumerate(fourth):
        copy.wait_recv()
        joint = joint + r4[k]
    sums_ref[at.c] = joint
    spot = sums_ref.at[at.c]
    fifth = [remote(spot, spot, psend.at[k], precv.at[k], mate) for k, mate in enumerate(at.mates)]
    for copy in fifth:
        copy.start()
    for copy in fifth:
        copy.wait_recv()
    for copy in third + fourth + fifth:
        copy.wait_send()
    branch_sum.finish()
    norm_sum.finish()
    total.finish()

MESH = pl.DeviceIdType.MESH


def remote(src, dst, send, recv, peer):
    return pltpu.make_async_remote_copy(
        src_ref=src, dst_ref=dst, send_sem=send, recv_sem=recv,
        device_id={"seq": peer[0], "ch": peer[1]}, device_id_type=MESH,
    )


def rows_at(start, size):
    return pl.ds(pl.multiple_of(start * size, 8), size)


def lanes_at(start, size):
    return pl.ds(pl.multiple_of(start * size, LANES), size)


class Place:
    def __init__(self, seqs, chs):
        self.seqs, self.chs, self.depth = seqs, chs, seqs // 2
        self.s, self.c = lax.axis_index("seq"), lax.axis_index("ch")
        self.z, self.x = self.s // 2, lax.rem(self.s, 2)
        self.y, self.o = self.c // 2, lax.rem(self.c, 2)
        self.side = (self.s, self.y * 2 + 1 - self.o)
        self.across = (self.s, (1 - self.y) * 2 + self.o)
        self.beside = (self.z * 2 + 1 - self.x, self.c)
        self.deep = [(lax.rem(self.z + k, self.depth) * 2 + self.x, self.c) for k in range(1, self.depth)]
        self.others = [(lax.rem(self.s + k, seqs), self.c) for k in range(1, seqs)]
        self.mates = [(self.s, lax.rem(self.c + k, chs)) for k in range(1, chs)]

    def greet(self, peers):
        barrier = pltpu.get_barrier_semaphore()
        for seq, ch in peers:
            pl.semaphore_signal(barrier, inc=1, device_id={"seq": seq, "ch": ch}, device_id_type=MESH)
        pl.semaphore_wait(barrier, len(peers))


class Spread:
    ORDERS = ((0, 1, 2, 3), (0, 2, 1, 3))
    ORIGIN = (0, 0, 0, 0)

    @staticmethod
    def semaphores(seqs):
        dma = pltpu.SemaphoreType.DMA
        return [dma((2, 4 * seqs)), dma((2, 4 * seqs)), dma((1,))]

    def __init__(self, at, src, out, send, recv, local):
        self.at, self.src, self.out, self.send, self.recv = at, src, out, send, recv
        self.half = src.shape[0] // 2
        self.home = pltpu.make_async_copy(src, out.at[at.s * at.chs + at.c], local.at[0])
        self.started = []

    def index(self, role):
        return ((role[0] * 2 + role[1]) * 2 + role[2]) * 2 + role[3]

    def piece(self, cut, role):
        at = self.at
        dz, dx, dy, do = role
        src = lax.rem(at.z + at.depth - dz, at.depth) * 2 + (1 - at.x if dx else at.x)
        col = (1 - at.y if dy else at.y) * 2 + (1 - at.o if do else at.o)
        return self.out.at[src * at.chs + col, pl.ds(cut * self.half, self.half)]

    def forward(self, cut, role, axis, step=1):
        at = self.at
        peer = (at.deep[step - 1], at.beside, at.across, at.side)[axis]
        src = self.piece(cut, role)
        if role == self.ORIGIN:
            src = self.src.at[pl.ds(cut * self.half, self.half)]
        index = self.index(tuple(step if i == axis else v for i, v in enumerate(role)))
        copy = remote(src, self.piece(cut, role), self.send.at[cut, index], self.recv.at[cut, index], peer)
        copy.start()
        self.started.append(copy)

    def arrived(self, cut, role):
        spot, index = self.piece(cut, role), self.index(role)
        remote(spot, spot, self.send.at[cut, index], self.recv.at[cut, index], self.at.side).wait_recv()

    def start(self):
        for cut in range(2):
            for step in range(1, self.at.depth):
                self.forward(cut, self.ORIGIN, 0, step)
        for cut in range(2):
            for axis in self.ORDERS[cut][1:]:
                self.forward(cut, self.ORIGIN, axis)
        self.home.start()

    def relay(self, level):
        for cut in range(2):
            order = self.ORDERS[cut]
            for step in range(self.at.depth):
                for extra in range(max(level, 1)):
                    role = [step, 0, 0, 0]
                    if level:
                        role[order[level]] = 1
                    if extra:
                        role[order[1]] = 1
                    role = tuple(role)
                    if role == self.ORIGIN:
                        continue
                    self.arrived(cut, role)
                    for axis in order[level + 1 :]:
                        self.forward(cut, role, axis)

    def finish(self):
        for cut in range(2):
            for step in range(self.at.depth):
                for dx in range(2):
                    for dy in range(2):
                        self.arrived(cut, (step, dx, dy, 1))
        self.home.wait()
        for copy in self.started:
            copy.wait_send()


class Trade:
    @staticmethod
    def semaphores(seqs):
        dma = pltpu.SemaphoreType.DMA
        return [dma((seqs - 1,)), dma((seqs - 1,)), dma((1,))]

    def __init__(self, at, src_for, dst, send, recv, local):
        self.copies = [
            remote(src_for(peer[0]), dst, send.at[k], recv.at[k], peer) for k, peer in enumerate(at.others)
        ]
        self.home = pltpu.make_async_copy(src_for(at.s), dst, local.at[0])

    def start(self):
        for copy in self.copies:
            copy.start()
        self.home.start()

    def finish(self):
        for copy in self.copies:
            copy.wait_recv()
        self.home.wait()
        for copy in self.copies:
            copy.wait_send()


class Share:
    @staticmethod
    def semaphores(seqs, cuts):
        dma = pltpu.SemaphoreType.DMA
        return [dma((cuts, seqs // 2))] * 4 + [dma((1,))]

    def __init__(self, at, src, out, cuts, send, recv, hop_s, hop_r, local):
        self.at, self.src, self.out, self.cuts = at, src, out, cuts
        self.size = src.shape[0] // cuts
        self.z = (send, recv)
        self.x = (hop_s, hop_r)
        self.home = pltpu.make_async_copy(src, out.at[at.s], local.at[0])

    def rows(self, cut):
        return pl.ds(cut * self.size, self.size)

    def deep(self, cut, k):
        at = self.at
        return remote(
            self.src.at[self.rows(cut)], self.out.at[at.s, self.rows(cut)],
            self.z[0].at[cut, k - 1], self.z[1].at[cut, k - 1], at.deep[k - 1],
        )

    def beside(self, cut, k):
        at = self.at
        owner = lax.rem(at.z + at.depth - k, at.depth) * 2 + at.x
        spot = self.out.at[owner, self.rows(cut)]
        src = spot if k else self.src.at[self.rows(cut)]
        return remote(src, spot, self.x[0].at[cut, k], self.x[1].at[cut, k], at.beside)

    def start(self):
        for cut in range(self.cuts):
            for k in range(1, self.at.depth):
                self.deep(cut, k).start()
            self.beside(cut, 0).start()
        self.home.start()

    def relay(self, cut):
        for k in range(1, self.at.depth):
            self.deep(cut, k).wait_recv()
            self.beside(cut, k).start()

    def finish(self):
        for cut in range(self.cuts):
            for k in range(self.at.depth):
                self.beside(cut, k).wait_recv()
        self.home.wait()
        for cut in range(self.cuts):
            for k in range(1, self.at.depth):
                self.deep(cut, k).wait_send()
            for k in range(self.at.depth):
                self.beside(cut, k).wait_send()


class Total:
    @staticmethod
    def scratch(seqs, rows):
        depth = seqs // 2
        n = 2 * (depth + 2)
        dma = pltpu.SemaphoreType.DMA

        def vmem(*shape):
            return pltpu.VMEM(shape + (LANES,), F32)

        return [
            vmem(rows), vmem(rows // 2), vmem(rows // 4), vmem(rows // 8), vmem(depth - 1, rows // 8 // depth),
            vmem(rows // 2), vmem(rows // 4), vmem(rows // 8), dma((n,)), dma((n,)),
        ]

    def __init__(self, at, out, own, r0, r1, r2, r3, a1, a2, a3, send, recv):
        self.at, self.out, self.own = at, out, own
        self.got, self.held = (r0, r1, r2), (own, a1, a2, a3)
        self.last, self.send, self.recv = r3, send, recv
        self.block = (at.o * 2 + at.y) * 2 + at.x
        self.sends = []

    def halve(self, n):
        at = self.at
        bit, peer = ((at.o, at.side), (at.y, at.across), (at.x, at.beside))[n]
        size = self.own.shape[0] >> (n + 1)
        src, dst = self.held[n], self.held[n + 1]
        copy = remote(src.at[rows_at(1 - bit, size)], self.got[n], self.send.at[n], self.recv.at[n], peer)
        copy.start()
        copy.wait_recv()
        dst[...] = src[rows_at(bit, size)] + self.got[n][...]
        self.sends.append(copy)

    def meet(self):
        at = self.at
        size = self.own.shape[0] // 8 // at.depth
        last = self.held[3]
        copies = []
        for k, peer in enumerate(at.deep):
            there = lax.rem(at.z + 1 + k, at.depth)
            copies.append(
                remote(last.at[rows_at(there, size)], self.last.at[k], self.send.at[3 + k], self.recv.at[3 + k], peer)
            )
            copies[-1].start()
        total = last[rows_at(at.z, size)]
        for k, copy in enumerate(copies):
            copy.wait_recv()
            total = total + self.last[k]
        self.sends += copies
        self.out[rows_at(self.block * at.depth + at.z, size)] = total
        base = at.depth + 2
        spot = self.out.at[rows_at(self.block * at.depth + at.z, size)]
        copies = []
        for k, peer in enumerate(at.deep):
            copies.append(remote(spot, spot, self.send.at[base + k], self.recv.at[base + k], peer))
            copies[-1].start()
        for copy in copies:
            copy.wait_recv()
        self.sends += copies

    def double(self, n):
        at = self.at
        size = self.own.shape[0] >> (n + 1)
        index, peer = ((at.o, at.side), (at.o * 2 + at.y, at.across), (self.block, at.beside))[n]
        spot = self.out.at[rows_at(index, size)]
        base = 2 * at.depth + 1 + n
        copy = remote(spot, spot, self.send.at[base], self.recv.at[base], peer)
        copy.start()
        copy.wait_recv()
        self.sends.append(copy)

    def finish(self):
        for copy in self.sends:
            copy.wait_send()


class Regroup:
    @staticmethod
    def scratch(seqs, chs, tokens, part):
        folds, vmem, dma = seqs // chs, pltpu.VMEM, pltpu.SemaphoreType.DMA
        rows = tokens // seqs
        return [
            vmem((tokens // 2, part), F32), vmem((tokens // 2, part), F32), vmem((tokens // 4, part), BF16),
            vmem((tokens // 4, part), BF16), vmem((tokens // 4, part), BF16), vmem((folds, rows, part), BF16),
            dma((2,)), dma((2,)), dma((folds,)), dma((folds,)),
        ]

    @staticmethod
    def sources(at):
        folds = at.seqs // at.chs
        return [(at.c * folds + f, Regroup.owner(at)) for f in range(folds)]

    @staticmethod
    def owner(at):
        home = at.s // (at.seqs // at.chs)
        return lax.rem(home, 2) * 2 + home // 2

    def __init__(self, at, src, r0, a1, sb, r1, fb, r2, send, recv, fsend, frecv):
        self.at, self.src = at, src
        self.r0, self.a1, self.sb, self.r1, self.fb, self.r2 = r0, a1, sb, r1, fb, r2
        self.fsend, self.frecv = fsend, frecv
        self.half, self.quarter = r0.shape[0], r1.shape[0]
        self.folds = at.seqs // at.chs
        self.rows = self.quarter // self.folds
        self.first = remote(src.at[rows_at(1 - at.o, self.half)], r0, send.at[0], recv.at[0], at.side)
        self.second = remote(sb, r1, send.at[1], recv.at[1], at.across)

    def one(self):
        self.first.start()

    def two(self):
        at = self.at
        self.first.wait_recv()
        self.a1[...] = self.src[rows_at(at.o, self.half)] + self.r0[...]
        self.sb[...] = self.a1[rows_at(1 - at.y, self.quarter)].astype(BF16)
        self.second.start()

    def hops(self):
        at = self.at
        home, slot = at.s // self.folds, lax.rem(at.s, self.folds)
        quarter = at.o * 2 + at.y
        for f in range(self.folds):
            there = quarter * self.folds + f
            away = jnp.logical_or(there != at.s, home != at.c)
            src, dst = self.fb.at[pl.ds(f * self.rows, self.rows)], self.r2.at[slot]
            yield away, remote(src, dst, self.fsend.at[f], self.frecv.at[slot], (there, home)), (src, dst, slot)

    def three(self):
        at = self.at
        self.second.wait_recv()
        self.fb[...] = (self.a1[rows_at(at.y, self.quarter)] + self.r1[...].astype(F32)).astype(BF16)
        for away, copy, (src, dst, slot) in self.hops():
            pl.when(away)(copy.start)
            pl.when(jnp.logical_not(away))(pltpu.make_async_copy(src, dst, self.frecv.at[slot]).start)

    def result(self):
        for f in range(self.folds):
            spot = self.fb.at[pl.ds(0, self.rows)]
            remote(spot, self.r2.at[f], self.fsend.at[f], self.frecv.at[f], self.at.side).wait_recv()
        return jnp.concatenate([self.r2[f] for f in range(self.folds)], axis=1).astype(F32)

    def finish(self):
        self.first.wait_send()
        self.second.wait_send()
        for away, copy, _ in self.hops():
            pl.when(away)(copy.wait_send)


def split(refs, *counts):
    out, start = [], 0
    for count in counts:
        out.append(refs[start : start + count])
        start += count
    return out

ANY = pl.BlockSpec(memory_space=pl.ANY)
WHOLE = pl.BlockSpec(memory_space=pltpu.VMEM)
SCALAR = pl.BlockSpec(memory_space=pltpu.SMEM)


def comm(kernel, ins, outs, scratch, ident, name, moved):
    return pl.pallas_call(
        kernel,
        out_shape=[jax.ShapeDtypeStruct(shape, dtype) for shape, dtype, _ in outs],
        in_specs=[spec for _, spec in ins],
        out_specs=[spec for _, _, spec in outs],
        scratch_shapes=scratch,
        compiler_params=pltpu.CompilerParams(
            collective_id=ident, has_side_effects=True, vmem_limit_bytes=60 * 2**20
        ),
        cost_estimate=pl.CostEstimate(flops=0, bytes_accessed=moved, transcendentals=0),
        name=name,
    )(*[array for array, _ in ins])


def per_device(
    stream, norm_gain, w_in, conv_w, conv_b, w_xdt, w_xbc, w_dt, dt_bias, a_log, d_skip, w_out,
    cotangent, seg_ids, modality,
):
    seqs, chs = lax.axis_size("seq"), lax.axis_size("ch")
    s = lax.axis_index("seq")
    rows, cols = stream.shape
    tokens, width = seg_ids.shape[0], norm_gain.shape[0]
    channels = conv_b.shape[0]
    own = channels // seqs
    part = width // seqs
    flat = tokens * STATE // LANES
    dma, vmem = pltpu.SemaphoreType.DMA, pltpu.VMEM
    bound = jnp.sum(seg_ids == 0).astype(jnp.int32)[None]
    mod = jnp.broadcast_to(modality.astype(F32)[None], (8, rows))
    own_rows = jnp.concatenate([a_log, d_skip[None], conv_b[None], conv_w, dt_bias], 0)
    own_rows = lax.dynamic_slice_in_dim(own_rows, s * own, own, 1)
    gain = norm_gain[None]
    xdbl, u, conv, x_pre, d_y, dt, sig, gated, d_gate, hs, normed, cot, inv, wx, wdt, mod, d_skip_own = comm(
        partial(forward_kernel, seqs, chs),
        [
            (bound, SCALAR), (stream, ANY), (cotangent, ANY), (w_in, ANY), (w_out, ANY), (w_xdt, ANY), (w_dt, ANY),
            (mod, ANY), (gain, WHOLE), (w_xbc, WHOLE), (own_rows, WHOLE),
        ],
        [
            ((tokens + 2 * flat, LANES), F32, WHOLE),
            ((tokens, own), BF16, WHOLE),
            ((tokens, own), F32, WHOLE),
            ((tokens, own), BF16, WHOLE),
            ((tokens, own), F32, WHOLE),
            ((tokens, own), F32, WHOLE),
            ((tokens, own), F32, WHOLE),
            ((tokens, own), BF16, WHOLE),
            ((tokens, own), BF16, WHOLE),
            ((tokens + 1, STATE, own), F32, ANY),
            ((tokens, part), BF16, WHOLE),
            ((tokens, part), BF16, ANY),
            ((tokens, LANES), F32, WHOLE),
            ((2, RANK, own), BF16, WHOLE),
            ((2, RANK, own), BF16, WHOLE),
            ((seqs, 8, rows), F32, WHOLE),
            ((1, own), F32, WHOLE),
        ],
        Total.scratch(seqs, tokens + 2 * flat) + 2 * Spread.semaphores(seqs) + 5 * Trade.semaphores(seqs)
        + [
            vmem((seqs * chs, rows, cols), BF16), vmem((seqs * chs, rows, cols), BF16),
            vmem((2, 2, width, own), BF16), vmem((2, own, width), BF16),
            vmem((tokens, own), F32), vmem((tokens, own), F32), vmem((ROWS + 8, own), F32), vmem((ROWS, width), BF16),
            vmem((STATE, own), F32), vmem((CHUNK, own), F32), vmem((CHUNK, STATE, own), F32),
            vmem((2, CHUNK, STATE, own), F32), dma((3 + seqs,)),
        ],
        1, "forward", 64 << 20,
    )
    output, grad_stream, sums, own_w_in, own_w_out, small, parts = comm(
        partial(backward_kernel, seqs, chs),
        [
            (bound, SCALAR), (xdbl, WHOLE), (u, WHOLE), (conv, ANY), (x_pre, ANY), (d_y, WHOLE), (dt, WHOLE),
            (sig, WHOLE), (gated, WHOLE), (d_gate, WHOLE), (hs, ANY), (normed, ANY), (cot, ANY), (inv, ANY),
            (wx, WHOLE), (wdt, WHOLE), (mod, WHOLE), (d_skip_own, WHOLE), (w_xbc, WHOLE), (own_rows, WHOLE),
            (w_in, ANY), (w_out, ANY), (gain, WHOLE), (stream, WHOLE), (cotangent, WHOLE),
        ],
        [
            ((rows, cols), BF16, WHOLE),
            ((rows, cols), F32, WHOLE),
            ((chs, 8, cols), F32, WHOLE),
            (w_in.shape, F32, WHOLE),
            (w_out.shape, F32, WHOLE),
            ((96, channels), F32, WHOLE),
            ((2, 2, RANK // seqs, channels), F32, ANY),
        ],
        Total.scratch(seqs, tokens + 2 * flat) + 2 * Regroup.scratch(seqs, chs, tokens, part)
        + 3 * Share.semaphores(seqs, CUTS) + 2 * Trade.semaphores(seqs)
        + [
            vmem((tokens + 2 * flat, LANES), F32), vmem((tokens, own), F32), vmem((tokens, own), BF16),
            vmem((seqs, tokens, own), BF16), vmem((seqs, tokens, own), BF16), vmem((seqs, tokens, own), BF16),
            vmem((tokens, own), F32), vmem((tokens, own), BF16), vmem((tokens, part), BF16), vmem((tokens, part), BF16),
            vmem(w_in.shape, BF16), vmem(w_out.shape, BF16), vmem((rows, LANES), F32),
            vmem((tokens, part), F32), vmem((tokens, part), F32), vmem((2, CHUNK + 1, STATE, own), F32),
            vmem((STATE, own), F32), vmem((STATE, own), F32), vmem((CHUNK, own), F32), vmem((CHUNK, STATE, own), F32),
            vmem((CHUNK, STATE, own), BF16), vmem((CHUNK, STATE, own), BF16),
            vmem((ROWS + 8, own), F32), vmem((ROWS + 8, own), F32), vmem((2, 2, RANK, own), F32),
            vmem((2, 2 * STATE, own), F32), vmem((2, own), F32), vmem((8, own), F32),
            vmem((96, own), F32), vmem((seqs, 96, own), F32), vmem((8, rows), F32), vmem((chs - 1, 8, rows), F32),
            vmem((8, cols), F32), vmem((seqs - 1, 8, cols), F32),
            dma((2,)), dma((7,)), dma((chs - 1,)), dma((chs - 1,)), dma((seqs - 1,)), dma((seqs - 1,)),
            dma((chs - 1,)), dma((chs - 1,)),
        ],
        2, "backward", 64 << 20,
    )
    return (
        output,
        grad_stream,
        sums[:, 0].reshape(width),
        own_w_in,
        small[STATE : STATE + CONV],
        small[STATE + CONV],
        parts[0],
        small[32:].reshape(w_xbc.shape),
        parts[1],
        small[24:26],
        small[:STATE],
        small[26],
        own_w_out,
        jnp.sqrt(jnp.sum(sums[:, 1:4], axis=(0, 2)) / float(tokens * width)),
    )


def per_device_by_token(
    stream,
    norm_gain,
    w_in,
    conv_w,
    conv_b,
    w_xdt,
    w_xbc,
    w_dt,
    dt_bias,
    a_log,
    d_skip,
    w_out,
    cotangent,
    seg_ids,
    modality,
):
    length = stream.shape[0]
    channels = conv_b.shape[0]
    model_width = norm_gain.shape[0]
    mod_count = w_in.shape[0]
    rim_len = CONV - 1
    ch_start = lax.axis_index("ch") * channels
    col_start = lax.axis_index("ch") * stream.shape[1]
    x_full, grad_full = (
        lax.all_gather(stream, "ch", axis=1, tiled=True),
        lax.all_gather(cotangent, "ch", axis=1, tiled=True),
    )
    w_in_full, w_xdt_full, w_dt_full, w_out_full = (
        lax.all_gather(w_in, "seq", axis=2, tiled=True),
        lax.all_gather(w_xdt, "seq", axis=1, tiled=True),
        lax.all_gather(w_dt, "seq", axis=1, tiled=True),
        lax.all_gather(w_out, "seq", axis=2, tiled=True),
    )
    mod_mask = modality[None, :] == jnp.arange(mod_count, dtype=jnp.int32)[:, None]
    mod_float = mod_mask.astype(jnp.float32)

    def by_mod(value):
        chosen = mod_mask.reshape(mod_mask.shape + (1,) * (value.ndim - 1))
        return jnp.where(chosen, value[None], jnp.zeros((), value.dtype))

    stream_f = x_full.astype(jnp.float32)
    inv_rms = lax.rsqrt(jnp.mean(stream_f * stream_f, axis=1, keepdims=True) + EPSILON)
    x_hat = stream_f * inv_rms
    normed = (x_hat * norm_gain[None, :]).astype(jnp.bfloat16)
    normed_split = by_mod(normed)
    projected = jnp.einsum(
        "mtd,mkde->tke", normed_split, w_in_full, preferred_element_type=jnp.float32
    )
    x_pre = projected[:, 0].astype(jnp.bfloat16)
    gate_in = projected[:, 1]
    rim_rows = passed_along(x_pre[length - rim_len :], "seq", 1)
    padded_seg = jnp.concatenate([jnp.full((rim_len,), -1, jnp.int32), seg_ids])
    seg_win = lax.dynamic_slice_in_dim(padded_seg, lax.axis_index("seq") * length, length + rim_len)
    seg_now = seg_win[rim_len:]
    extended = jnp.concatenate([rim_rows, x_pre], 0).astype(jnp.float32)
    tap_mask = [
        (seg_win[offset : offset + length] == seg_now).astype(jnp.float32)[:, None]
        for offset in range(CONV)
    ]
    conv_out = conv_b[None, :] + sum(
        (
            conv_w[offset][None, :] * extended[offset : offset + length] * tap_mask[offset]
            for offset in range(CONV)
        )
    )
    u_val = (conv_out * jax.nn.sigmoid(conv_out)).astype(jnp.bfloat16)
    u_split = by_mod(u_val)
    dt_part = jnp.einsum("mte,mre->tr", u_split, w_xdt_full, preferred_element_type=jnp.float32)
    bc_part = jnp.einsum("mte,mne->tn", u_split, w_xbc, preferred_element_type=jnp.float32)
    dt_sum, bc_sum = lax.psum((dt_part, bc_part), "ch")
    dt_low = dt_sum.astype(jnp.bfloat16)
    b_in = bc_sum[:, :STATE]
    c_out = bc_sum[:, STATE:]
    low_split = by_mod(dt_low)
    dt_raw = jnp.einsum(
        "mtr,mre->te", low_split, w_dt_full, preferred_element_type=jnp.float32
    ) + jnp.dot(mod_float.T, dt_bias, precision=PRECISE)
    dt_val = jax.nn.softplus(dt_raw)
    u_float = u_val.astype(jnp.float32)
    dt_u = dt_val * u_float
    neg_a = -jnp.exp(a_log)
    keep_mask = (seg_now == seg_win[rim_len - 1 : rim_len - 1 + length]).astype(jnp.float32)
    decay_all = jnp.exp(neg_a * jnp.sum(dt_val, axis=0)[None, :]) * jnp.prod(keep_mask)
    zero_state = jnp.zeros_like(neg_a)
    local_end, _, _ = run_forward(zero_state, dt_val, dt_u, b_in, c_out, keep_mask, neg_a)
    _, start_state = entering(
        (decay_all, local_end), "seq", chain_link, (jnp.ones_like(neg_a), zero_state), False
    )
    _, starts, y_ssm = run_forward(start_state, dt_val, dt_u, b_in, c_out, keep_mask, neg_a)
    y_val = y_ssm + d_skip[None, :] * u_float
    sig_gate = jax.nn.sigmoid(gate_in)
    gated = (y_val * (gate_in * sig_gate)).astype(jnp.bfloat16)
    gated_split = by_mod(gated)
    branch = lax.psum_scatter(
        jnp.einsum("mte,med->dt", gated_split, w_out_full, preferred_element_type=jnp.float32),
        "ch",
        scatter_dimension=0,
        tiled=True,
    ).T
    x_own = stream.astype(jnp.float32)
    mixed = x_own + branch
    output = mixed.astype(jnp.bfloat16)
    stats_part = jnp.stack(
        [jnp.sum(x_own * x_own), jnp.sum(branch * branch), jnp.sum(mixed * mixed)]
    )
    grad_split = by_mod(grad_full)
    d_gated = jnp.einsum("mtd,med->te", grad_split, w_out_full, preferred_element_type=jnp.float32)
    d_w_out = jnp.einsum("mte,td->med", gated_split, grad_full, preferred_element_type=jnp.float32)
    d_y = d_gated * gate_in * sig_gate
    d_gate = d_gated * y_val * silu_grad(gate_in)
    d_skip_part = jnp.sum(d_y * u_float, axis=0)
    local_back = local_adjoint(dt_val, c_out, keep_mask, d_y, neg_a)
    _, incoming = entering(
        (decay_all, local_back), "seq", chain_link, (jnp.ones_like(neg_a), zero_state), True
    )
    d_neg, d_dt_ssm, d_dtu, d_b, d_c = run_adjoint(
        incoming, starts, dt_val, dt_u, b_in, c_out, keep_mask, d_y, neg_a
    )
    d_a_log = d_neg * neg_a
    d_dt = d_dt_ssm + d_dtu * u_float
    d_u = d_y * d_skip[None, :] + d_dtu * dt_val
    d_raw = (d_dt * jax.nn.sigmoid(dt_raw)).astype(jnp.bfloat16)
    d_w_dt = jnp.einsum("mtr,te->mre", low_split, d_raw, preferred_element_type=jnp.float32)
    d_dt_bias = jnp.dot(mod_float, d_raw.astype(jnp.float32), precision=PRECISE)
    d_low_part = jnp.einsum(
        "mte,mre->tr", by_mod(d_raw), w_dt_full, preferred_element_type=jnp.float32
    )
    d_bc_part = jnp.concatenate([d_b, d_c], 1)
    d_low_sum, d_bc_sum = lax.psum((d_low_part, d_bc_part), "ch")
    d_low = d_low_sum.astype(jnp.bfloat16)
    d_bc = d_bc_sum.astype(jnp.bfloat16)
    d_w_xdt = jnp.einsum("mte,tr->mre", u_split, d_low, preferred_element_type=jnp.float32)
    d_w_xbc = jnp.einsum("mte,tn->mne", u_split, d_bc, preferred_element_type=jnp.float32)
    d_u = d_u + jnp.einsum(
        "mtr,mre->te", by_mod(d_low), w_xdt_full, preferred_element_type=jnp.float32
    )
    d_u = d_u + jnp.einsum("mtn,mne->te", by_mod(d_bc), w_xbc, preferred_element_type=jnp.float32)
    d_conv = d_u * silu_grad(conv_out)
    d_conv_b = jnp.sum(d_conv, axis=0)
    d_conv_w = jnp.stack(
        [
            jnp.sum(d_conv * extended[offset : offset + length] * tap_mask[offset], axis=0)
            for offset in range(CONV)
        ]
    )
    d_ext = sum(
        (
            jnp.pad(
                conv_w[offset][None, :] * d_conv * tap_mask[offset],
                ((offset, rim_len - offset), (0, 0)),
            )
            for offset in range(CONV)
        )
    )
    back_rim = passed_along(d_ext[:rim_len], "seq", -1)
    d_pre = d_ext[rim_len:] + jnp.pad(back_rim, ((length - rim_len, 0), (0, 0)))
    d_xz = jnp.stack([d_pre, d_gate], 1).astype(jnp.bfloat16)
    d_w_in = jnp.einsum("mtd,tke->mkde", normed_split, d_xz, preferred_element_type=jnp.float32)
    d_norm_part = jnp.einsum(
        "mtke,mkde->dt", by_mod(d_xz), w_in_full, preferred_element_type=jnp.float32
    )
    d_gain_part = jnp.einsum("dt,td->d", d_norm_part, x_hat, precision=PRECISE)
    d_norm = lax.psum(d_norm_part, "ch").T
    d_hat = d_norm * norm_gain[None, :]
    inner_dot = jnp.mean(d_hat * x_hat, axis=1, keepdims=True)
    d_x_full = inv_rms * (d_hat - x_hat * inner_dot)
    grad_stream = lax.dynamic_slice_in_dim(
        d_x_full, col_start, stream.shape[1], 1
    ) + cotangent.astype(jnp.float32)
    own_w_in, own_w_xdt, own_w_dt, own_w_out = (
        lax.psum_scatter(d_w_in, "seq", scatter_dimension=2, tiled=True),
        lax.psum_scatter(d_w_xdt, "seq", scatter_dimension=1, tiled=True),
        lax.psum_scatter(d_w_dt, "seq", scatter_dimension=1, tiled=True),
        lax.psum_scatter(d_w_out, "seq", scatter_dimension=2, tiled=True),
    )

    def spread(value):
        full_shape = value.shape[:-1] + (INNER,)
        return lax.dynamic_update_slice_in_dim(
            jnp.zeros(full_shape, jnp.float32), value, ch_start, value.ndim - 1
        )

    def own_slice(value):
        return lax.dynamic_slice_in_dim(value, ch_start, channels, value.ndim - 1)

    summed = lax.psum(
        (
            spread(d_conv_w),
            spread(d_conv_b),
            spread(d_w_xbc),
            spread(d_dt_bias),
            spread(d_a_log),
            spread(d_skip_part),
            d_gain_part,
            stats_part,
        ),
        ("seq", "ch"),
    )
    stats = jnp.sqrt(summed[7] / float(length * lax.axis_size("seq") * model_width))
    return (
        output,
        grad_stream,
        summed[6],
        own_w_in,
        own_slice(summed[0]),
        own_slice(summed[1]),
        own_w_xdt,
        own_slice(summed[2]),
        own_w_dt,
        own_slice(summed[3]),
        own_slice(summed[4]),
        own_slice(summed[5]),
        own_w_out,
        stats,
    )


def solution(mesh):
    in_specs = (
        P("seq", "ch"),
        P(),
        P(None, None, "seq", "ch"),
        P(None, "ch"),
        P("ch"),
        P(None, "seq", "ch"),
        P(None, None, "ch"),
        P(None, "seq", "ch"),
        P(None, "ch"),
        P(None, "ch"),
        P("ch"),
        P(None, "ch", "seq"),
        P("seq", "ch"),
        P(),
        P("seq"),
    )
    out_specs = (
        P("seq", "ch"),
        P("seq", "ch"),
        P(),
        P(None, None, "seq", "ch"),
        P(None, "ch"),
        P("ch"),
        P(None, "seq", "ch"),
        P(None, None, "ch"),
        P(None, "seq", "ch"),
        P(None, "ch"),
        P(None, "ch"),
        P("ch"),
        P(None, "ch", "seq"),
        P(),
    )
    seqs, chs = mesh.shape["seq"], mesh.shape["ch"]
    whole_lanes = INNER == seqs * chs * LANES and seqs == 2 * chs and chs == 4
    return jax.shard_map(
        per_device if whole_lanes else per_device_by_token, mesh=mesh, in_specs=in_specs, out_specs=out_specs, check_vma=False
    )
```

```python
from functools import partial

import jax
import jax.numpy as jnp
from jax import lax
from jax.experimental import pallas as pl
from jax.experimental.pallas import tpu as pltpu
from jax.sharding import PartitionSpec as P

INNER = 4096
STATE = 16
CONV = 4
BLK = 64
RANK = 128


EPSILON = 1e-05
PRECISE = lax.Precision.HIGHEST


def passed_along(value, axis, steps):
    count = lax.axis_size(axis)
    initial, last = (max(0, -steps), min(count, count - steps))
    return lax.ppermute(value, axis, [(source, source + steps) for source in range(initial, last)])


def entering(part, axis, combine, identity, reverse):
    count = lax.axis_size(axis)
    place = lax.axis_index(axis)
    ahead = count - 1 - place if reverse else place
    gathered = jax.tree.map(lambda a: lax.all_gather(a, axis), part)
    state = jax.tree.map(lambda a, e: jnp.zeros_like(a) + jnp.asarray(e, a.dtype), part, identity)

    def one(step, state):
        source = count - 1 - step if reverse else step
        return combine(
            state, jax.tree.map(lambda a: lax.dynamic_index_in_dim(a, source, 0, False), gathered)
        )

    return lax.fori_loop(0, ahead, one, state)


def silu_grad(value):
    sigma = jax.nn.sigmoid(value)
    return sigma * (1.0 + value * (1.0 - sigma))


def chain_link(earlier, latter):
    return (earlier[0] * latter[0], latter[0] * earlier[1] + latter[1])


def decay_terms(dt_blk, keep_blk, neg_a):
    return keep_blk[:, None, None] * jnp.exp(dt_blk[:, None, :] * neg_a[None])


def drive_terms(b_blk, dtu_blk):
    return b_blk[:, :, None] * dtu_blk[:, None, :]


def to_blocks(values):
    block_count = values[0].shape[0] // BLK
    return tuple((value.reshape((block_count, BLK) + value.shape[1:]) for value in values))


def run_forward(state_in, dt_val, dt_u, b_in, c_out, keep_mask, neg_a):

    def block_step(state_now, blk_rows):
        dt_blk, dtu_blk, b_blk, c_blk, keep_blk = blk_rows
        cum_a, cum_b = lax.associative_scan(
            chain_link, (decay_terms(dt_blk, keep_blk, neg_a), drive_terms(b_blk, dtu_blk))
        )
        states = cum_a * state_now[None] + cum_b
        y_blk = jnp.einsum("tn,tne->te", c_blk, states, precision=PRECISE)
        return (states[-1], (state_now, y_blk))

    state_end, (starts, y_ssm) = lax.scan(
        block_step, state_in, to_blocks((dt_val, dt_u, b_in, c_out, keep_mask))
    )
    return (state_end, starts, y_ssm.reshape(dt_val.shape))


def adjoint_states(decay, c_blk, dy_blk, incoming):
    source = c_blk[:, :, None] * dy_blk[:, None, :]
    shifted = jnp.concatenate([decay[1:], jnp.ones_like(decay[:1])], 0)
    prod_a, acc_g = lax.associative_scan(chain_link, (shifted, source), reverse=True)
    return prod_a * incoming[None] + acc_g


def local_adjoint(dt_val, c_out, keep_mask, d_y, neg_a):

    def block_step(incoming, blk_rows):
        dt_blk, c_blk, keep_blk, dy_blk = blk_rows
        decay = decay_terms(dt_blk, keep_blk, neg_a)
        adjoint = adjoint_states(decay, c_blk, dy_blk, incoming)
        return (decay[0] * adjoint[0], None)

    outgoing, _ = lax.scan(
        block_step, jnp.zeros_like(neg_a), to_blocks((dt_val, c_out, keep_mask, d_y)), reverse=True
    )
    return outgoing


def run_adjoint(incoming, starts, dt_val, dt_u, b_in, c_out, keep_mask, d_y, neg_a):

    def block_step(carried, blk_rows):
        later_in, d_neg = carried
        state_in, dt_blk, dtu_blk, b_blk, c_blk, keep_blk, dy_blk = blk_rows
        decay = decay_terms(dt_blk, keep_blk, neg_a)
        adjoint = adjoint_states(decay, c_blk, dy_blk, later_in)
        cum_a, cum_b = lax.associative_scan(chain_link, (decay, drive_terms(b_blk, dtu_blk)))
        states = cum_a * state_in[None] + cum_b
        before = jnp.concatenate([state_in[None], states[:-1]], 0)
        flow = adjoint * before * decay
        d_dt_blk = jnp.sum(flow * neg_a[None], axis=1)
        d_neg = d_neg + jnp.einsum("tne,te->ne", flow, dt_blk, precision=PRECISE)
        d_dtu_blk = jnp.einsum("tne,tn->te", adjoint, b_blk, precision=PRECISE)
        d_b_blk = jnp.einsum("tne,te->tn", adjoint, dtu_blk, precision=PRECISE)
        d_c_blk = jnp.einsum("tne,te->tn", states, dy_blk, precision=PRECISE)
        return ((decay[0] * adjoint[0], d_neg), (d_dt_blk, d_dtu_blk, d_b_blk, d_c_blk))

    blk_rows = (starts,) + to_blocks((dt_val, dt_u, b_in, c_out, keep_mask, d_y))
    (_, d_neg), outs = lax.scan(
        block_step, (incoming, jnp.zeros_like(neg_a)), blk_rows, reverse=True
    )
    length = dt_val.shape[0]
    return (d_neg,) + tuple((value.reshape((length,) + value.shape[2:]) for value in outs))


F32 = jnp.float32
BF16 = jnp.bfloat16
LANES = 128
ROWS = 256
CHUNK = 128
GROUP = 16
LOG2E = 1.4426950408889634
CUT = 1e4
CUTS = 8
SKIP, CONV_B, CONV_W, BIAS = STATE, STATE + 1, STATE + 2, STATE + 2 + CONV


def dot(a, b, da, db):
    return lax.dot_general(a, b, (((da,), (db,)), ((), ())), preferred_element_type=F32)


def column(row):
    return jnp.transpose(jnp.broadcast_to(row, (LANES, row.shape[1])))


def silu_slope(value, sigma):
    return sigma * (1.0 + value * (1.0 - sigma))


def flat_mask(rows):
    t = lax.broadcasted_iota(jnp.int32, (rows, LANES), 0)
    lane = lax.broadcasted_iota(jnp.int32, (rows, LANES), 1)
    return lax.rem(t, 8) == lane // STATE


def two_parts(value):
    high = value.astype(BF16).astype(F32)
    return high, value - high


def stacked(value):
    return jnp.concatenate(two_parts(value), axis=0).astype(BF16)


def outer(flat, value, out):
    mask = flat_mask(8)
    for r in range(CHUNK // 8):
        bh, bl = two_parts(jnp.where(mask, flat[r : r + 1], 0.0))
        vh, vl = two_parts(value[8 * r : 8 * r + 8])
        left = jnp.concatenate([bh, bh, bl, bl], axis=0).astype(BF16)
        right = jnp.concatenate([vh, vl, vh, vl], axis=0).astype(BF16)
        out[8 * r : 8 * r + 8] = dot(left, right, 0, 0).reshape(8, STATE, LANES)


def block_at(i, size):
    return pl.ds(pl.multiple_of(i * size, size), size)


def token_at(i, size):
    return i * size + lax.broadcasted_iota(jnp.int32, (size, LANES), 0)


def decay_step(i, bound, dt):
    t = token_at(i, CHUNK)
    return jnp.where((t == 0) | (t == bound), CUT, dt)


class Front:
    def __init__(self, bound, x_all, gain, wi, rows, wx, wbc, mod, own, outs, scratch):
        self.bound, self.x_all, self.gain, self.wi, self.rows, self.wx, self.wbc = bound, x_all, gain, wi, rows, wx, wbc
        self.mod, self.own = mod, own
        self.normed, self.inv, self.xpre, self.conv, self.u, self.gate = outs
        self.ext, self.wide = scratch
        self.ext[0:8] = jnp.zeros((8, LANES), F32)

    def block(self, at, i):
        chs, part = at.chs, self.normed.shape[1]
        tokens = self.u.shape[0]
        span = block_at(i, ROWS)
        x = jnp.concatenate([self.x_all[i * chs + c] for c in range(chs)], axis=1).astype(F32)
        inv = lax.rsqrt(jnp.mean(x * x, axis=1, keepdims=True) + EPSILON)
        normed = (x * inv * self.gain[...]).astype(BF16)
        self.inv[span] = jnp.broadcast_to(inv, (ROWS, LANES))
        self.wide[...] = normed
        self.normed[span] = self.wide[:, lanes_at(at.s, part)]
        image = column(self.mod[i, 0:1]) > 0.5
        both = [dot(normed, jnp.concatenate([self.wi[m, 0], self.wi[m, 1]], axis=1), 1, 0) for m in range(2)]
        x_pre = jnp.where(image, both[1][:, :LANES], both[0][:, :LANES]).astype(BF16)
        self.gate[span] = jnp.where(image, both[1][:, LANES:], both[0][:, LANES:])
        self.xpre[span] = x_pre
        ext = self.ext
        ext[8:] = x_pre.astype(F32)
        t = token_at(i, ROWS)
        conv = None
        for j in range(CONV):
            lag = CONV - 1 - j
            term = self.rows[CONV_W + j : CONV_W + j + 1] * ext[8 - lag : 8 - lag + ROWS]
            if lag:
                term = jnp.where((t < lag) | ((t >= self.bound) & (t - lag < self.bound)), 0.0, term)
            conv = term if conv is None else conv + term
        conv = self.rows[CONV_B : CONV_B + 1] + conv
        self.conv[span] = conv
        ext[0:8] = ext[ROWS : ROWS + 8]
        u = (conv * jax.nn.sigmoid(conv)).astype(BF16)
        self.u[span] = u
        self.own[span] = jnp.where(image, dot(u, self.wx[1], 1, 1), dot(u, self.wx[0], 1, 1))
        mask = flat_mask(ROWS)
        few = ROWS // 8
        for n in range(2):
            tiled = [
                jnp.concatenate([self.wbc[m, n * STATE : (n + 1) * STATE, lanes_at(at.s, LANES)]] * 8, axis=0)
                for m in range(2)
            ]
            wide = jnp.where(mask, jnp.where(image, dot(u, tiled[1], 1, 1), dot(u, tiled[0], 1, 1)), 0.0)
            start = pl.multiple_of(tokens + n * (tokens // 8) + i * few, few)
            self.own[pl.ds(start, few)] = jnp.sum(wide.reshape(few, 8, LANES), axis=1)


def first_of_second(seg_ref):
    return jnp.sum(jnp.where(seg_ref[...] == 0, 1, 0))


def chunk_image(mod, i):
    fold = ROWS // CHUNK
    return column(mod[i // fold, 0:1, lanes_at(lax.rem(i, fold), CHUNK)]) > 0.5


def flats_at(xdbl, i, n):
    tokens = xdbl.shape[0] // 5 * 4
    few = CHUNK // 8
    return xdbl[pl.ds(pl.multiple_of(tokens + n * (tokens // 8) + i * few, few), few)]


def forward_kernel(
    seqs, chs, x_ref, cot_ref, wi_ref, wo_ref, wx_ref, wdt_ref, mod_ref, seg_ref, gain_ref, wbc_ref,
    alog_ref, skip_ref, convb_ref, convw_ref, bias_ref,
    xdbl, u_all, conv_all, xpre_all, dy_all, dt_all, sig_all, gated_all, dgate_all, hs_out, normed_s, cot_s, inv_all,
    wx, wdt, mod, dskip, rows_ref, *rest,
):
    totals, spread1, spread2, trades, rest = split(rest, 10, 3, 3, 15, 14)
    x_all, cot_all, wi, wo, gate_all, y_all, ext, wide, h_s, dta_s, x_s, hbuf, mod_own, sems = rest
    at = Place(seqs, chs)
    bound = first_of_second(seg_ref)
    mod_own[...] = jnp.broadcast_to(mod_ref[...].astype(F32), mod_own.shape)
    mine = lanes_at(at.s, LANES)
    rows_ref[...] = jnp.concatenate(
        [alog_ref[:, mine], skip_ref[:, mine], convb_ref[:, mine], convw_ref[:, mine], bias_ref[:, mine]], axis=0
    )
    own, part, low = LANES, wi_ref.shape[2], wx_ref.shape[1]
    tokens = u_all.shape[0]
    total = Total(at, xdbl, *totals)
    stream = Spread(at, x_ref, x_all, *spread1)
    cot = Spread(at, cot_ref, cot_all, *spread2)
    lows = pl.ds(pl.multiple_of(at.s * low, 16), low)
    plans = [
        (lambda t: wi_ref.at[:, :, :, lanes_at(t, own)], wi.at[:, :, rows_at(at.s, part)]),
        (lambda t: wx_ref.at[:, :, lanes_at(t, own)], wx.at[:, lows]),
        (lambda t: mod_own, mod.at[at.s]),
        (lambda t: wdt_ref.at[:, :, lanes_at(t, own)], wdt.at[:, lows]),
        (lambda t: wo_ref.at[:, rows_at(t, own)], wo.at[:, :, lanes_at(at.s, part)]),
    ]
    trades = [Trade(at, src, dst, *trades[3 * n : 3 * n + 3]) for n, (src, dst) in enumerate(plans)]
    at.greet(at.others + [at.side, at.across])
    stream.post()
    stream.post_near()
    for trade in trades[:4]:
        trade.start()
    for level in range(3):
        stream.relay(level)
    stream.finish()
    for trade in trades[:4]:
        trade.finish()
    front = Front(
        bound, x_all, gain_ref, wi, rows_ref, wx, wbc_ref, mod, total.own,
        (normed_s, inv_all, xpre_all, conv_all, u_all, gate_all), (ext, wide),
    )

    trades[4].start()
    run(tokens // ROWS, partial(front.block, at), {})
    total.halve(0)
    total.halve(1)
    total.halve(2)
    total.meet()
    total.part()
    cot.post()
    total.parted()
    total.double(2)
    total.double(1)
    cot.post_near()
    total.double(0)
    rate = -jnp.exp(rows_ref[0:STATE]) * LOG2E
    h_s[...] = jnp.zeros_like(h_s)
    first = pltpu.make_async_copy(h_s, hs_out.at[0], sems.at[2])
    first.start()
    first.wait()

    def out_copy(i, slot):
        start = i * CHUNK + 1
        return pltpu.make_async_copy(hbuf.at[slot], hs_out.at[pl.ds(start, CHUNK)], sems.at[slot])

    def scan_step(i):
        slot = lax.rem(i, 2)
        span = block_at(i, CHUNK)
        image = chunk_image(mod, i)
        low = xdbl[span].astype(BF16)
        raw = jnp.where(
            image,
            dot(low, wdt[1], 1, 0) + rows_ref[BIAS + 1 : BIAS + 2],
            dot(low, wdt[0], 1, 0) + rows_ref[BIAS : BIAS + 1],
        )
        dt = jnp.maximum(raw, 0.0) + jnp.log1p(jnp.exp(-jnp.abs(raw)))
        u = u_all[span].astype(F32)
        dt_all[span] = dt
        sig_all[span] = jax.nn.sigmoid(raw)
        dta_s[...] = decay_step(i, bound, dt)
        outer(flats_at(xdbl, i, 0), dt * u, x_s)

        @pl.when(i >= 2)
        def _():
            out_copy(i - 2, slot).wait()

        def group(g, h):
            base = pl.multiple_of(g * GROUP, GROUP)
            for k in range(GROUP):
                h = jnp.exp2(dta_s[pl.ds(base + k, 1)] * rate) * h + x_s[base + k]
                hbuf[slot, base + k] = h
            return h

        h_s[...] = lax.fori_loop(0, CHUNK // GROUP, group, h_s[...])
        out_copy(i, slot).start()
        c_all = flats_at(xdbl, i, 1)
        mask = flat_mask(8)
        parts = []
        for r in range(CHUNK // 8):
            left = stacked(jnp.where(mask, c_all[r : r + 1], 0.0))
            made = dot(left, hbuf[slot, 8 * r : 8 * r + 8].reshape(8 * STATE, LANES).astype(BF16), 1, 0)
            parts.append(made[0:8] + made[8:16])
        y = jnp.concatenate(parts, axis=0) + rows_ref[SKIP : SKIP + 1] * u
        y_all[span] = y
        gate = gate_all[span]
        gated_all[span] = (y * (gate * jax.nn.sigmoid(gate))).astype(BF16)

    chunks = tokens // CHUNK
    run(chunks, scan_step, {4 * n + 3: [partial(cot.relay, n)] for n in range(3)})
    cot.finish()
    trades[4].finish()
    folds = seqs // chs
    slices = []
    for n in range(seqs):
        src = cot_all.at[n * chs + at.s // folds, :, lanes_at(lax.rem(at.s, folds), part)]
        slices.append(pltpu.make_async_copy(src, cot_s.at[pl.ds(n * ROWS, ROWS)], sems.at[3 + n]))
        slices[-1].start()
    dskip[...] = jnp.zeros_like(dskip)

    def gate_step(i):
        span = block_at(i, ROWS)
        image = column(mod[i, 0:1]) > 0.5
        cots = jnp.concatenate([cot_all[i * chs + c] for c in range(chs)], axis=1)
        d_gated = jnp.where(image, dot(cots, wo[1], 1, 1), dot(cots, wo[0], 1, 1))
        gate = gate_all[span]
        sigma = jax.nn.sigmoid(gate)
        d_y = d_gated * gate * sigma
        dy_all[span] = d_y
        dgate_all[span] = (d_gated * y_all[span] * silu_slope(gate, sigma)).astype(BF16)
        dskip[...] += jnp.sum(d_y * u_all[span].astype(F32), axis=0, keepdims=True)

    run(tokens // ROWS, gate_step, {})
    for i in (chunks - 2, chunks - 1):
        out_copy(i, i % 2).wait()
    for copy in slices:
        copy.wait()
    total.finish()


def adjoint_chunk(bound, i, state, xdbl, u_all, dy_all, dt_all, sig_all, mod, wdt, rows_ref, own, du_all, grads, scratch):
    ga_s, dn_s, dta_s, x_s, g_s, f_s = scratch
    dwdt, dbias = grads
    tokens = u_all.shape[0]
    span = block_at(i, CHUNK)
    dt = dt_all[span]
    u = u_all[span].astype(F32)
    d_y = dy_all[span]
    dta_s[...] = decay_step(i, bound, dt)
    neg_a = -jnp.exp(rows_ref[0:STATE])
    rate = neg_a * LOG2E
    outer(flats_at(xdbl, i, 1), d_y, x_s)
    start = pl.multiple_of(i * CHUNK, CHUNK)

    def group(step, carried):
        ga, dn = carried
        base = pl.multiple_of((CHUNK // GROUP - 1 - step) * GROUP, GROUP)
        for k in reversed(range(GROUP)):
            adjoint = x_s[base + k] + ga
            ga = jnp.exp2(dta_s[pl.ds(base + k, 1)] * rate) * adjoint
            slow = ga * state[base + k] * neg_a
            dn = dn + slow * dt_all[pl.ds(start + base + k, 1)]
            g_s[base + k] = adjoint.astype(BF16)
            f_s[base + k] = slow.astype(BF16)
        return ga, dn

    ga, dn = lax.fori_loop(0, CHUNK // GROUP, group, (ga_s[...], dn_s[...]))
    ga_s[...] = ga
    dn_s[...] = dn
    dtu = dt * u
    b_all = flats_at(xdbl, i, 0)
    mask = flat_mask(8)
    ones = jnp.where(flat_mask(16), 1.0, 0.0).astype(BF16)
    pu, pd, db, dc = [], [], [], []
    for r in range(CHUNK // 8):
        few = slice(8 * r, 8 * r + 8)
        adjoint = g_s[few].reshape(8 * STATE, LANES)
        slow = f_s[few].reshape(8 * STATE, LANES)
        h = state[8 * r + 1 : 8 * r + 9].reshape(8 * STATE, LANES).astype(BF16)
        made = dot(stacked(jnp.where(mask, b_all[r : r + 1], 0.0)), adjoint, 1, 0)
        pu.append(made[0:8] + made[8:16])
        pd.append(dot(ones, slow, 1, 0)[0:8])
        for out, value, other in ((db, dtu, adjoint), (dc, d_y, h)):
            made = dot(stacked(value[few]), other, 1, 1)
            out.append(jnp.sum(jnp.where(mask, made[0:8] + made[8:16], 0.0), axis=0, keepdims=True))
    d_dtu = jnp.concatenate(pu, axis=0)
    d_dt = jnp.concatenate(pd, axis=0) + d_dtu * u
    few = CHUNK // 8
    for n, part in enumerate((db, dc)):
        first = pl.multiple_of(tokens + n * (tokens // 8) + i * few, few)
        own[pl.ds(first, few)] = jnp.concatenate(part, axis=0)
    du_all[span] = d_y * rows_ref[SKIP : SKIP + 1] + d_dtu * dt
    d_raw = (d_dt * sig_all[span]).astype(BF16)
    image = chunk_image(mod, i)
    low = xdbl[span].astype(BF16)
    own[span] = jnp.where(image, dot(d_raw, wdt[1], 1, 1), dot(d_raw, wdt[0], 1, 1))
    raw_f = d_raw.astype(F32)
    for m in range(2):
        mine = jnp.where(image == (m == 1), raw_f, 0.0)
        dwdt[m] += dot(low, mine.astype(BF16), 0, 0)
        dbias[m : m + 1] += jnp.sum(mine, axis=0, keepdims=True)


def rear_block(bound, i, at, dx, du_all, u_all, conv_all, xpre_all, mod, wx, wbc, rows_ref, dpre_all, grads, scratch):
    dwx, dwbc, dconv = grads
    ext, ahead = scratch
    tokens = u_all.shape[0]
    span = block_at(i, ROWS)
    few = ROWS // 8
    image = column(mod[i, 0:1]) > 0.5
    low = dx[span].astype(BF16)
    mask = flat_mask(ROWS)
    lane = lax.broadcasted_iota(jnp.int32, (LANES, 2 * STATE), 0)
    state = lax.broadcasted_iota(jnp.int32, (LANES, 2 * STATE), 1)
    d_bc = None
    for n in range(2):
        fold = jnp.where(lax.rem(lane, STATE) + n * STATE == state, 1.0, 0.0).astype(BF16)
        flat = dx[pl.ds(pl.multiple_of(tokens + n * (tokens // 8) + i * few, few), few)]
        wide = jnp.broadcast_to(flat[:, None, :], (few, 8, LANES)).reshape(ROWS, LANES)
        part = dot(jnp.where(mask, wide, 0.0).astype(BF16), fold, 1, 0)
        d_bc = part if d_bc is None else d_bc + part
    d_bc = d_bc.astype(BF16)
    u = u_all[span]
    extra = [dot(low, wx[m], 1, 0) + dot(d_bc, wbc[m, :, lanes_at(at.s, LANES)], 1, 0) for m in range(2)]
    d_u = du_all[span] + jnp.where(image, extra[1], extra[0])
    u_f = u.astype(F32)
    for m in range(2):
        mine = jnp.where(image == (m == 1), u_f, 0.0).astype(BF16)
        dwx[m] += dot(low, mine, 0, 0)
        dwbc[m] += dot(d_bc, mine, 0, 0)
    conv = conv_all[span]
    d_conv = d_u * silu_slope(conv, jax.nn.sigmoid(conv))
    before = lax.rem(i * ROWS + tokens - 16, tokens)
    ext[0:8] = xpre_all[pl.ds(pl.multiple_of(before, 16), 16)].astype(F32)[8:16]
    ext[8:] = xpre_all[span].astype(F32)
    ahead[ROWS : ROWS + 8] = ahead[0:8]
    ahead[0:ROWS] = d_conv
    t = token_at(i, ROWS)
    d_pre = None
    for tap in range(CONV):
        lag = CONV - 1 - tap
        seen = ext[8 - lag : 8 - lag + ROWS] * d_conv
        term = rows_ref[CONV_W + tap : CONV_W + tap + 1] * ahead[lag : lag + ROWS]
        if lag:
            seen = jnp.where((t < lag) | ((t >= bound) & (t - lag < bound)), 0.0, seen)
            term = jnp.where((t < bound) & (t + lag >= bound), 0.0, term)
        dconv[tap : tap + 1] += jnp.sum(seen, axis=0, keepdims=True)
        d_pre = term if d_pre is None else d_pre + term
    dconv[CONV : CONV + 1] += jnp.sum(d_conv, axis=0, keepdims=True)
    dpre_all[span] = d_pre.astype(BF16)


def grown(image, width):
    return jnp.concatenate([image] * (width // LANES), axis=1)


def out_block(i, gated, cot_s, mod, wo, branch, dwo):
    span = block_at(i, ROWS)
    wide = jnp.concatenate([gated[n, span] for n in range(gated.shape[0])], axis=1)
    cot = cot_s[span].astype(F32)
    image = grown(column(mod[i, 0:1]) > 0.5, cot.shape[1])
    branch[span] = jnp.where(image, dot(wide, wo[1], 1, 0), dot(wide, wo[0], 1, 0))
    for m in range(2):
        dwo[m] += dot(wide, jnp.where(image == (m == 1), cot, 0.0).astype(BF16), 0, 0)


def in_block(i, k, first, dz_all, normed_s, mod, wi, d_norm, dwi):
    span = block_at(i, ROWS)
    dz = jnp.concatenate([dz_all[n, span] for n in range(dz_all.shape[0])], axis=1)
    normed = normed_s[span].astype(F32)
    image = grown(column(mod[i, 0:1]) > 0.5, normed.shape[1])
    total = jnp.where(image, dot(dz, wi[1, k], 1, 1), dot(dz, wi[0, k], 1, 1))
    d_norm[span] = total if first else d_norm[span] + total
    for m in range(2):
        dwi[m, k] += dot(jnp.where(image == (m == 1), normed, 0.0).astype(BF16), dz, 0, 0)


def backward_kernel(
    seqs, chs, seg_ref, xdbl, u_all, conv_hbm, xpre_hbm, dy_all, dt_all, sig_all, gated_own, dgate_own, hs,
    normed_hbm, cot_hbm, inv_hbm, wx, wdt, mod, dskip, wbc, rows_ref, wi_hbm, wo_hbm, gain_ref, x_ref, own_cot,
    out_ref, grad_ref, sums_ref, dwi, dwo, small_ref, parts_ref, *rest,
):
    totals, branches, norms, shares, trades, rest = split(rest, 10, 9, 9, 20, 3, len(rest) - 51)
    (
        dx, du_all, dpre_own, gated_all, dgate_all, dpre_all, conv_all, xpre_all, normed_s, cot_s, wi, wo, inv,
        branch, d_norm, hbuf, ga_s, dn_s, dta_s, x_s, g_s, f_s, ext, ahead, dwdx, dwbc, dbias, dconv,
        small_own, small_all, dots, r3, pay, r4, hsem, lsem, dsend, drecv, gsend, grecv, psend, precv,
    ) = rest
    at = Place(seqs, chs)
    bound = first_of_second(seg_ref)
    tokens, own, rows = u_all.shape[0], LANES, x_ref.shape[0]
    chunks, blocks = tokens // CHUNK, tokens // ROWS

    def state_copy(i, slot):
        return pltpu.make_async_copy(hs.at[pl.ds(i * CHUNK, CHUNK + 1)], hbuf.at[slot], hsem.at[slot])

    state_copy(chunks - 1, 0).start()
    late = [
        (conv_hbm, conv_all), (xpre_hbm, xpre_all), (normed_hbm, normed_s), (cot_hbm, cot_s), (wi_hbm, wi),
        (wo_hbm, wo), (inv_hbm.at[block_at(at.s, rows)], inv),
    ]
    late = [pltpu.make_async_copy(src, dst, lsem.at[n]) for n, (src, dst) in enumerate(late)]
    for copy in late:
        copy.start()
    total = Total(at, dx, *totals)
    ups, downs = list(range(CUTS)), list(reversed(range(CUTS)))
    gated = Share(at, gated_own, gated_all, CUTS, ups[-1:], *shares[0:5])
    d_gate = Share(at, dgate_own, dgate_all, CUTS, ups[-1:], *shares[5:10])
    d_pre = Share(at, dpre_own, dpre_all, CUTS, downs[-1:], *shares[10:15])
    small = Share(at, small_own, small_all, 1, [], *shares[15:20])

    def wave(share, order, *numbers):
        def go():
            for d in numbers:
                for n in range(at.depth - 1):
                    if 0 <= d - n < len(order):
                        share.serve(order[d - n], n)

        return go

    def post(share, *cuts):
        def go():
            for cut in cuts:
                share.post(cut)

        return go

    at.greet(at.mates + at.others + Regroup.sources(at))
    post(gated, *ups)()
    gated.home.start()
    d_gate.home.start()
    for ref in (ga_s, dn_s, dwdx, dwbc, dbias, dconv, ahead, dwi, dwo):
        ref[...] = jnp.zeros_like(ref)

    def adjoint_step(j):
        i = chunks - 1 - j
        slot = lax.rem(j, 2)
        state_copy(i, slot).wait()

        @pl.when(j < chunks - 1)
        def _():
            state_copy(i - 1, 1 - slot).start()

        adjoint_chunk(
            bound, i, hbuf.at[slot], xdbl, u_all, dy_all, dt_all, sig_all, mod, wdt, rows_ref, total.own, du_all,
            (dwdx.at[1], dbias), (ga_s, dn_s, dta_s, x_s, g_s, f_s),
        )

    events = {2 * d + 3: [wave(gated, ups, d)] for d in range(7)}
    run(chunks, adjoint_step, events)
    total.halve(0)
    wave(gated, ups, 7)()
    total.halve(1)
    wave(gated, ups, 8)()
    total.halve(2)
    wave(gated, ups, 9)()
    total.meet()
    total.part()
    total.parted()
    total.double(2)
    post(d_gate, *ups)()
    total.double(1)
    wave(d_gate, ups, 0)()
    total.double(0)
    wave(d_gate, ups, 1)()
    for copy in late:
        copy.wait()

    def rear_step(j):
        rear_block(
            bound, blocks - 1 - j, at, dx, du_all, u_all, conv_all, xpre_all, mod, wx, wbc, rows_ref, dpre_own,
            (dwdx.at[0], dwbc, dconv), (ext, ahead),
        )
        d_pre.post(blocks - 1 - j)

    run(blocks, rear_step, {2: [wave(d_gate, ups, 2)], 6: [wave(d_gate, ups, 3)]})
    d_pre.home.start()
    small_own[...] = jnp.concatenate(
        [dn_s[...], dconv[...], dbias[...], dskip[...], jnp.zeros((5, own), F32), dwbc[0], dwbc[1]], axis=0
    )
    low = parts_ref.shape[2]
    parts = Trade(
        at, lambda t: dwdx.at[:, :, rows_at(t, low)], parts_ref.at[:, :, :, lanes_at(at.s, own)], *trades
    )
    for cut in range(CUTS):
        gated.arrived(cut)
    gated.home.wait()
    branch_sum = Regroup(at, branch, *branches)
    norm_sum = Regroup(at, d_norm, *norms)

    def out_step(i):
        out_block(i, gated_all, cot_s, mod, wo, branch, dwo)

        @pl.when(lax.rem(i, 2) == 1)
        def _():
            branch_sum.one(i // 2)

    run(blocks, out_step, {n: [wave(d_gate, ups, 4 + n // 2)] for n in (0, 2, 4, 6)})
    quarters = blocks // 2
    wave(d_gate, ups, 8, 9)()
    for q in range(quarters):
        branch_sum.two(q)
    wave(d_pre, downs, 0, 1)()
    small.post(0)
    small.home.start()
    parts.start()
    for q in range(quarters):
        branch_sum.three(q)
    for cut in range(CUTS):
        d_gate.arrived(cut)
    d_gate.home.wait()
    def first_step(i):
        in_block(i, 1, True, dgate_all, normed_s, mod, wi, d_norm, dwi)

    run(blocks, first_step, {2: [wave(d_pre, downs, 2)], 6: [wave(d_pre, downs, 3)]})
    d_pre.home.wait()

    def second_step(j):
        i = blocks - 1 - j
        in_block(i, 0, False, dpre_all, normed_s, mod, wi, d_norm, dwi)
        q = i // 2

        @pl.when(lax.rem(j, 2) == 1)
        def _():
            norm_sum.one(q)

        @pl.when((lax.rem(j, 2) == 0) & (j > 1))
        def _():
            norm_sum.two(q + 1)

        @pl.when((lax.rem(j, 2) == 1) & (j > 2))
        def _():
            norm_sum.three(q + 1)

    events = {j: [wave(d_pre, downs, j + 4), partial(d_pre.arrived, downs[j])] for j in range(blocks)}
    for n in range(3):
        events[2 * n + 1].append(partial(small.serve, 0, n))
    run(blocks, second_step, events)
    added = branch_sum.result()
    xs = x_ref[...].astype(F32)
    mixed = xs + added
    out_ref[...] = mixed.astype(BF16)
    norm_sum.two(0)
    small.arrived(0)
    small.home.wait()
    parts.finish()
    for n in range(seqs):
        small_ref[:, n * own : (n + 1) * own] = small_all[n]
    norm_sum.three(0)
    for share in (gated, d_gate, d_pre, small):
        share.finish()
    inv_own = inv[...][:, 0:1]
    x_hat = xs * inv_own
    width = chs * x_ref.shape[1]
    gain = gain_ref[:, lanes_at(at.c, x_ref.shape[1])]
    total_norm = norm_sum.result()
    d_hat = total_norm * gain
    dot_part = jnp.sum(d_hat * x_hat, axis=1, keepdims=True)
    dots[...] = jnp.transpose(jnp.broadcast_to(dot_part, (rows, LANES)))[0:8]
    third = [remote(dots, r3.at[k], dsend.at[k], drecv.at[k], mate) for k, mate in enumerate(at.mates)]
    for copy in third:
        copy.start()
    rows_of = [total_norm * x_hat, xs * xs, added * added, mixed * mixed]
    pay[...] = jnp.concatenate(
        [jnp.sum(v, axis=0, keepdims=True) for v in rows_of] + [jnp.zeros((4, x_ref.shape[1]), F32)], axis=0
    )
    fourth = [remote(pay, r4.at[k], gsend.at[k], grecv.at[k], other) for k, other in enumerate(at.others)]
    for copy in fourth:
        copy.start()
    dot_sum = dots[...]
    for k, copy in enumerate(third):
        copy.wait_recv()
        dot_sum = dot_sum + r3[k]
    inner = column(dot_sum[0:1])[:, 0:1] / width
    grad_ref[...] = own_cot[...].astype(F32) + inv_own * (d_hat - x_hat * inner)
    joint = pay[...]
    for k, copy in enumerate(fourth):
        copy.wait_recv()
        joint = joint + r4[k]
    sums_ref[at.c] = joint
    spot = sums_ref.at[at.c]
    fifth = [remote(spot, spot, psend.at[k], precv.at[k], mate) for k, mate in enumerate(at.mates)]
    for copy in fifth:
        copy.start()
    for copy in fifth:
        copy.wait_recv()
    for copy in third + fourth + fifth:
        copy.wait_send()
    branch_sum.finish()
    norm_sum.finish()
    total.finish()


def unpack_kernel(
    small_ref, sums_ref, parts_ref, gain, conv_w, conv_b, w_xdt, w_xbc, w_dt, bias, a_log, skip, stats
):
    a_log[...] = small_ref[0:STATE]
    conv_w[...] = small_ref[STATE : STATE + CONV]
    conv_b[...] = small_ref[STATE + CONV : STATE + CONV + 1]
    bias[...] = small_ref[STATE + 8 : STATE + 10]
    skip[...] = small_ref[STATE + 10 : STATE + 11]
    for m in range(2):
        w_xbc[m] = small_ref[32 + 2 * STATE * m : 32 + 2 * STATE * (m + 1)]
    w_xdt[...] = parts_ref[0]
    w_dt[...] = parts_ref[1]
    cols = sums_ref.shape[2]
    total = sums_ref[0]
    for c in range(sums_ref.shape[0]):
        gain[:, c * cols : (c + 1) * cols] = sums_ref[c, 0:1]
        if c:
            total = total + sums_ref[c]
    size = float(gain.shape[1] * sums_ref.shape[0] * cols)
    mean = jnp.sum(total, axis=1, keepdims=True)[1:4] / size
    stats[...] = jnp.sqrt(jnp.transpose(jnp.broadcast_to(mean, (3, LANES)))[0:1, 0:3])

MESH = pl.DeviceIdType.MESH


def remote(src, dst, send, recv, peer):
    return pltpu.make_async_remote_copy(
        src_ref=src, dst_ref=dst, send_sem=send, recv_sem=recv,
        device_id={"seq": peer[0], "ch": peer[1]}, device_id_type=MESH,
    )


def rows_at(start, size):
    return pl.ds(pl.multiple_of(start * size, 8), size)


def lanes_at(start, size):
    return pl.ds(pl.multiple_of(start * size, LANES), size)


class Place:
    def __init__(self, seqs, chs):
        self.seqs, self.chs, self.depth = seqs, chs, seqs // 2
        self.s, self.c = lax.axis_index("seq"), lax.axis_index("ch")
        self.z, self.x = self.s // 2, lax.rem(self.s, 2)
        self.y, self.o = self.c // 2, lax.rem(self.c, 2)
        self.side = (self.s, self.y * 2 + 1 - self.o)
        self.across = (self.s, (1 - self.y) * 2 + self.o)
        self.beside = (self.z * 2 + 1 - self.x, self.c)
        self.deep = [(lax.rem(self.z + k, self.depth) * 2 + self.x, self.c) for k in range(1, self.depth)]
        self.others = [(lax.rem(self.s + k, seqs), self.c) for k in range(1, seqs)]
        self.mates = [(self.s, lax.rem(self.c + k, chs)) for k in range(1, chs)]

    def greet(self, peers):
        barrier = pltpu.get_barrier_semaphore()
        for seq, ch in peers:
            pl.semaphore_signal(barrier, inc=1, device_id={"seq": seq, "ch": ch}, device_id_type=MESH)
        pl.semaphore_wait(barrier, len(peers))


class Spread:
    ORDERS = ((0, 1, 2, 3), (0, 2, 1, 3))
    ORIGIN = (0, 0, 0, 0)

    @staticmethod
    def semaphores(seqs):
        dma = pltpu.SemaphoreType.DMA
        return [dma((2, 4 * seqs)), dma((2, 4 * seqs)), dma((1,))]

    def __init__(self, at, src, out, send, recv, local):
        self.at, self.src, self.out, self.send, self.recv = at, src, out, send, recv
        self.half = src.shape[0] // 2
        self.home = pltpu.make_async_copy(src, out.at[at.s * at.chs + at.c], local.at[0])

    def index(self, role):
        return ((role[0] * 2 + role[1]) * 2 + role[2]) * 2 + role[3]

    def piece(self, cut, role):
        at = self.at
        dz, dx, dy, do = role
        src = lax.rem(at.z + at.depth - dz, at.depth) * 2 + (1 - at.x if dx else at.x)
        col = (1 - at.y if dy else at.y) * 2 + (1 - at.o if do else at.o)
        return self.out.at[src * at.chs + col, pl.ds(cut * self.half, self.half)]

    def hop(self, cut, role, axis, step=1):
        at = self.at
        peer = (at.deep[step - 1], at.beside, at.across, at.side)[axis]
        src = self.piece(cut, role)
        if role == self.ORIGIN:
            src = self.src.at[pl.ds(cut * self.half, self.half)]
        index = self.index(tuple(step if i == axis else v for i, v in enumerate(role)))
        return remote(src, self.piece(cut, role), self.send.at[cut, index], self.recv.at[cut, index], peer)

    def roles(self, cut, level):
        order = self.ORDERS[cut]
        for step in range(self.at.depth):
            for extra in range(max(level, 1)):
                role = [step, 0, 0, 0]
                if level:
                    role[order[level]] = 1
                if extra:
                    role[order[1]] = 1
                if tuple(role) != self.ORIGIN:
                    yield tuple(role)

    def arrived(self, cut, role):
        spot, index = self.piece(cut, role), self.index(role)
        remote(spot, spot, self.send.at[cut, index], self.recv.at[cut, index], self.at.side).wait_recv()

    def post(self):
        for cut in range(2):
            for step in range(1, self.at.depth):
                self.hop(cut, self.ORIGIN, 0, step).start()

    def post_near(self):
        for cut in range(2):
            for axis in self.ORDERS[cut][1:]:
                self.hop(cut, self.ORIGIN, axis).start()
        self.home.start()

    def relay(self, level):
        for cut in range(2):
            for role in self.roles(cut, level):
                self.arrived(cut, role)
                for axis in self.ORDERS[cut][level + 1 :]:
                    self.hop(cut, role, axis).start()

    def finish(self):
        for cut in range(2):
            for step in range(self.at.depth):
                for dx in range(2):
                    for dy in range(2):
                        self.arrived(cut, (step, dx, dy, 1))
        self.home.wait()
        for cut in range(2):
            order = self.ORDERS[cut]
            for step in range(1, self.at.depth):
                self.hop(cut, self.ORIGIN, 0, step).wait_send()
            for axis in order[1:]:
                self.hop(cut, self.ORIGIN, axis).wait_send()
            for level in range(3):
                for role in self.roles(cut, level):
                    for axis in order[level + 1 :]:
                        self.hop(cut, role, axis).wait_send()


class Trade:
    @staticmethod
    def semaphores(seqs):
        dma = pltpu.SemaphoreType.DMA
        return [dma((seqs - 1,)), dma((seqs - 1,)), dma((1,))]

    def __init__(self, at, src_for, dst, send, recv, local):
        self.copies = [
            remote(src_for(peer[0]), dst, send.at[k], recv.at[k], peer) for k, peer in enumerate(at.others)
        ]
        self.home = pltpu.make_async_copy(src_for(at.s), dst, local.at[0])

    def start(self):
        for copy in self.copies:
            copy.start()
        self.home.start()

    def finish(self):
        for copy in self.copies:
            copy.wait_recv()
        self.home.wait()
        for copy in self.copies:
            copy.wait_send()


class Share:
    @staticmethod
    def semaphores(seqs, cuts):
        dma, depth = pltpu.SemaphoreType.DMA, seqs // 2
        return [dma((cuts, 4, depth)), dma((cuts, 2, depth)), dma((cuts, depth)), dma((cuts, depth)), dma((1,))]

    def __init__(self, at, src, out, cuts, turned, send, recv, hop_s, hop_r, local):
        self.at, self.src, self.out, self.cuts, self.turned = at, src, out, cuts, turned
        self.size = src.shape[0] // cuts
        self.z = (send, recv)
        self.x = (hop_s, hop_r)
        self.home = pltpu.make_async_copy(src, out.at[at.s], local.at[0])
        first, last = (at.depth - 1 - at.z) // (at.depth - 1), at.z // (at.depth - 1)
        self.order = (1 + 2 * first, 3 - first - last, 2 - first + last)

    def piece(self, cut, side, r):
        at = self.at
        owner = lax.rem(at.z + at.depth - r, at.depth) * 2 + (1 - at.x if side else at.x)
        return self.out.at[owner, pl.ds(cut * self.size, self.size)]

    def origin(self, cut):
        return self.src.at[pl.ds(cut * self.size, self.size)]

    def along(self, cut, side, r, way):
        at = self.at
        own = isinstance(r, int) and r == 0
        if way == 0:
            there = at.z < at.depth - 1 if own else (at.z >= r) & (at.z < at.depth - 1)
            role, peer = r + 1, at.z + 1
        else:
            there = at.z > 0 if own else (at.z < r) & (at.z > 0)
            role, peer = (at.depth - 1 if own else r - 1), at.z - 1
        spot = self.piece(cut, side, r)
        src = self.origin(cut) if own and not side else spot
        copy = remote(
            src, spot, self.z[0].at[cut, 2 * side + way, r], self.z[1].at[cut, side, role], (peer * 2 + at.x, at.c)
        )
        return there, copy

    def pass_on(self, cut, side, r):
        for way in range(2):
            there, copy = self.along(cut, side, r, way)
            pl.when(there)(copy.start)

    def beside(self, cut, r):
        spot = self.piece(cut, 0, r)
        src = self.origin(cut) if isinstance(r, int) and r == 0 else spot
        return remote(src, spot, self.x[0].at[cut, r], self.x[1].at[cut, r], self.at.beside)

    def is_turned(self, cut):
        return cut in self.turned

    def post(self, cut):
        self.pass_on(cut, 0, 0)
        self.beside(cut, 0).start()

    def wait_z(self, cut, side, r):
        spot = self.piece(cut, side, r)
        remote(spot, spot, self.z[0].at[cut, 0, 0], self.z[1].at[cut, side, r], self.at.beside).wait_recv()

    def wait_x(self, cut, r):
        spot = self.piece(cut, 1, r)
        remote(spot, spot, self.x[0].at[cut, r], self.x[1].at[cut, r], self.at.beside).wait_recv()

    def serve(self, cut, n):
        r = self.order[n]
        if not self.is_turned(cut):
            self.wait_z(cut, 0, r)
            self.pass_on(cut, 0, r)
            self.beside(cut, r).start()
            return
        if n == 0:
            self.wait_x(cut, 0)
            self.pass_on(cut, 1, 0)
        for side in range(2):
            self.wait_z(cut, side, r)
            self.pass_on(cut, side, r)

    def arrived(self, cut):
        if not self.is_turned(cut):
            for r in range(self.at.depth):
                self.wait_x(cut, r)

    def finish(self):
        for cut in range(self.cuts):
            turned = self.is_turned(cut)
            for side in range(2 if turned else 1):
                for r in range(self.at.depth):
                    for way in range(2):
                        there, copy = self.along(cut, side, r, way)
                        pl.when(there)(copy.wait_send)
            for r in range(1 if turned else self.at.depth):
                self.beside(cut, r).wait_send()


class Total:
    @staticmethod
    def scratch(seqs, rows):
        depth = seqs // 2
        n = 2 * (depth + 2)
        dma = pltpu.SemaphoreType.DMA

        def vmem(*shape):
            return pltpu.VMEM(shape + (LANES,), F32)

        return [
            vmem(rows), vmem(rows // 2), vmem(rows // 4), vmem(rows // 8), vmem(depth - 1, rows // 8 // depth),
            vmem(rows // 2), vmem(rows // 4), vmem(rows // 8), dma((n,)), dma((n,)),
        ]

    def __init__(self, at, out, own, r0, r1, r2, r3, a1, a2, a3, send, recv):
        self.at, self.out, self.own = at, out, own
        self.got, self.held = (r0, r1, r2), (own, a1, a2, a3)
        self.last, self.send, self.recv = r3, send, recv
        self.block = (at.o * 2 + at.y) * 2 + at.x
        self.sends = []

    def halve(self, n):
        at = self.at
        bit, peer = ((at.o, at.side), (at.y, at.across), (at.x, at.beside))[n]
        size = self.own.shape[0] >> (n + 1)
        src, dst = self.held[n], self.held[n + 1]
        copy = remote(src.at[rows_at(1 - bit, size)], self.got[n], self.send.at[n], self.recv.at[n], peer)
        copy.start()
        copy.wait_recv()
        dst[...] = src[rows_at(bit, size)] + self.got[n][...]
        self.sends.append(copy)

    def meet(self):
        at = self.at
        size = self.own.shape[0] // 8 // at.depth
        last = self.held[3]
        copies = []
        for k, peer in enumerate(at.deep):
            there = lax.rem(at.z + 1 + k, at.depth)
            copies.append(
                remote(last.at[rows_at(there, size)], self.last.at[k], self.send.at[3 + k], self.recv.at[3 + k], peer)
            )
            copies[-1].start()
        total = last[rows_at(at.z, size)]
        for k, copy in enumerate(copies):
            copy.wait_recv()
            total = total + self.last[k]
        self.sends += copies
        self.out[rows_at(self.block * at.depth + at.z, size)] = total

    def part(self):
        at = self.at
        size = self.own.shape[0] // 8 // at.depth
        base = at.depth + 2
        spot = self.out.at[rows_at(self.block * at.depth + at.z, size)]
        copies = []
        for k, peer in enumerate(at.deep):
            copies.append(remote(spot, spot, self.send.at[base + k], self.recv.at[base + k], peer))
            copies[-1].start()
        self.parting = copies

    def parted(self):
        for copy in self.parting:
            copy.wait_recv()
        self.sends += self.parting

    def double(self, n):
        at = self.at
        size = self.own.shape[0] >> (n + 1)
        index, peer = ((at.o, at.side), (at.o * 2 + at.y, at.across), (self.block, at.beside))[n]
        spot = self.out.at[rows_at(index, size)]
        base = 2 * at.depth + 1 + n
        copy = remote(spot, spot, self.send.at[base], self.recv.at[base], peer)
        copy.start()
        copy.wait_recv()
        self.sends.append(copy)

    def finish(self):
        for copy in self.sends:
            copy.wait_send()


class Regroup:
    @staticmethod
    def scratch(seqs, chs, tokens, part):
        folds, vmem, dma = seqs // chs, pltpu.VMEM, pltpu.SemaphoreType.DMA
        n, rows = seqs // 2, tokens // seqs
        half = rows // 2
        return [
            vmem((n, rows, part), F32), vmem((n, rows, part), F32), vmem((n, half, part), BF16),
            vmem((n, half, part), BF16), vmem((n, half, part), BF16), vmem((folds, 2, half, part), BF16),
            dma((n, 3)), dma((n, 2)), dma((folds, 2)),
        ]

    @staticmethod
    def sources(at):
        folds = at.seqs // at.chs
        return [(at.c * folds + f, y * 2 + lax.rem(at.s, 2)) for f in range(folds) for y in range(2)]

    def __init__(self, at, src, r0, a1, sb, r1, fb, r2, send, recv, last):
        self.at, self.src = at, src
        self.r0, self.a1, self.sb, self.r1, self.fb, self.r2 = r0, a1, sb, r1, fb, r2
        self.send, self.recv, self.last = send, recv, last
        self.quarters, self.rows, self.half = r0.shape[0], r0.shape[1], r1.shape[1]
        self.folds = at.seqs // at.chs
        self.home, self.slot = at.s // self.folds, lax.rem(at.s, self.folds)

    def first(self, q):
        at = self.at
        src = self.src.at[rows_at(2 * q + 1 - at.o, self.rows)]
        return remote(src, self.r0.at[q], self.send.at[q, 0], self.recv.at[q, 0], at.side)

    def second(self, q):
        return remote(self.sb.at[q], self.r1.at[q], self.send.at[q, 1], self.recv.at[q, 1], self.at.across)

    def third(self, q):
        at = self.at
        dst, sem = self.r2.at[self.slot, at.y], self.last.at[self.slot, at.y]
        away = jnp.logical_or(2 * q + at.o != at.s, self.home != at.c)
        there = remote(self.fb.at[q], dst, self.send.at[q, 2], sem, (2 * q + at.o, self.home))
        return away, there, pltpu.make_async_copy(self.fb.at[q], dst, sem)

    def one(self, q):
        self.first(q).start()

    def two(self, q):
        at = self.at
        self.first(q).wait_recv()
        self.a1[q] = self.src[rows_at(2 * q + at.o, self.rows)] + self.r0[q]
        self.sb[q] = self.a1[q, rows_at(1 - at.y, self.half)].astype(BF16)
        self.second(q).start()

    def three(self, q):
        at = self.at
        self.second(q).wait_recv()
        self.fb[q] = (self.a1[q, rows_at(at.y, self.half)] + self.r1[q].astype(F32)).astype(BF16)
        away, there, here = self.third(q)
        pl.when(away)(there.start)
        pl.when(jnp.logical_not(away))(here.start)

    def result(self):
        for f in range(self.folds):
            for y in range(2):
                spot = self.r2.at[f, y]
                remote(self.fb.at[0], spot, self.send.at[0, 2], self.last.at[f, y], self.at.side).wait_recv()
        rows = [jnp.concatenate([self.r2[f, 0], self.r2[f, 1]], axis=0) for f in range(self.folds)]
        return jnp.concatenate(rows, axis=1).astype(F32)

    def finish(self):
        for q in range(self.quarters):
            self.first(q).wait_send()
            self.second(q).wait_send()
            away, there, _ = self.third(q)
            pl.when(away)(there.wait_send)


def run(count, body, events):
    def step(j, carry):
        for when, things in events.items():

            @pl.when(j == when)
            def _():
                for thing in things:
                    thing()

        body(j)
        return carry

    lax.fori_loop(0, count, step, 0)


def split(refs, *counts):
    out, start = [], 0
    for count in counts:
        out.append(refs[start : start + count])
        start += count
    return out

ANY = pl.BlockSpec(memory_space=pl.ANY)
WHOLE = pl.BlockSpec(memory_space=pltpu.VMEM)


def comm(kernel, ins, outs, scratch, ident, name, moved):
    return pl.pallas_call(
        kernel,
        out_shape=[jax.ShapeDtypeStruct(shape, dtype) for shape, dtype, _ in outs],
        in_specs=[spec for _, spec in ins],
        out_specs=[spec for _, _, spec in outs],
        scratch_shapes=scratch,
        compiler_params=pltpu.CompilerParams(
            collective_id=ident, has_side_effects=True, vmem_limit_bytes=60 * 2**20
        ),
        cost_estimate=pl.CostEstimate(flops=0, bytes_accessed=moved, transcendentals=0),
        name=name,
    )(*[array for array, _ in ins])


def per_device(
    stream, norm_gain, w_in, conv_w, conv_b, w_xdt, w_xbc, w_dt, dt_bias, a_log, d_skip, w_out,
    cotangent, seg_ids, modality,
):
    seqs, chs = lax.axis_size("seq"), lax.axis_size("ch")
    s = lax.axis_index("seq")
    rows, cols = stream.shape
    tokens, width = seg_ids.shape[0], norm_gain.shape[0]
    channels = conv_b.shape[0]
    own = channels // seqs
    part = width // seqs
    flat = tokens * STATE // LANES
    dma, vmem = pltpu.SemaphoreType.DMA, pltpu.VMEM
    segs = seg_ids.reshape(tokens // LANES, LANES)
    gain = norm_gain[None]
    xdbl, u, conv, x_pre, d_y, dt, sig, gated, d_gate, hs, normed, cot, inv, wx, wdt, mod, d_skip_own, own_rows = comm(
        partial(forward_kernel, seqs, chs),
        [
            (stream, ANY), (cotangent, ANY), (w_in, ANY), (w_out, ANY), (w_xdt, ANY), (w_dt, ANY),
            (modality[None], WHOLE), (segs, WHOLE), (gain, WHOLE), (w_xbc, WHOLE), (a_log, WHOLE),
            (d_skip[None], WHOLE), (conv_b[None], WHOLE), (conv_w, WHOLE), (dt_bias, WHOLE),
        ],
        [
            ((tokens + 2 * flat, LANES), F32, WHOLE),
            ((tokens, own), BF16, WHOLE),
            ((tokens, own), F32, WHOLE),
            ((tokens, own), BF16, WHOLE),
            ((tokens, own), F32, WHOLE),
            ((tokens, own), F32, WHOLE),
            ((tokens, own), F32, WHOLE),
            ((tokens, own), BF16, WHOLE),
            ((tokens, own), BF16, WHOLE),
            ((tokens + 1, STATE, own), F32, ANY),
            ((tokens, part), BF16, WHOLE),
            ((tokens, part), BF16, ANY),
            ((tokens, LANES), F32, WHOLE),
            ((2, RANK, own), BF16, WHOLE),
            ((2, RANK, own), BF16, WHOLE),
            ((seqs, 8, rows), F32, WHOLE),
            ((1, own), F32, WHOLE),
            ((STATE + 8, own), F32, WHOLE),
        ],
        Total.scratch(seqs, tokens + 2 * flat) + 2 * Spread.semaphores(seqs) + 5 * Trade.semaphores(seqs)
        + [
            vmem((seqs * chs, rows, cols), BF16), vmem((seqs * chs, rows, cols), BF16),
            vmem((2, 2, width, own), BF16), vmem((2, own, width), BF16),
            vmem((tokens, own), F32), vmem((tokens, own), F32), vmem((ROWS + 8, own), F32), vmem((ROWS, width), BF16),
            vmem((STATE, own), F32), vmem((CHUNK, own), F32), vmem((CHUNK, STATE, own), F32),
            vmem((2, CHUNK, STATE, own), F32), vmem((8, rows), F32), dma((3 + seqs,)),
        ],
        1, "forward", 64 << 20,
    )
    output, grad_stream, sums, own_w_in, own_w_out, small, parts = comm(
        partial(backward_kernel, seqs, chs),
        [
            (segs, WHOLE), (xdbl, WHOLE), (u, WHOLE), (conv, ANY), (x_pre, ANY), (d_y, WHOLE), (dt, WHOLE),
            (sig, WHOLE), (gated, WHOLE), (d_gate, WHOLE), (hs, ANY), (normed, ANY), (cot, ANY), (inv, ANY),
            (wx, WHOLE), (wdt, WHOLE), (mod, WHOLE), (d_skip_own, WHOLE), (w_xbc, WHOLE), (own_rows, WHOLE),
            (w_in, ANY), (w_out, ANY), (gain, WHOLE), (stream, WHOLE), (cotangent, WHOLE),
        ],
        [
            ((rows, cols), BF16, WHOLE),
            ((rows, cols), F32, WHOLE),
            ((chs, 8, cols), F32, WHOLE),
            (w_in.shape, F32, WHOLE),
            (w_out.shape, F32, WHOLE),
            ((96, channels), F32, WHOLE),
            ((2, 2, RANK // seqs, channels), F32, ANY),
        ],
        Total.scratch(seqs, tokens + 2 * flat) + 2 * Regroup.scratch(seqs, chs, tokens, part)
        + 3 * Share.semaphores(seqs, CUTS) + Share.semaphores(seqs, 1) + Trade.semaphores(seqs)
        + [
            vmem((tokens + 2 * flat, LANES), F32), vmem((tokens, own), F32), vmem((tokens, own), BF16),
            vmem((seqs, tokens, own), BF16), vmem((seqs, tokens, own), BF16), vmem((seqs, tokens, own), BF16),
            vmem((tokens, own), F32), vmem((tokens, own), BF16), vmem((tokens, part), BF16), vmem((tokens, part), BF16),
            vmem(w_in.shape, BF16), vmem(w_out.shape, BF16), vmem((rows, LANES), F32),
            vmem((tokens, part), F32), vmem((tokens, part), F32), vmem((2, CHUNK + 1, STATE, own), F32),
            vmem((STATE, own), F32), vmem((STATE, own), F32), vmem((CHUNK, own), F32), vmem((CHUNK, STATE, own), F32),
            vmem((CHUNK, STATE, own), BF16), vmem((CHUNK, STATE, own), BF16),
            vmem((ROWS + 8, own), F32), vmem((ROWS + 8, own), F32), vmem((2, 2, RANK, own), F32),
            vmem((2, 2 * STATE, own), F32), vmem((2, own), F32), vmem((8, own), F32),
            vmem((96, own), F32), vmem((seqs, 96, own), F32), vmem((8, rows), F32), vmem((chs - 1, 8, rows), F32),
            vmem((8, cols), F32), vmem((seqs - 1, 8, cols), F32),
            dma((2,)), dma((7,)), dma((chs - 1,)), dma((chs - 1,)), dma((seqs - 1,)), dma((seqs - 1,)),
            dma((chs - 1,)), dma((chs - 1,)),
        ],
        2, "backward", 64 << 20,
    )
    shapes = [
        (1, width), conv_w.shape, (1, channels), parts.shape[1:], w_xbc.shape, parts.shape[1:], dt_bias.shape,
        a_log.shape, (1, channels), (1, 3),
    ]
    g_gain, g_conv_w, g_conv_b, g_w_xdt, g_w_xbc, g_w_dt, g_bias, g_a_log, g_skip, stats = pl.pallas_call(
        unpack_kernel, out_shape=[jax.ShapeDtypeStruct(shape, F32) for shape in shapes], name="unpack"
    )(small, sums, parts)
    return (
        output, grad_stream, g_gain[0], own_w_in, g_conv_w, g_conv_b[0], g_w_xdt, g_w_xbc, g_w_dt, g_bias,
        g_a_log, g_skip[0], own_w_out, stats[0],
    )


def per_device_by_token(
    stream,
    norm_gain,
    w_in,
    conv_w,
    conv_b,
    w_xdt,
    w_xbc,
    w_dt,
    dt_bias,
    a_log,
    d_skip,
    w_out,
    cotangent,
    seg_ids,
    modality,
):
    length = stream.shape[0]
    channels = conv_b.shape[0]
    model_width = norm_gain.shape[0]
    mod_count = w_in.shape[0]
    rim_len = CONV - 1
    ch_start = lax.axis_index("ch") * channels
    col_start = lax.axis_index("ch") * stream.shape[1]
    x_full, grad_full = (
        lax.all_gather(stream, "ch", axis=1, tiled=True),
        lax.all_gather(cotangent, "ch", axis=1, tiled=True),
    )
    w_in_full, w_xdt_full, w_dt_full, w_out_full = (
        lax.all_gather(w_in, "seq", axis=2, tiled=True),
        lax.all_gather(w_xdt, "seq", axis=1, tiled=True),
        lax.all_gather(w_dt, "seq", axis=1, tiled=True),
        lax.all_gather(w_out, "seq", axis=2, tiled=True),
    )
    mod_mask = modality[None, :] == jnp.arange(mod_count, dtype=jnp.int32)[:, None]
    mod_float = mod_mask.astype(jnp.float32)

    def by_mod(value):
        chosen = mod_mask.reshape(mod_mask.shape + (1,) * (value.ndim - 1))
        return jnp.where(chosen, value[None], jnp.zeros((), value.dtype))

    stream_f = x_full.astype(jnp.float32)
    inv_rms = lax.rsqrt(jnp.mean(stream_f * stream_f, axis=1, keepdims=True) + EPSILON)
    x_hat = stream_f * inv_rms
    normed = (x_hat * norm_gain[None, :]).astype(jnp.bfloat16)
    normed_split = by_mod(normed)
    projected = jnp.einsum(
        "mtd,mkde->tke", normed_split, w_in_full, preferred_element_type=jnp.float32
    )
    x_pre = projected[:, 0].astype(jnp.bfloat16)
    gate_in = projected[:, 1]
    rim_rows = passed_along(x_pre[length - rim_len :], "seq", 1)
    padded_seg = jnp.concatenate([jnp.full((rim_len,), -1, jnp.int32), seg_ids])
    seg_win = lax.dynamic_slice_in_dim(padded_seg, lax.axis_index("seq") * length, length + rim_len)
    seg_now = seg_win[rim_len:]
    extended = jnp.concatenate([rim_rows, x_pre], 0).astype(jnp.float32)
    tap_mask = [
        (seg_win[offset : offset + length] == seg_now).astype(jnp.float32)[:, None]
        for offset in range(CONV)
    ]
    conv_out = conv_b[None, :] + sum(
        (
            conv_w[offset][None, :] * extended[offset : offset + length] * tap_mask[offset]
            for offset in range(CONV)
        )
    )
    u_val = (conv_out * jax.nn.sigmoid(conv_out)).astype(jnp.bfloat16)
    u_split = by_mod(u_val)
    dt_part = jnp.einsum("mte,mre->tr", u_split, w_xdt_full, preferred_element_type=jnp.float32)
    bc_part = jnp.einsum("mte,mne->tn", u_split, w_xbc, preferred_element_type=jnp.float32)
    dt_sum, bc_sum = lax.psum((dt_part, bc_part), "ch")
    dt_low = dt_sum.astype(jnp.bfloat16)
    b_in = bc_sum[:, :STATE]
    c_out = bc_sum[:, STATE:]
    low_split = by_mod(dt_low)
    dt_raw = jnp.einsum(
        "mtr,mre->te", low_split, w_dt_full, preferred_element_type=jnp.float32
    ) + jnp.dot(mod_float.T, dt_bias, precision=PRECISE)
    dt_val = jax.nn.softplus(dt_raw)
    u_float = u_val.astype(jnp.float32)
    dt_u = dt_val * u_float
    neg_a = -jnp.exp(a_log)
    keep_mask = (seg_now == seg_win[rim_len - 1 : rim_len - 1 + length]).astype(jnp.float32)
    decay_all = jnp.exp(neg_a * jnp.sum(dt_val, axis=0)[None, :]) * jnp.prod(keep_mask)
    zero_state = jnp.zeros_like(neg_a)
    local_end, _, _ = run_forward(zero_state, dt_val, dt_u, b_in, c_out, keep_mask, neg_a)
    _, start_state = entering(
        (decay_all, local_end), "seq", chain_link, (jnp.ones_like(neg_a), zero_state), False
    )
    _, starts, y_ssm = run_forward(start_state, dt_val, dt_u, b_in, c_out, keep_mask, neg_a)
    y_val = y_ssm + d_skip[None, :] * u_float
    sig_gate = jax.nn.sigmoid(gate_in)
    gated = (y_val * (gate_in * sig_gate)).astype(jnp.bfloat16)
    gated_split = by_mod(gated)
    branch = lax.psum_scatter(
        jnp.einsum("mte,med->dt", gated_split, w_out_full, preferred_element_type=jnp.float32),
        "ch",
        scatter_dimension=0,
        tiled=True,
    ).T
    x_own = stream.astype(jnp.float32)
    mixed = x_own + branch
    output = mixed.astype(jnp.bfloat16)
    stats_part = jnp.stack(
        [jnp.sum(x_own * x_own), jnp.sum(branch * branch), jnp.sum(mixed * mixed)]
    )
    grad_split = by_mod(grad_full)
    d_gated = jnp.einsum("mtd,med->te", grad_split, w_out_full, preferred_element_type=jnp.float32)
    d_w_out = jnp.einsum("mte,td->med", gated_split, grad_full, preferred_element_type=jnp.float32)
    d_y = d_gated * gate_in * sig_gate
    d_gate = d_gated * y_val * silu_grad(gate_in)
    d_skip_part = jnp.sum(d_y * u_float, axis=0)
    local_back = local_adjoint(dt_val, c_out, keep_mask, d_y, neg_a)
    _, incoming = entering(
        (decay_all, local_back), "seq", chain_link, (jnp.ones_like(neg_a), zero_state), True
    )
    d_neg, d_dt_ssm, d_dtu, d_b, d_c = run_adjoint(
        incoming, starts, dt_val, dt_u, b_in, c_out, keep_mask, d_y, neg_a
    )
    d_a_log = d_neg * neg_a
    d_dt = d_dt_ssm + d_dtu * u_float
    d_u = d_y * d_skip[None, :] + d_dtu * dt_val
    d_raw = (d_dt * jax.nn.sigmoid(dt_raw)).astype(jnp.bfloat16)
    d_w_dt = jnp.einsum("mtr,te->mre", low_split, d_raw, preferred_element_type=jnp.float32)
    d_dt_bias = jnp.dot(mod_float, d_raw.astype(jnp.float32), precision=PRECISE)
    d_low_part = jnp.einsum(
        "mte,mre->tr", by_mod(d_raw), w_dt_full, preferred_element_type=jnp.float32
    )
    d_bc_part = jnp.concatenate([d_b, d_c], 1)
    d_low_sum, d_bc_sum = lax.psum((d_low_part, d_bc_part), "ch")
    d_low = d_low_sum.astype(jnp.bfloat16)
    d_bc = d_bc_sum.astype(jnp.bfloat16)
    d_w_xdt = jnp.einsum("mte,tr->mre", u_split, d_low, preferred_element_type=jnp.float32)
    d_w_xbc = jnp.einsum("mte,tn->mne", u_split, d_bc, preferred_element_type=jnp.float32)
    d_u = d_u + jnp.einsum(
        "mtr,mre->te", by_mod(d_low), w_xdt_full, preferred_element_type=jnp.float32
    )
    d_u = d_u + jnp.einsum("mtn,mne->te", by_mod(d_bc), w_xbc, preferred_element_type=jnp.float32)
    d_conv = d_u * silu_grad(conv_out)
    d_conv_b = jnp.sum(d_conv, axis=0)
    d_conv_w = jnp.stack(
        [
            jnp.sum(d_conv * extended[offset : offset + length] * tap_mask[offset], axis=0)
            for offset in range(CONV)
        ]
    )
    d_ext = sum(
        (
            jnp.pad(
                conv_w[offset][None, :] * d_conv * tap_mask[offset],
                ((offset, rim_len - offset), (0, 0)),
            )
            for offset in range(CONV)
        )
    )
    back_rim = passed_along(d_ext[:rim_len], "seq", -1)
    d_pre = d_ext[rim_len:] + jnp.pad(back_rim, ((length - rim_len, 0), (0, 0)))
    d_xz = jnp.stack([d_pre, d_gate], 1).astype(jnp.bfloat16)
    d_w_in = jnp.einsum("mtd,tke->mkde", normed_split, d_xz, preferred_element_type=jnp.float32)
    d_norm_part = jnp.einsum(
        "mtke,mkde->dt", by_mod(d_xz), w_in_full, preferred_element_type=jnp.float32
    )
    d_gain_part = jnp.einsum("dt,td->d", d_norm_part, x_hat, precision=PRECISE)
    d_norm = lax.psum(d_norm_part, "ch").T
    d_hat = d_norm * norm_gain[None, :]
    inner_dot = jnp.mean(d_hat * x_hat, axis=1, keepdims=True)
    d_x_full = inv_rms * (d_hat - x_hat * inner_dot)
    grad_stream = lax.dynamic_slice_in_dim(
        d_x_full, col_start, stream.shape[1], 1
    ) + cotangent.astype(jnp.float32)
    own_w_in, own_w_xdt, own_w_dt, own_w_out = (
        lax.psum_scatter(d_w_in, "seq", scatter_dimension=2, tiled=True),
        lax.psum_scatter(d_w_xdt, "seq", scatter_dimension=1, tiled=True),
        lax.psum_scatter(d_w_dt, "seq", scatter_dimension=1, tiled=True),
        lax.psum_scatter(d_w_out, "seq", scatter_dimension=2, tiled=True),
    )

    def spread(value):
        full_shape = value.shape[:-1] + (INNER,)
        return lax.dynamic_update_slice_in_dim(
            jnp.zeros(full_shape, jnp.float32), value, ch_start, value.ndim - 1
        )

    def own_slice(value):
        return lax.dynamic_slice_in_dim(value, ch_start, channels, value.ndim - 1)

    summed = lax.psum(
        (
            spread(d_conv_w),
            spread(d_conv_b),
            spread(d_w_xbc),
            spread(d_dt_bias),
            spread(d_a_log),
            spread(d_skip_part),
            d_gain_part,
            stats_part,
        ),
        ("seq", "ch"),
    )
    stats = jnp.sqrt(summed[7] / float(length * lax.axis_size("seq") * model_width))
    return (
        output,
        grad_stream,
        summed[6],
        own_w_in,
        own_slice(summed[0]),
        own_slice(summed[1]),
        own_w_xdt,
        own_slice(summed[2]),
        own_w_dt,
        own_slice(summed[3]),
        own_slice(summed[4]),
        own_slice(summed[5]),
        own_w_out,
        stats,
    )


def solution(mesh):
    in_specs = (
        P("seq", "ch"),
        P(),
        P(None, None, "seq", "ch"),
        P(None, "ch"),
        P("ch"),
        P(None, "seq", "ch"),
        P(None, None, "ch"),
        P(None, "seq", "ch"),
        P(None, "ch"),
        P(None, "ch"),
        P("ch"),
        P(None, "ch", "seq"),
        P("seq", "ch"),
        P(),
        P("seq"),
    )
    out_specs = (
        P("seq", "ch"),
        P("seq", "ch"),
        P(),
        P(None, None, "seq", "ch"),
        P(None, "ch"),
        P("ch"),
        P(None, "seq", "ch"),
        P(None, None, "ch"),
        P(None, "seq", "ch"),
        P(None, "ch"),
        P(None, "ch"),
        P("ch"),
        P(None, "ch", "seq"),
        P(),
    )
    seqs, chs = mesh.shape["seq"], mesh.shape["ch"]
    whole_lanes = INNER == seqs * chs * LANES and seqs == 2 * chs and chs == 4
    return jax.shard_map(
        per_device if whole_lanes else per_device_by_token, mesh=mesh, in_specs=in_specs, out_specs=out_specs, check_vma=False
    )
```

```python
from functools import partial

import jax
import jax.numpy as jnp
from jax import lax
from jax.experimental import pallas as pl
from jax.experimental.pallas import tpu as pltpu
from jax.sharding import PartitionSpec as P

INNER = 4096
STATE = 16
CONV = 4
BLK = 64
RANK = 128


EPSILON = 1e-05
PRECISE = lax.Precision.HIGHEST


def passed_along(value, axis, steps):
    count = lax.axis_size(axis)
    initial, last = (max(0, -steps), min(count, count - steps))
    return lax.ppermute(value, axis, [(source, source + steps) for source in range(initial, last)])


def entering(part, axis, combine, identity, reverse):
    count = lax.axis_size(axis)
    place = lax.axis_index(axis)
    ahead = count - 1 - place if reverse else place
    gathered = jax.tree.map(lambda a: lax.all_gather(a, axis), part)
    state = jax.tree.map(lambda a, e: jnp.zeros_like(a) + jnp.asarray(e, a.dtype), part, identity)

    def one(step, state):
        source = count - 1 - step if reverse else step
        return combine(
            state, jax.tree.map(lambda a: lax.dynamic_index_in_dim(a, source, 0, False), gathered)
        )

    return lax.fori_loop(0, ahead, one, state)


def silu_grad(value):
    sigma = jax.nn.sigmoid(value)
    return sigma * (1.0 + value * (1.0 - sigma))


def chain_link(earlier, latter):
    return (earlier[0] * latter[0], latter[0] * earlier[1] + latter[1])


def decay_terms(dt_blk, keep_blk, neg_a):
    return keep_blk[:, None, None] * jnp.exp(dt_blk[:, None, :] * neg_a[None])


def drive_terms(b_blk, dtu_blk):
    return b_blk[:, :, None] * dtu_blk[:, None, :]


def to_blocks(values):
    block_count = values[0].shape[0] // BLK
    return tuple((value.reshape((block_count, BLK) + value.shape[1:]) for value in values))


def run_forward(state_in, dt_val, dt_u, b_in, c_out, keep_mask, neg_a):

    def block_step(state_now, blk_rows):
        dt_blk, dtu_blk, b_blk, c_blk, keep_blk = blk_rows
        cum_a, cum_b = lax.associative_scan(
            chain_link, (decay_terms(dt_blk, keep_blk, neg_a), drive_terms(b_blk, dtu_blk))
        )
        states = cum_a * state_now[None] + cum_b
        y_blk = jnp.einsum("tn,tne->te", c_blk, states, precision=PRECISE)
        return (states[-1], (state_now, y_blk))

    state_end, (starts, y_ssm) = lax.scan(
        block_step, state_in, to_blocks((dt_val, dt_u, b_in, c_out, keep_mask))
    )
    return (state_end, starts, y_ssm.reshape(dt_val.shape))


def adjoint_states(decay, c_blk, dy_blk, incoming):
    source = c_blk[:, :, None] * dy_blk[:, None, :]
    shifted = jnp.concatenate([decay[1:], jnp.ones_like(decay[:1])], 0)
    prod_a, acc_g = lax.associative_scan(chain_link, (shifted, source), reverse=True)
    return prod_a * incoming[None] + acc_g


def local_adjoint(dt_val, c_out, keep_mask, d_y, neg_a):

    def block_step(incoming, blk_rows):
        dt_blk, c_blk, keep_blk, dy_blk = blk_rows
        decay = decay_terms(dt_blk, keep_blk, neg_a)
        adjoint = adjoint_states(decay, c_blk, dy_blk, incoming)
        return (decay[0] * adjoint[0], None)

    outgoing, _ = lax.scan(
        block_step, jnp.zeros_like(neg_a), to_blocks((dt_val, c_out, keep_mask, d_y)), reverse=True
    )
    return outgoing


def run_adjoint(incoming, starts, dt_val, dt_u, b_in, c_out, keep_mask, d_y, neg_a):

    def block_step(carried, blk_rows):
        later_in, d_neg = carried
        state_in, dt_blk, dtu_blk, b_blk, c_blk, keep_blk, dy_blk = blk_rows
        decay = decay_terms(dt_blk, keep_blk, neg_a)
        adjoint = adjoint_states(decay, c_blk, dy_blk, later_in)
        cum_a, cum_b = lax.associative_scan(chain_link, (decay, drive_terms(b_blk, dtu_blk)))
        states = cum_a * state_in[None] + cum_b
        before = jnp.concatenate([state_in[None], states[:-1]], 0)
        flow = adjoint * before * decay
        d_dt_blk = jnp.sum(flow * neg_a[None], axis=1)
        d_neg = d_neg + jnp.einsum("tne,te->ne", flow, dt_blk, precision=PRECISE)
        d_dtu_blk = jnp.einsum("tne,tn->te", adjoint, b_blk, precision=PRECISE)
        d_b_blk = jnp.einsum("tne,te->tn", adjoint, dtu_blk, precision=PRECISE)
        d_c_blk = jnp.einsum("tne,te->tn", states, dy_blk, precision=PRECISE)
        return ((decay[0] * adjoint[0], d_neg), (d_dt_blk, d_dtu_blk, d_b_blk, d_c_blk))

    blk_rows = (starts,) + to_blocks((dt_val, dt_u, b_in, c_out, keep_mask, d_y))
    (_, d_neg), outs = lax.scan(
        block_step, (incoming, jnp.zeros_like(neg_a)), blk_rows, reverse=True
    )
    length = dt_val.shape[0]
    return (d_neg,) + tuple((value.reshape((length,) + value.shape[2:]) for value in outs))


F32 = jnp.float32
BF16 = jnp.bfloat16
LANES = 128
ROWS = 256
CHUNK = 128
GROUP = 16
LOG2E = 1.4426950408889634
CUT = 1e4
CUTS = 8
LATE = 4
SKIP, CONV_B, CONV_W, BIAS = STATE, STATE + 1, STATE + 2, STATE + 2 + CONV


def dot(a, b, da, db):
    return lax.dot_general(a, b, (((da,), (db,)), ((), ())), preferred_element_type=F32)


def column(row):
    return jnp.transpose(jnp.broadcast_to(row, (LANES, row.shape[1])))


def silu_slope(value, sigma):
    return sigma * (1.0 + value * (1.0 - sigma))


def flat_mask(rows):
    t = lax.broadcasted_iota(jnp.int32, (rows, LANES), 0)
    lane = lax.broadcasted_iota(jnp.int32, (rows, LANES), 1)
    return lax.rem(t, 8) == lane // STATE


def two_parts(value):
    high = value.astype(BF16).astype(F32)
    return high, value - high


def stacked(value):
    return jnp.concatenate(two_parts(value), axis=0).astype(BF16)


def outer(flat, value, out):
    mask = flat_mask(8)
    for r in range(CHUNK // 8):
        bh, bl = two_parts(jnp.where(mask, flat[r : r + 1], 0.0))
        vh, vl = two_parts(value[8 * r : 8 * r + 8])
        left = jnp.concatenate([bh, bh, bl, bl], axis=0).astype(BF16)
        right = jnp.concatenate([vh, vl, vh, vl], axis=0).astype(BF16)
        out[8 * r : 8 * r + 8] = dot(left, right, 0, 0).reshape(8, STATE, LANES)


def block_at(i, size):
    return pl.ds(pl.multiple_of(i * size, size), size)


def token_at(i, size):
    return i * size + lax.broadcasted_iota(jnp.int32, (size, LANES), 0)


def decay_step(i, bound, dt):
    t = token_at(i, CHUNK)
    return jnp.where((t == 0) | (t == bound), CUT, dt)


class Front:
    def __init__(self, bound, x_all, gain, wi, rows, wx, wbc, mod, own, outs, scratch):
        self.bound, self.x_all, self.gain, self.wi, self.rows, self.wx, self.wbc = bound, x_all, gain, wi, rows, wx, wbc
        self.mod, self.own = mod, own
        self.normed, self.inv, self.xpre, self.conv, self.u, self.gate = outs
        self.ext, self.wide = scratch
        self.ext[0:8] = jnp.zeros((8, LANES), F32)

    def block(self, at, i):
        chs, part = at.chs, self.normed.shape[1]
        tokens = self.u.shape[0]
        span = block_at(i, ROWS)
        x = jnp.concatenate([self.x_all[i * chs + c] for c in range(chs)], axis=1).astype(F32)
        inv = lax.rsqrt(jnp.mean(x * x, axis=1, keepdims=True) + EPSILON)
        normed = (x * inv * self.gain[...]).astype(BF16)
        self.inv[span] = jnp.broadcast_to(inv, (ROWS, LANES))
        self.wide[...] = normed
        self.normed[span] = self.wide[:, lanes_at(at.s, part)]
        image = column(self.mod[i, 0:1]) > 0.5
        both = [dot(normed, jnp.concatenate([self.wi[m, 0], self.wi[m, 1]], axis=1), 1, 0) for m in range(2)]
        x_pre = jnp.where(image, both[1][:, :LANES], both[0][:, :LANES]).astype(BF16)
        self.gate[span] = jnp.where(image, both[1][:, LANES:], both[0][:, LANES:])
        self.xpre[span] = x_pre
        ext = self.ext
        ext[8:] = x_pre.astype(F32)
        t = token_at(i, ROWS)
        conv = None
        for j in range(CONV):
            lag = CONV - 1 - j
            term = self.rows[CONV_W + j : CONV_W + j + 1] * ext[8 - lag : 8 - lag + ROWS]
            if lag:
                term = jnp.where((t < lag) | ((t >= self.bound) & (t - lag < self.bound)), 0.0, term)
            conv = term if conv is None else conv + term
        conv = self.rows[CONV_B : CONV_B + 1] + conv
        self.conv[span] = conv
        ext[0:8] = ext[ROWS : ROWS + 8]
        u = (conv * jax.nn.sigmoid(conv)).astype(BF16)
        self.u[span] = u
        fold = tokens // 2 // ROWS
        part_of, place_in = i // fold, lax.rem(i, fold)
        self.own[part_of, block_at(place_in, ROWS)] = jnp.where(image, dot(u, self.wx[1], 1, 1), dot(u, self.wx[0], 1, 1))
        mask = flat_mask(ROWS)
        few = ROWS // 8
        for n in range(2):
            tiled = [
                jnp.concatenate([self.wbc[m, n * STATE : (n + 1) * STATE, lanes_at(at.s, LANES)]] * 8, axis=0)
                for m in range(2)
            ]
            wide = jnp.where(mask, jnp.where(image, dot(u, tiled[1], 1, 1), dot(u, tiled[0], 1, 1)), 0.0)
            start = pl.multiple_of(tokens // 2 + n * (tokens // 16) + place_in * few, few)
            self.own[part_of, pl.ds(start, few)] = jnp.sum(wide.reshape(few, 8, LANES), axis=1)


def waves(share, order, *numbers):
    def go():
        for d in numbers:
            for n in range(share.at.depth - 1):
                if 0 <= d - n < len(order):
                    share.serve(order[d - n], n)

    return go


def first_of_second(seg_ref):
    return jnp.sum(jnp.where(seg_ref[...] == 0, 1, 0))


def chunk_image(mod, i):
    fold = ROWS // CHUNK
    return column(mod[i // fold, 0:1, lanes_at(lax.rem(i, fold), CHUNK)]) > 0.5


def half_at(xdbl, i, size):
    tokens = xdbl.shape[1] // 5 * 4
    fold = tokens // size
    return tokens, i // fold, lax.rem(i, fold)


def flats_span(xdbl, i, n, size):
    tokens, half, place_in = half_at(xdbl, i, size)
    few = size // 8
    return half, pl.ds(pl.multiple_of(tokens + n * (tokens // 8) + place_in * few, few), few)


def low_span(xdbl, i, size):
    _, half, place_in = half_at(xdbl, i, size)
    return half, block_at(place_in, size)


def flats_at(xdbl, i, n):
    return xdbl[flats_span(xdbl, i, n, CHUNK)]


def forward_kernel(
    seqs, chs, x_ref, cot_ref, wi_ref, wo_ref, wx_ref, wdt_ref, mod_ref, seg_ref, gain_ref, wbc_ref,
    alog_ref, skip_ref, convb_ref, convw_ref, bias_ref,
    xdbl, u_all, conv_all, xpre_all, dy_all, dt_all, sig_all, gated_all, dgate_all, hs_out, normed_s, cot_s, inv_all,
    wx, wdt, mod, dskip, rows_ref, gathered, *rest,
):
    totals1, totals2, spread1, spread2, trades, shares, rest = split(rest, 9, 9, 3, 3, 15, 5, 15)
    x_all, cot_all, wi, wo, gate_all, y_all, ext, wide, h_s, dta_s, x_s, hbuf, mod_own, own_all, sems = rest
    at = Place(seqs, chs)
    bound = first_of_second(seg_ref)
    mod_own[...] = jnp.broadcast_to(mod_ref[...].astype(F32), mod_own.shape)
    mine = lanes_at(at.s, LANES)
    rows_ref[...] = jnp.concatenate(
        [alog_ref[:, mine], skip_ref[:, mine], convb_ref[:, mine], convw_ref[:, mine], bias_ref[:, mine]], axis=0
    )
    own, part, low = LANES, wi_ref.shape[2], wx_ref.shape[1]
    tokens = u_all.shape[0]
    sum1, sum2 = [Total(at, xdbl.at[n], own_all.at[n], *more) for n, more in enumerate((totals1, totals2))]
    stream = Spread(at, x_ref, x_all, *spread1)
    cot = Spread(at, cot_ref, cot_all, *spread2)
    lows = pl.ds(pl.multiple_of(at.s * low, 16), low)
    plans = [
        (lambda t: wi_ref.at[:, :, :, lanes_at(t, own)], wi.at[:, :, rows_at(at.s, part)]),
        (lambda t: wx_ref.at[:, :, lanes_at(t, own)], wx.at[:, lows]),
        (lambda t: mod_own, mod.at[at.s]),
        (lambda t: wdt_ref.at[:, :, lanes_at(t, own)], wdt.at[:, lows]),
        (lambda t: wo_ref.at[:, rows_at(t, own)], wo.at[:, :, lanes_at(at.s, part)]),
    ]
    trades = [Trade(at, src, dst, *trades[3 * n : 3 * n + 3]) for n, (src, dst) in enumerate(plans)]
    at.greet(at.others + [at.side, at.across])
    stream.post(0)
    stream.post(1)
    stream.post_near()
    for trade in trades[:4]:
        trade.start()
    for level in range(3):
        stream.relay(level)
    stream.finish()
    for trade in trades[:4]:
        trade.finish()
    front = Front(
        bound, x_all, gain_ref, wi, rows_ref, wx, wbc_ref, mod, own_all,
        (normed_s, inv_all, xpre_all, conv_all, u_all, gate_all), (ext, wide),
    )

    cot.post(0)
    cot.post_near()
    half = tokens // ROWS // 2
    events = {half + 1 + n: [partial(sum1.step, n)] for n in range(3)}
    events[half] = [partial(sum1.post, 0)]
    run(tokens // ROWS, partial(front.block, at), events)
    sum2.post(0)
    sum1.step(3)
    cot.post(1)
    sum2.step(0)
    sum1.step(4)
    sum2.step(1)
    sum1.step(5)
    sum2.step(2)
    sum1.step(6)
    cot.relay(0)
    sum2.step(3)
    trades[4].start()
    sum1.take(7)
    rate = -jnp.exp(rows_ref[0:STATE]) * LOG2E
    h_s[...] = jnp.zeros_like(h_s)
    first = pltpu.make_async_copy(h_s, hs_out.at[0], sems.at[2])
    first.start()
    first.wait()

    def out_copy(i, slot):
        start = i * CHUNK + 1
        return pltpu.make_async_copy(hbuf.at[slot], hs_out.at[pl.ds(start, CHUNK)], sems.at[slot])

    def scan_step(i):
        slot = lax.rem(i, 2)
        span = block_at(i, CHUNK)
        image = chunk_image(mod, i)
        low = xdbl[low_span(xdbl, i, CHUNK)].astype(BF16)
        raw = jnp.where(
            image,
            dot(low, wdt[1], 1, 0) + rows_ref[BIAS + 1 : BIAS + 2],
            dot(low, wdt[0], 1, 0) + rows_ref[BIAS : BIAS + 1],
        )
        dt = jnp.maximum(raw, 0.0) + jnp.log1p(jnp.exp(-jnp.abs(raw)))
        u = u_all[span].astype(F32)
        dt_all[span] = dt
        sig_all[span] = jax.nn.sigmoid(raw)
        dta_s[...] = decay_step(i, bound, dt)
        outer(flats_at(xdbl, i, 0), dt * u, x_s)

        @pl.when(i >= 2)
        def _():
            out_copy(i - 2, slot).wait()

        def group(g, h):
            base = pl.multiple_of(g * GROUP, GROUP)
            for k in range(GROUP):
                h = jnp.exp2(dta_s[pl.ds(base + k, 1)] * rate) * h + x_s[base + k]
                hbuf[slot, base + k] = h
            return h

        h_s[...] = lax.fori_loop(0, CHUNK // GROUP, group, h_s[...])
        out_copy(i, slot).start()
        c_all = flats_at(xdbl, i, 1)
        mask = flat_mask(8)
        parts = []
        for r in range(CHUNK // 8):
            left = stacked(jnp.where(mask, c_all[r : r + 1], 0.0))
            made = dot(left, hbuf[slot, 8 * r : 8 * r + 8].reshape(8 * STATE, LANES).astype(BF16), 1, 0)
            parts.append(made[0:8] + made[8:16])
        y = jnp.concatenate(parts, axis=0) + rows_ref[SKIP : SKIP + 1] * u
        y_all[span] = y
        gate = gate_all[span]
        gated_all[span] = (y * (gate * jax.nn.sigmoid(gate))).astype(BF16)

    chunks = tokens // CHUNK
    cuts = list(range(CUTS))
    gated = Share(at, gated_all, gathered, CUTS, cuts[-1:], *shares)
    gated_wave = partial(waves, gated, cuts)
    events = {j: [] for j in range(chunks)}
    for cut in cuts[:-1]:
        events[2 * cut + 2].append(partial(gated.post, cut))
    for d in range(LATE):
        events[2 * d + 15 - 2 * (LATE - 1)].append(gated_wave(d))
    for n in range(3):
        events[2 * n + 1].append(partial(sum2.step, 4 + n))
    events[7].append(partial(sum2.take, 7))
    events[2].append(partial(cot.relay, 1))
    events[6].append(partial(cot.relay, 2))
    run(chunks, scan_step, events)
    gated.post(cuts[-1])
    gated.home.start()
    cot.finish()
    trades[4].finish()
    folds = seqs // chs
    slices = []
    for n in range(seqs):
        src = cot_all.at[n * chs + at.s // folds, :, lanes_at(lax.rem(at.s, folds), part)]
        slices.append(pltpu.make_async_copy(src, cot_s.at[pl.ds(n * ROWS, ROWS)], sems.at[3 + n]))
        slices[-1].start()
    dskip[...] = jnp.zeros_like(dskip)

    def gate_step(i):
        span = block_at(i, ROWS)
        image = column(mod[i, 0:1]) > 0.5
        cots = jnp.concatenate([cot_all[i * chs + c] for c in range(chs)], axis=1)
        d_gated = jnp.where(image, dot(cots, wo[1], 1, 1), dot(cots, wo[0], 1, 1))
        gate = gate_all[span]
        sigma = jax.nn.sigmoid(gate)
        d_y = d_gated * gate * sigma
        dy_all[span] = d_y
        dgate_all[span] = (d_gated * y_all[span] * silu_slope(gate, sigma)).astype(BF16)
        dskip[...] += jnp.sum(d_y * u_all[span].astype(F32), axis=0, keepdims=True)

    run(tokens // ROWS, gate_step, {n: [gated_wave(LATE + n)] for n in range(10 - LATE)})
    for cut in cuts:
        gated.arrived(cut)
    gated.home.wait()
    gated.finish()
    for i in (chunks - 2, chunks - 1):
        out_copy(i, i % 2).wait()
    for copy in slices:
        copy.wait()
    sum1.finish()
    sum2.finish()


def adjoint_chunk(bound, i, state, xdbl, u_all, dy_all, dt_all, sig_all, mod, wdt, rows_ref, own, du_all, grads, scratch):
    ga_s, dn_s, dta_s, x_s, g_s, f_s = scratch
    dwdt, dbias = grads
    tokens = u_all.shape[0]
    span = block_at(i, CHUNK)
    dt = dt_all[span]
    u = u_all[span].astype(F32)
    d_y = dy_all[span]
    dta_s[...] = decay_step(i, bound, dt)
    neg_a = -jnp.exp(rows_ref[0:STATE])
    rate = neg_a * LOG2E
    outer(flats_at(xdbl, i, 1), d_y, x_s)
    start = pl.multiple_of(i * CHUNK, CHUNK)

    def group(step, carried):
        ga, dn = carried
        base = pl.multiple_of((CHUNK // GROUP - 1 - step) * GROUP, GROUP)
        for k in reversed(range(GROUP)):
            adjoint = x_s[base + k] + ga
            ga = jnp.exp2(dta_s[pl.ds(base + k, 1)] * rate) * adjoint
            slow = ga * state[base + k] * neg_a
            dn = dn + slow * dt_all[pl.ds(start + base + k, 1)]
            g_s[base + k] = adjoint.astype(BF16)
            f_s[base + k] = slow.astype(BF16)
        return ga, dn

    ga, dn = lax.fori_loop(0, CHUNK // GROUP, group, (ga_s[...], dn_s[...]))
    ga_s[...] = ga
    dn_s[...] = dn
    dtu = dt * u
    b_all = flats_at(xdbl, i, 0)
    mask = flat_mask(8)
    ones = jnp.where(flat_mask(16), 1.0, 0.0).astype(BF16)
    pu, pd, db, dc = [], [], [], []
    for r in range(CHUNK // 8):
        few = slice(8 * r, 8 * r + 8)
        adjoint = g_s[few].reshape(8 * STATE, LANES)
        slow = f_s[few].reshape(8 * STATE, LANES)
        h = state[8 * r + 1 : 8 * r + 9].reshape(8 * STATE, LANES).astype(BF16)
        made = dot(stacked(jnp.where(mask, b_all[r : r + 1], 0.0)), adjoint, 1, 0)
        pu.append(made[0:8] + made[8:16])
        pd.append(dot(ones, slow, 1, 0)[0:8])
        for out, value, other in ((db, dtu, adjoint), (dc, d_y, h)):
            made = dot(stacked(value[few]), other, 1, 1)
            out.append(jnp.sum(jnp.where(mask, made[0:8] + made[8:16], 0.0), axis=0, keepdims=True))
    d_dtu = jnp.concatenate(pu, axis=0)
    d_dt = jnp.concatenate(pd, axis=0) + d_dtu * u
    for n, part in enumerate((db, dc)):
        own[flats_span(own, i, n, CHUNK)] = jnp.concatenate(part, axis=0)
    du_all[span] = d_y * rows_ref[SKIP : SKIP + 1] + d_dtu * dt
    d_raw = (d_dt * sig_all[span]).astype(BF16)
    image = chunk_image(mod, i)
    low = xdbl[low_span(xdbl, i, CHUNK)].astype(BF16)
    own[low_span(own, i, CHUNK)] = jnp.where(image, dot(d_raw, wdt[1], 1, 1), dot(d_raw, wdt[0], 1, 1))
    raw_f = d_raw.astype(F32)
    for m in range(2):
        mine = jnp.where(image == (m == 1), raw_f, 0.0)
        dwdt[m] += dot(low, mine.astype(BF16), 0, 0)
        dbias[m : m + 1] += jnp.sum(mine, axis=0, keepdims=True)


def rear_block(bound, i, at, dx, du_all, u_all, conv_all, xpre_all, mod, wx, wbc, rows_ref, dpre_all, grads, scratch):
    dwx, dwbc, dconv = grads
    ext, ahead = scratch
    tokens = u_all.shape[0]
    span = block_at(i, ROWS)
    few = ROWS // 8
    image = column(mod[i, 0:1]) > 0.5
    low = dx[low_span(dx, i, ROWS)].astype(BF16)
    mask = flat_mask(ROWS)
    lane = lax.broadcasted_iota(jnp.int32, (LANES, 2 * STATE), 0)
    state = lax.broadcasted_iota(jnp.int32, (LANES, 2 * STATE), 1)
    d_bc = None
    for n in range(2):
        fold = jnp.where(lax.rem(lane, STATE) + n * STATE == state, 1.0, 0.0).astype(BF16)
        flat = dx[flats_span(dx, i, n, ROWS)]
        wide = jnp.broadcast_to(flat[:, None, :], (few, 8, LANES)).reshape(ROWS, LANES)
        part = dot(jnp.where(mask, wide, 0.0).astype(BF16), fold, 1, 0)
        d_bc = part if d_bc is None else d_bc + part
    d_bc = d_bc.astype(BF16)
    u = u_all[span]
    extra = [dot(low, wx[m], 1, 0) + dot(d_bc, wbc[m, :, lanes_at(at.s, LANES)], 1, 0) for m in range(2)]
    d_u = du_all[span] + jnp.where(image, extra[1], extra[0])
    u_f = u.astype(F32)
    for m in range(2):
        mine = jnp.where(image == (m == 1), u_f, 0.0).astype(BF16)
        dwx[m] += dot(low, mine, 0, 0)
        dwbc[m] += dot(d_bc, mine, 0, 0)
    conv = conv_all[span]
    d_conv = d_u * silu_slope(conv, jax.nn.sigmoid(conv))
    before = lax.rem(i * ROWS + tokens - 16, tokens)
    ext[0:8] = xpre_all[pl.ds(pl.multiple_of(before, 16), 16)].astype(F32)[8:16]
    ext[8:] = xpre_all[span].astype(F32)
    ahead[ROWS : ROWS + 8] = ahead[0:8]
    ahead[0:ROWS] = d_conv
    t = token_at(i, ROWS)
    d_pre = None
    for tap in range(CONV):
        lag = CONV - 1 - tap
        seen = ext[8 - lag : 8 - lag + ROWS] * d_conv
        term = rows_ref[CONV_W + tap : CONV_W + tap + 1] * ahead[lag : lag + ROWS]
        if lag:
            seen = jnp.where((t < lag) | ((t >= bound) & (t - lag < bound)), 0.0, seen)
            term = jnp.where((t < bound) & (t + lag >= bound), 0.0, term)
        dconv[tap : tap + 1] += jnp.sum(seen, axis=0, keepdims=True)
        d_pre = term if d_pre is None else d_pre + term
    dconv[CONV : CONV + 1] += jnp.sum(d_conv, axis=0, keepdims=True)
    dpre_all[span] = d_pre.astype(BF16)


def grown(image, width):
    return jnp.concatenate([image] * (width // LANES), axis=1)


def out_block(i, gated, cot_s, mod, wo, branch, dwo):
    span = block_at(i, ROWS)
    wide = jnp.concatenate([gated[n, span] for n in range(gated.shape[0])], axis=1)
    cot = cot_s[span].astype(F32)
    image = grown(column(mod[i, 0:1]) > 0.5, cot.shape[1])
    branch[span] = jnp.where(image, dot(wide, wo[1], 1, 0), dot(wide, wo[0], 1, 0))
    for m in range(2):
        dwo[m] += dot(wide, jnp.where(image == (m == 1), cot, 0.0).astype(BF16), 0, 0)


def in_block(i, k, first, dz_all, normed_s, mod, wi, d_norm, dwi):
    span = block_at(i, ROWS)
    dz = jnp.concatenate([dz_all[n, span] for n in range(dz_all.shape[0])], axis=1)
    normed = normed_s[span].astype(F32)
    image = grown(column(mod[i, 0:1]) > 0.5, normed.shape[1])
    total = jnp.where(image, dot(dz, wi[1, k], 1, 1), dot(dz, wi[0, k], 1, 1))
    d_norm[span] = total if first else d_norm[span] + total
    for m in range(2):
        dwi[m, k] += dot(jnp.where(image == (m == 1), normed, 0.0).astype(BF16), dz, 0, 0)


def backward_kernel(
    seqs, chs, seg_ref, xdbl, u_all, conv_hbm, xpre_hbm, dy_all, dt_all, sig_all, gated_hbm, dgate_own, hs,
    normed_hbm, cot_hbm, inv_hbm, wx, wdt, mod, dskip, wbc, rows_ref, wi_hbm, wo_hbm, gain_ref, x_ref, own_cot,
    out_ref, grad_ref, sums_ref, dwi_out, dwo_out, small_ref, parts_ref, *rest,
):
    totals1, totals2, branches, norms, shares, trades, rest = split(rest, 9, 9, 9, 9, 15, 3, len(rest) - 54)
    (
        dx, du_all, dpre_own, gated_all, dgate_all, dpre_all, conv_all, xpre_all, normed_s, cot_s, wi, wo, inv,
        branch, d_norm, hbuf, ga_s, dn_s, dta_s, x_s, g_s, f_s, ext, ahead, dwdx, dwbc, dbias, dconv,
        small_own, small_all, dots, r3, pay, r4, hsem, lsem, dsend, drecv, gsend, grecv, psend, precv, dwi, dwo, own_all, osem,
    ) = rest
    at = Place(seqs, chs)
    bound = first_of_second(seg_ref)
    tokens, own, rows = u_all.shape[0], LANES, x_ref.shape[0]
    chunks, blocks = tokens // CHUNK, tokens // ROWS

    def state_copy(i, slot):
        return pltpu.make_async_copy(hs.at[pl.ds(i * CHUNK, CHUNK + 1)], hbuf.at[slot], hsem.at[slot])

    state_copy(chunks - 1, 0).start()
    late = [
        (conv_hbm, conv_all), (xpre_hbm, xpre_all), (normed_hbm, normed_s), (cot_hbm, cot_s), (wi_hbm, wi),
        (wo_hbm, wo), (gated_hbm, gated_all), (inv_hbm.at[block_at(at.s, rows)], inv),
    ]
    late = [pltpu.make_async_copy(src, dst, lsem.at[n]) for n, (src, dst) in enumerate(late)]
    for copy in late:
        copy.start()
    sum1, sum2 = [Total(at, dx.at[n], own_all.at[n], *more) for n, more in enumerate((totals1, totals2))]
    ups, downs = list(range(CUTS)), list(reversed(range(CUTS)))
    d_gate = Share(at, dgate_own, dgate_all, CUTS, ups[-1:], *shares[0:5])
    d_pre = Share(at, dpre_own, dpre_all, CUTS, downs[-1:], *shares[5:10])
    small = Share(at, small_own, small_all, 1, [], *shares[10:15])

    wave = waves

    def post(share, *cuts):
        def go():
            for cut in cuts:
                share.post(cut)

        return go

    at.greet(at.mates + at.others + Regroup.sources(at))
    post(d_gate, *ups)()
    d_gate.home.start()
    for ref in (ga_s, dn_s, dwdx, dwbc, dbias, dconv, ahead, dwi, dwo):
        ref[...] = jnp.zeros_like(ref)

    def adjoint_step(j):
        i = chunks - 1 - j
        slot = lax.rem(j, 2)
        state_copy(i, slot).wait()

        @pl.when(j < chunks - 1)
        def _():
            state_copy(i - 1, 1 - slot).start()

        adjoint_chunk(
            bound, i, hbuf.at[slot], xdbl, u_all, dy_all, dt_all, sig_all, mod, wdt, rows_ref, own_all, du_all,
            (dwdx.at[1], dbias), (ga_s, dn_s, dta_s, x_s, g_s, f_s),
        )

    events = {j: [] for j in range(chunks)}
    for d in range(7):
        events[2 * d + 3].append(wave(d_gate, ups, d))
    half = chunks // 2
    events[half].append(partial(sum2.post, 0))
    for n, j in enumerate((half + 1, half + 3, half + 6)):
        events[j].append(partial(sum2.step, n))
    run(chunks, adjoint_step, events)
    sum1.post(0)
    for copy in late:
        copy.wait()
    branch_sum = Regroup(at, branch, *branches)
    norm_sum = Regroup(at, d_norm, *norms)

    def rear_step(j):
        rear_block(
            bound, blocks - 1 - j, at, dx, du_all, u_all, conv_all, xpre_all, mod, wx, wbc, rows_ref, dpre_own,
            (dwdx.at[0], dwbc, dconv), (ext, ahead),
        )
        d_pre.post(blocks - 1 - j)

    def rear_late(j):
        rear_step(blocks // 2 + j)

    def out_step(i):
        out_block(i, gated_all, cot_s, mod, wo, branch, dwo)

    def first_step(i):
        in_block(i, 1, True, dgate_all, normed_s, mod, wi, d_norm, dwi)

    quarters = blocks // 2

    def outs(q):
        run(2, lambda n: out_step(2 * q + n), {})
        branch_sum.one(q)

    sum2.step(3)
    sum1.step(0)
    wave(d_gate, ups, 7)()
    outs(0)
    sum2.step(4)
    sum1.step(1)
    outs(1)
    sum2.step(5)
    sum1.step(2)
    wave(d_gate, ups, 8)()
    outs(2)
    sum2.step(6)
    sum1.step(3)
    outs(3)
    sum2.take(7)
    run(blocks // 2, rear_step, {3: [partial(sum1.step, 4)]})
    sum1.step(5)
    wave(d_gate, ups, 9)()
    for q in range(quarters):
        branch_sum.two(q)
    sum1.step(6)
    wave(d_pre, downs, 0)()
    for cut in range(CUTS):
        d_gate.arrived(cut)
    d_gate.home.wait()
    run(blocks // 2, first_step, {2: [wave(d_pre, downs, 1)]})
    sum1.take(7)
    run(blocks // 2, rear_late, {0: [wave(d_pre, downs, 2)], 2: [wave(d_pre, downs, 3)]})
    d_pre.home.start()
    small_own[...] = jnp.concatenate(
        [dn_s[...], dconv[...], dbias[...], dskip[...], jnp.zeros((5, own), F32), dwbc[0], dwbc[1]], axis=0
    )
    low = parts_ref.shape[2]
    parts = Trade(
        at, lambda t: dwdx.at[:, :, rows_at(t, low)], parts_ref.at[:, :, :, lanes_at(at.s, own)], *trades
    )
    written = [pltpu.make_async_copy(dwo, dwo_out, osem.at[2])]
    for k in range(2):
        written.append(pltpu.make_async_copy(dwi.at[:, k], dwi_out.at[:, k], osem.at[k]))
    written[0].start()
    for q in range(quarters):
        branch_sum.three(q)
    run(blocks // 2, lambda j: first_step(blocks // 2 + j), {0: [wave(d_pre, downs, 4)], 2: [wave(d_pre, downs, 5)]})
    small.post(0)
    small.home.start()
    parts.start()
    written[2].start()
    d_pre.home.wait()

    def second_step(j):
        i = blocks - 1 - j
        in_block(i, 0, False, dpre_all, normed_s, mod, wi, d_norm, dwi)
        q = i // 2

        @pl.when(lax.rem(j, 2) == 1)
        def _():
            norm_sum.one(q)

        @pl.when((lax.rem(j, 2) == 0) & (j > 1))
        def _():
            norm_sum.two(q + 1)

        @pl.when((lax.rem(j, 2) == 1) & (j > 2))
        def _():
            norm_sum.three(q + 1)

    events = {j: [wave(d_pre, downs, j + 6), partial(d_pre.arrived, downs[j])] for j in range(blocks)}
    for n in range(3):
        events[2 * n + 1].append(partial(small.serve, 0, n))
    run(blocks, second_step, events)
    written[1].start()
    added = branch_sum.result()
    xs = x_ref[...].astype(F32)
    mixed = xs + added
    out_ref[...] = mixed.astype(BF16)
    norm_sum.two(0)
    norm_sum.three(0)
    inv_own = inv[...][:, 0:1]
    x_hat = xs * inv_own
    width = chs * x_ref.shape[1]
    gain = gain_ref[:, lanes_at(at.c, x_ref.shape[1])]
    total_norm = norm_sum.result()
    d_hat = total_norm * gain
    dot_part = jnp.sum(d_hat * x_hat, axis=1, keepdims=True)
    dots[...] = jnp.transpose(jnp.broadcast_to(dot_part, (rows, LANES)))[0:8]
    third = [remote(dots, r3.at[k], dsend.at[k], drecv.at[k], mate) for k, mate in enumerate(at.mates)]
    for copy in third:
        copy.start()
    rows_of = [total_norm * x_hat, xs * xs, added * added, mixed * mixed]
    pay[...] = jnp.concatenate(
        [jnp.sum(v, axis=0, keepdims=True) for v in rows_of] + [jnp.zeros((4, x_ref.shape[1]), F32)], axis=0
    )
    fourth = [remote(pay, r4.at[k], gsend.at[k], grecv.at[k], other) for k, other in enumerate(at.others)]
    for copy in fourth:
        copy.start()
    dot_sum = dots[...]
    for k, copy in enumerate(third):
        copy.wait_recv()
        dot_sum = dot_sum + r3[k]
    inner = column(dot_sum[0:1])[:, 0:1] / width
    grad_ref[...] = own_cot[...].astype(F32) + inv_own * (d_hat - x_hat * inner)
    joint = pay[...]
    for k, copy in enumerate(fourth):
        copy.wait_recv()
        joint = joint + r4[k]
    sums_ref[at.c] = joint
    spot = sums_ref.at[at.c]
    fifth = [remote(spot, spot, psend.at[k], precv.at[k], mate) for k, mate in enumerate(at.mates)]
    for copy in fifth:
        copy.start()
    for copy in fifth:
        copy.wait_recv()
    for copy in written:
        copy.wait()
    small.arrived(0)
    small.home.wait()
    parts.finish()
    for n in range(seqs):
        small_ref[:, n * own : (n + 1) * own] = small_all[n]
    for share in (d_gate, d_pre, small):
        share.finish()
    for copy in third + fourth + fifth:
        copy.wait_send()
    branch_sum.finish()
    norm_sum.finish()
    sum1.finish()
    sum2.finish()


def unpack_kernel(
    small_ref, sums_ref, parts_ref, in0, in1, in2, in3,
    gain, conv_w, conv_b, w_xdt, w_xbc, w_dt, bias, a_log, skip, stats, out0, out1, out2, out3,
):
    for src, dst in ((in0, out0), (in1, out1), (in2, out2), (in3, out3)):
        dst[...] = src[...]

    @pl.when(pl.program_id(0) == 0)
    def _():
        a_log[...] = small_ref[0:STATE]
        conv_w[...] = small_ref[STATE : STATE + CONV]
        conv_b[...] = small_ref[STATE + CONV : STATE + CONV + 1]
        bias[...] = small_ref[STATE + 8 : STATE + 10]
        skip[...] = small_ref[STATE + 10 : STATE + 11]
        for m in range(2):
            w_xbc[m] = small_ref[32 + 2 * STATE * m : 32 + 2 * STATE * (m + 1)]
        w_xdt[...] = parts_ref[0]
        w_dt[...] = parts_ref[1]
        cols = sums_ref.shape[2]
        total = sums_ref[0]
        for c in range(sums_ref.shape[0]):
            gain[:, c * cols : (c + 1) * cols] = sums_ref[c, 0:1]
            if c:
                total = total + sums_ref[c]
        size = float(gain.shape[1] * sums_ref.shape[0] * cols)
        mean = jnp.sum(total, axis=1, keepdims=True)[1:4] / size
        stats[...] = jnp.sqrt(jnp.transpose(jnp.broadcast_to(mean, (3, LANES)))[0:1, 0:3])

MESH = pl.DeviceIdType.MESH


def remote(src, dst, send, recv, peer):
    return pltpu.make_async_remote_copy(
        src_ref=src, dst_ref=dst, send_sem=send, recv_sem=recv,
        device_id={"seq": peer[0], "ch": peer[1]}, device_id_type=MESH,
    )


def rows_at(start, size):
    return pl.ds(pl.multiple_of(start * size, 8), size)


def lanes_at(start, size):
    return pl.ds(pl.multiple_of(start * size, LANES), size)


class Place:
    def __init__(self, seqs, chs):
        self.seqs, self.chs, self.depth = seqs, chs, seqs // 2
        self.s, self.c = lax.axis_index("seq"), lax.axis_index("ch")
        self.z, self.x = self.s // 2, lax.rem(self.s, 2)
        self.y, self.o = self.c // 2, lax.rem(self.c, 2)
        self.side = (self.s, self.y * 2 + 1 - self.o)
        self.across = (self.s, (1 - self.y) * 2 + self.o)
        self.beside = (self.z * 2 + 1 - self.x, self.c)
        self.deep = [(lax.rem(self.z + k, self.depth) * 2 + self.x, self.c) for k in range(1, self.depth)]
        self.others = [(lax.rem(self.s + k, seqs), self.c) for k in range(1, seqs)]
        self.mates = [(self.s, lax.rem(self.c + k, chs)) for k in range(1, chs)]

    def greet(self, peers):
        barrier = pltpu.get_barrier_semaphore()
        for seq, ch in peers:
            pl.semaphore_signal(barrier, inc=1, device_id={"seq": seq, "ch": ch}, device_id_type=MESH)
        pl.semaphore_wait(barrier, len(peers))


class Spread:
    ORDERS = ((0, 1, 2, 3), (0, 2, 1, 3))
    ORIGIN = (0, 0, 0, 0)

    @staticmethod
    def semaphores(seqs):
        dma = pltpu.SemaphoreType.DMA
        return [dma((2, 4 * seqs)), dma((2, 4 * seqs)), dma((1,))]

    def __init__(self, at, src, out, send, recv, local):
        self.at, self.src, self.out, self.send, self.recv = at, src, out, send, recv
        self.half = src.shape[0] // 2
        self.home = pltpu.make_async_copy(src, out.at[at.s * at.chs + at.c], local.at[0])

    def index(self, role):
        return ((role[0] * 2 + role[1]) * 2 + role[2]) * 2 + role[3]

    def piece(self, cut, role):
        at = self.at
        dz, dx, dy, do = role
        src = lax.rem(at.z + at.depth - dz, at.depth) * 2 + (1 - at.x if dx else at.x)
        col = (1 - at.y if dy else at.y) * 2 + (1 - at.o if do else at.o)
        return self.out.at[src * at.chs + col, pl.ds(cut * self.half, self.half)]

    def hop(self, cut, role, axis, step=1):
        at = self.at
        peer = (at.deep[step - 1], at.beside, at.across, at.side)[axis]
        src = self.piece(cut, role)
        if role == self.ORIGIN:
            src = self.src.at[pl.ds(cut * self.half, self.half)]
        index = self.index(tuple(step if i == axis else v for i, v in enumerate(role)))
        return remote(src, self.piece(cut, role), self.send.at[cut, index], self.recv.at[cut, index], peer)

    def roles(self, cut, level):
        order = self.ORDERS[cut]
        for step in range(self.at.depth):
            for extra in range(max(level, 1)):
                role = [step, 0, 0, 0]
                if level:
                    role[order[level]] = 1
                if extra:
                    role[order[1]] = 1
                if tuple(role) != self.ORIGIN:
                    yield tuple(role)

    def arrived(self, cut, role):
        spot, index = self.piece(cut, role), self.index(role)
        remote(spot, spot, self.send.at[cut, index], self.recv.at[cut, index], self.at.side).wait_recv()

    def post(self, cut):
        for step in range(1, self.at.depth):
            self.hop(cut, self.ORIGIN, 0, step).start()

    def post_near(self):
        for cut in range(2):
            for axis in self.ORDERS[cut][1:]:
                self.hop(cut, self.ORIGIN, axis).start()
        self.home.start()

    def relay(self, level):
        for cut in range(2):
            for role in self.roles(cut, level):
                self.arrived(cut, role)
                for axis in self.ORDERS[cut][level + 1 :]:
                    self.hop(cut, role, axis).start()

    def finish(self):
        for cut in range(2):
            for step in range(self.at.depth):
                for dx in range(2):
                    for dy in range(2):
                        self.arrived(cut, (step, dx, dy, 1))
        self.home.wait()
        for cut in range(2):
            order = self.ORDERS[cut]
            for step in range(1, self.at.depth):
                self.hop(cut, self.ORIGIN, 0, step).wait_send()
            for axis in order[1:]:
                self.hop(cut, self.ORIGIN, axis).wait_send()
            for level in range(3):
                for role in self.roles(cut, level):
                    for axis in order[level + 1 :]:
                        self.hop(cut, role, axis).wait_send()


class Trade:
    @staticmethod
    def semaphores(seqs):
        dma = pltpu.SemaphoreType.DMA
        return [dma((seqs - 1,)), dma((seqs - 1,)), dma((1,))]

    def __init__(self, at, src_for, dst, send, recv, local):
        self.copies = [
            remote(src_for(peer[0]), dst, send.at[k], recv.at[k], peer) for k, peer in enumerate(at.others)
        ]
        self.home = pltpu.make_async_copy(src_for(at.s), dst, local.at[0])

    def start(self):
        for copy in self.copies:
            copy.start()
        self.home.start()

    def finish(self):
        for copy in self.copies:
            copy.wait_recv()
        self.home.wait()
        for copy in self.copies:
            copy.wait_send()


class Share:
    @staticmethod
    def semaphores(seqs, cuts):
        dma, depth = pltpu.SemaphoreType.DMA, seqs // 2
        return [dma((cuts, 4, depth)), dma((cuts, 2, depth)), dma((cuts, depth)), dma((cuts, depth)), dma((1,))]

    def __init__(self, at, src, out, cuts, turned, send, recv, hop_s, hop_r, local, base=0, rows=None):
        self.at, self.src, self.out, self.cuts, self.turned = at, src, out, cuts, turned
        rows = rows or src.shape[0]
        self.size, self.base = rows // cuts, base
        self.z = (send, recv)
        self.x = (hop_s, hop_r)
        span = pl.ds(base, rows)
        self.home = pltpu.make_async_copy(src.at[span], out.at[at.s, span], local.at[0])
        first, last = (at.depth - 1 - at.z) // (at.depth - 1), at.z // (at.depth - 1)
        self.order = (1 + 2 * first, 3 - first - last, 2 - first + last)

    def piece(self, cut, side, r):
        at = self.at
        owner = lax.rem(at.z + at.depth - r, at.depth) * 2 + (1 - at.x if side else at.x)
        return self.out.at[owner, pl.ds(self.base + cut * self.size, self.size)]

    def origin(self, cut):
        return self.src.at[pl.ds(self.base + cut * self.size, self.size)]

    def along(self, cut, side, r, way):
        at = self.at
        own = isinstance(r, int) and r == 0
        if way == 0:
            there = at.z < at.depth - 1 if own else (at.z >= r) & (at.z < at.depth - 1)
            role, peer = r + 1, at.z + 1
        else:
            there = at.z > 0 if own else (at.z < r) & (at.z > 0)
            role, peer = (at.depth - 1 if own else r - 1), at.z - 1
        spot = self.piece(cut, side, r)
        src = self.origin(cut) if own and not side else spot
        copy = remote(
            src, spot, self.z[0].at[cut, 2 * side + way, r], self.z[1].at[cut, side, role], (peer * 2 + at.x, at.c)
        )
        return there, copy

    def pass_on(self, cut, side, r):
        for way in range(2):
            there, copy = self.along(cut, side, r, way)
            pl.when(there)(copy.start)

    def beside(self, cut, r):
        spot = self.piece(cut, 0, r)
        src = self.origin(cut) if isinstance(r, int) and r == 0 else spot
        return remote(src, spot, self.x[0].at[cut, r], self.x[1].at[cut, r], self.at.beside)

    def is_turned(self, cut):
        return cut in self.turned

    def post(self, cut):
        self.pass_on(cut, 0, 0)
        self.beside(cut, 0).start()

    def wait_z(self, cut, side, r):
        spot = self.piece(cut, side, r)
        remote(spot, spot, self.z[0].at[cut, 0, 0], self.z[1].at[cut, side, r], self.at.beside).wait_recv()

    def wait_x(self, cut, r):
        spot = self.piece(cut, 1, r)
        remote(spot, spot, self.x[0].at[cut, r], self.x[1].at[cut, r], self.at.beside).wait_recv()

    def serve(self, cut, n):
        r = self.order[n]
        if not self.is_turned(cut):
            self.wait_z(cut, 0, r)
            self.pass_on(cut, 0, r)
            self.beside(cut, r).start()
            return
        if n == 0:
            self.wait_x(cut, 0)
            self.pass_on(cut, 1, 0)
        for side in range(2):
            self.wait_z(cut, side, r)
            self.pass_on(cut, side, r)

    def arrived(self, cut):
        if not self.is_turned(cut):
            for r in range(self.at.depth):
                self.wait_x(cut, r)

    def finish(self):
        for cut in range(self.cuts):
            turned = self.is_turned(cut)
            for side in range(2 if turned else 1):
                for r in range(self.at.depth):
                    for way in range(2):
                        there, copy = self.along(cut, side, r, way)
                        pl.when(there)(copy.wait_send)
            for r in range(1 if turned else self.at.depth):
                self.beside(cut, r).wait_send()


class Total:
    @staticmethod
    def scratch(seqs, rows):
        depth, dma = seqs // 2, pltpu.SemaphoreType.DMA

        def vmem(*shape):
            return pltpu.VMEM(shape + (LANES,), F32)

        return [
            vmem(rows // 2), vmem(2, rows // 8), vmem(2, rows // 16), vmem(depth - 1, rows // 8 // depth),
            vmem(rows // 2), vmem(2, rows // 8), vmem(2, rows // 16), dma((8, 2, depth)), dma((8, 2, depth)),
        ]

    def __init__(self, at, out, own, r0, r1, r2, r3, a1, a2, a3, send, recv):
        self.at, self.out, self.own = at, out, own
        self.r0, self.r1, self.r2, self.r3, self.a1, self.a2, self.a3 = r0, r1, r2, r3, a1, a2, a3
        self.send, self.recv = send, recv
        self.rows = own.shape[0]
        self.bits = ((at.y, at.x), (at.x, at.y))
        self.peers = ((at.across, at.beside), (at.beside, at.across))

    def halved(self, n, g):
        rows = self.rows
        src = self.a1.at[pl.ds(g * (rows // 4), rows // 4)] if n == 1 else self.a2.at[g]
        size = (self.r1, self.r2)[n - 1].shape[1]
        return src, self.bits[g][n - 1], size

    def spot(self, g, level):
        at, rows = self.at, self.rows
        start = at.o * (rows // 2)
        if level > 0:
            start = start + g * (rows // 4) + self.bits[g][0] * (rows // 8)
        if level > 1:
            start = start + self.bits[g][1] * (rows // 16)
        size = (rows // 2, rows // 8, rows // 16)[level]
        return pl.ds(pl.multiple_of(start, 8), size)

    def band(self, z):
        fold = self.at.depth // 2
        return z // fold, rows_at(lax.rem(z, fold), self.r3.shape[1])

    def band_spot(self):
        at, rows = self.at, self.rows
        g, fold = at.z // (at.depth // 2), at.depth // 2
        start = at.o * (rows // 2) + g * (rows // 4) + lax.rem(at.z, fold) * self.r3.shape[1]
        start = start + (at.y + g * (at.x - at.y)) * (rows // 8) + (at.x + g * (at.y - at.x)) * (rows // 16)
        return pl.ds(pl.multiple_of(start, 8), self.r3.shape[1])

    def transfers(self, n):
        at, rows = self.at, self.rows
        plan = []
        for g in range(1 if n in (0, 3, 4, 7) else 2):
            if n == 0:
                plan.append((self.own.at[rows_at(1 - at.o, rows // 2)], self.r0, g, 0, at.side))
            elif n < 3:
                src, bit, size = self.halved(n, g)
                plan.append((src.at[rows_at(1 - bit, size)], (self.r1, self.r2)[n - 1].at[g], g, 0, self.peers[g][n - 1]))
            elif n == 3:
                for k, peer in enumerate(at.deep):
                    there = lax.rem(at.z + 1 + k, at.depth)
                    plan.append((self.a3.at[self.band(there)], self.r3.at[k], g, k, peer))
            else:
                spot = self.out.at[self.band_spot() if n == 4 else self.spot(g, 7 - n)]
                peers = at.deep if n == 4 else [at.side if n == 7 else self.peers[g][6 - n]]
                for k, peer in enumerate(peers):
                    plan.append((spot, spot, g, k, peer))
        return [remote(src, dst, self.send.at[n, g, k], self.recv.at[n, g, k], peer) for src, dst, g, k, peer in plan]

    def post(self, n):
        for copy in self.transfers(n):
            copy.start()

    def take(self, n):
        at = self.at
        for copy in self.transfers(n):
            copy.wait_recv()
        if n == 0:
            self.a1[...] = self.own[rows_at(at.o, self.rows // 2)] + self.r0[...]
        elif n < 3:
            for g in range(2):
                src, bit, size = self.halved(n, g)
                (self.a2, self.a3)[n - 1][g] = src[rows_at(bit, size)] + (self.r1, self.r2)[n - 1][g]
        elif n == 3:
            total = self.a3[self.band(at.z)]
            for k in range(at.depth - 1):
                total = total + self.r3[k]
            self.out[self.band_spot()] = total

    def step(self, n):
        self.take(n)
        self.post(n + 1)

    def finish(self):
        for n in range(8):
            for copy in self.transfers(n):
                copy.wait_send()


class Regroup:
    @staticmethod
    def scratch(seqs, chs, tokens, part):
        folds, vmem, dma = seqs // chs, pltpu.VMEM, pltpu.SemaphoreType.DMA
        n, rows = seqs // 2, tokens // seqs
        half = rows // 2
        return [
            vmem((n, rows, part), F32), vmem((n, rows, part), F32), vmem((n, half, part), BF16),
            vmem((n, half, part), BF16), vmem((n, half, part), BF16), vmem((folds, 2, half, part), BF16),
            dma((n, 3)), dma((n, 2)), dma((folds, 2)),
        ]

    @staticmethod
    def sources(at):
        folds = at.seqs // at.chs
        return [(at.c * folds + f, y * 2 + lax.rem(at.s, 2)) for f in range(folds) for y in range(2)]

    def __init__(self, at, src, r0, a1, sb, r1, fb, r2, send, recv, last):
        self.at, self.src = at, src
        self.r0, self.a1, self.sb, self.r1, self.fb, self.r2 = r0, a1, sb, r1, fb, r2
        self.send, self.recv, self.last = send, recv, last
        self.quarters, self.rows, self.half = r0.shape[0], r0.shape[1], r1.shape[1]
        self.folds = at.seqs // at.chs
        self.home, self.slot = at.s // self.folds, lax.rem(at.s, self.folds)

    def first(self, q):
        at = self.at
        src = self.src.at[rows_at(2 * q + 1 - at.o, self.rows)]
        return remote(src, self.r0.at[q], self.send.at[q, 0], self.recv.at[q, 0], at.side)

    def second(self, q):
        return remote(self.sb.at[q], self.r1.at[q], self.send.at[q, 1], self.recv.at[q, 1], self.at.across)

    def third(self, q):
        at = self.at
        dst, sem = self.r2.at[self.slot, at.y], self.last.at[self.slot, at.y]
        away = jnp.logical_or(2 * q + at.o != at.s, self.home != at.c)
        there = remote(self.fb.at[q], dst, self.send.at[q, 2], sem, (2 * q + at.o, self.home))
        return away, there, pltpu.make_async_copy(self.fb.at[q], dst, sem)

    def one(self, q):
        self.first(q).start()

    def two(self, q):
        at = self.at
        self.first(q).wait_recv()
        self.a1[q] = self.src[rows_at(2 * q + at.o, self.rows)] + self.r0[q]
        self.sb[q] = self.a1[q, rows_at(1 - at.y, self.half)].astype(BF16)
        self.second(q).start()

    def three(self, q):
        at = self.at
        self.second(q).wait_recv()
        self.fb[q] = (self.a1[q, rows_at(at.y, self.half)] + self.r1[q].astype(F32)).astype(BF16)
        away, there, here = self.third(q)
        pl.when(away)(there.start)
        pl.when(jnp.logical_not(away))(here.start)

    def result(self):
        for f in range(self.folds):
            for y in range(2):
                spot = self.r2.at[f, y]
                remote(self.fb.at[0], spot, self.send.at[0, 2], self.last.at[f, y], self.at.side).wait_recv()
        rows = [jnp.concatenate([self.r2[f, 0], self.r2[f, 1]], axis=0) for f in range(self.folds)]
        return jnp.concatenate(rows, axis=1).astype(F32)

    def finish(self):
        for q in range(self.quarters):
            self.first(q).wait_send()
            self.second(q).wait_send()
            away, there, _ = self.third(q)
            pl.when(away)(there.wait_send)


def run(count, body, events):
    def step(j, carry):
        for when, things in events.items():

            @pl.when(j == when)
            def _():
                for thing in things:
                    thing()

        body(j)
        return carry

    lax.fori_loop(0, count, step, 0)


def split(refs, *counts):
    out, start = [], 0
    for count in counts:
        out.append(refs[start : start + count])
        start += count
    return out

ANY = pl.BlockSpec(memory_space=pl.ANY)
WHOLE = pl.BlockSpec(memory_space=pltpu.VMEM)


def comm(kernel, ins, outs, scratch, ident, name, moved):
    return pl.pallas_call(
        kernel,
        out_shape=[jax.ShapeDtypeStruct(shape, dtype) for shape, dtype, _ in outs],
        in_specs=[spec for _, spec in ins],
        out_specs=[spec for _, _, spec in outs],
        scratch_shapes=scratch,
        compiler_params=pltpu.CompilerParams(
            collective_id=ident, has_side_effects=True, vmem_limit_bytes=60 * 2**20
        ),
        cost_estimate=pl.CostEstimate(flops=0, bytes_accessed=moved, transcendentals=0),
        name=name,
    )(*[array for array, _ in ins])


def per_device(
    stream, norm_gain, w_in, conv_w, conv_b, w_xdt, w_xbc, w_dt, dt_bias, a_log, d_skip, w_out,
    cotangent, seg_ids, modality,
):
    seqs, chs = lax.axis_size("seq"), lax.axis_size("ch")
    s = lax.axis_index("seq")
    rows, cols = stream.shape
    tokens, width = seg_ids.shape[0], norm_gain.shape[0]
    channels = conv_b.shape[0]
    own = channels // seqs
    part = width // seqs
    flat = tokens * STATE // LANES
    dma, vmem = pltpu.SemaphoreType.DMA, pltpu.VMEM
    segs = seg_ids.reshape(tokens // LANES, LANES)
    gain = norm_gain[None]
    xdbl, u, conv, x_pre, d_y, dt, sig, _, d_gate, hs, normed, cot, inv, wx, wdt, mod, d_skip_own, own_rows, gathered = comm(
        partial(forward_kernel, seqs, chs),
        [
            (stream, ANY), (cotangent, ANY), (w_in, ANY), (w_out, ANY), (w_xdt, ANY), (w_dt, ANY),
            (modality[None], WHOLE), (segs, WHOLE), (gain, WHOLE), (w_xbc, WHOLE), (a_log, WHOLE),
            (d_skip[None], WHOLE), (conv_b[None], WHOLE), (conv_w, WHOLE), (dt_bias, WHOLE),
        ],
        [
            ((2, tokens // 2 + flat, LANES), F32, WHOLE),
            ((tokens, own), BF16, WHOLE),
            ((tokens, own), F32, WHOLE),
            ((tokens, own), BF16, WHOLE),
            ((tokens, own), F32, WHOLE),
            ((tokens, own), F32, WHOLE),
            ((tokens, own), F32, WHOLE),
            ((tokens, own), BF16, WHOLE),
            ((tokens, own), BF16, WHOLE),
            ((tokens + 1, STATE, own), F32, ANY),
            ((tokens, part), BF16, WHOLE),
            ((tokens, part), BF16, ANY),
            ((tokens, LANES), F32, WHOLE),
            ((2, RANK, own), BF16, WHOLE),
            ((2, RANK, own), BF16, WHOLE),
            ((seqs, 8, rows), F32, WHOLE),
            ((1, own), F32, WHOLE),
            ((STATE + 8, own), F32, WHOLE),
            ((seqs, tokens, own), BF16, ANY),
        ],
        2 * Total.scratch(seqs, tokens // 2 + flat) + 2 * Spread.semaphores(seqs) + 5 * Trade.semaphores(seqs)
        + Share.semaphores(seqs, CUTS)
        + [
            vmem((seqs * chs, rows, cols), BF16), vmem((seqs * chs, rows, cols), BF16),
            vmem((2, 2, width, own), BF16), vmem((2, own, width), BF16),
            vmem((tokens, own), F32), vmem((tokens, own), F32), vmem((ROWS + 8, own), F32), vmem((ROWS, width), BF16),
            vmem((STATE, own), F32), vmem((CHUNK, own), F32), vmem((CHUNK, STATE, own), F32),
            vmem((2, CHUNK, STATE, own), F32), vmem((8, rows), F32), vmem((2, tokens // 2 + flat, LANES), F32),
            dma((3 + seqs,)),
        ],
        1, "forward", 64 << 20,
    )
    output, grad_stream, sums, own_w_in, own_w_out, small, parts = comm(
        partial(backward_kernel, seqs, chs),
        [
            (segs, WHOLE), (xdbl, WHOLE), (u, WHOLE), (conv, ANY), (x_pre, ANY), (d_y, WHOLE), (dt, WHOLE),
            (sig, WHOLE), (gathered, ANY), (d_gate, WHOLE), (hs, ANY), (normed, ANY), (cot, ANY), (inv, ANY),
            (wx, WHOLE), (wdt, WHOLE), (mod, WHOLE), (d_skip_own, WHOLE), (w_xbc, WHOLE), (own_rows, WHOLE),
            (w_in, ANY), (w_out, ANY), (gain, WHOLE), (stream, WHOLE), (cotangent, WHOLE),
        ],
        [
            ((rows, cols), BF16, WHOLE),
            ((rows, cols), F32, WHOLE),
            ((chs, 8, cols), F32, WHOLE),
            (w_in.shape, F32, ANY),
            (w_out.shape, F32, ANY),
            ((96, channels), F32, WHOLE),
            ((2, 2, RANK // seqs, channels), F32, ANY),
        ],
        2 * Total.scratch(seqs, tokens // 2 + flat) + 2 * Regroup.scratch(seqs, chs, tokens, part)
        + 2 * Share.semaphores(seqs, CUTS) + Share.semaphores(seqs, 1) + Trade.semaphores(seqs)
        + [
            vmem((2, tokens // 2 + flat, LANES), F32), vmem((tokens, own), F32), vmem((tokens, own), BF16),
            vmem((seqs, tokens, own), BF16), vmem((seqs, tokens, own), BF16), vmem((seqs, tokens, own), BF16),
            vmem((tokens, own), F32), vmem((tokens, own), BF16), vmem((tokens, part), BF16), vmem((tokens, part), BF16),
            vmem(w_in.shape, BF16), vmem(w_out.shape, BF16), vmem((rows, LANES), F32),
            vmem((tokens, part), F32), vmem((tokens, part), F32), vmem((2, CHUNK + 1, STATE, own), F32),
            vmem((STATE, own), F32), vmem((STATE, own), F32), vmem((CHUNK, own), F32), vmem((CHUNK, STATE, own), F32),
            vmem((CHUNK, STATE, own), BF16), vmem((CHUNK, STATE, own), BF16),
            vmem((ROWS + 8, own), F32), vmem((ROWS + 8, own), F32), vmem((2, 2, RANK, own), F32),
            vmem((2, 2 * STATE, own), F32), vmem((2, own), F32), vmem((8, own), F32),
            vmem((96, own), F32), vmem((seqs, 96, own), F32), vmem((8, rows), F32), vmem((chs - 1, 8, rows), F32),
            vmem((8, cols), F32), vmem((seqs - 1, 8, cols), F32),
            dma((2,)), dma((8,)), dma((chs - 1,)), dma((chs - 1,)), dma((seqs - 1,)), dma((seqs - 1,)),
            dma((chs - 1,)), dma((chs - 1,)), vmem(w_in.shape, F32), vmem(w_out.shape, F32),
            vmem((2, tokens // 2 + flat, LANES), F32), dma((3,)),
        ],
        2, "backward", 64 << 20,
    )
    shapes = [
        (1, width), conv_w.shape, (1, channels), parts.shape[1:], w_xbc.shape, parts.shape[1:], dt_bias.shape,
        a_log.shape, (1, channels), (1, 3),
    ]
    steps = 8

    def whole(shape):
        zeros = (0,) * len(shape)
        return pl.BlockSpec(shape, lambda i: zeros)

    def sliced(shape, axis):
        block = tuple(size // steps if n == axis else size for n, size in enumerate(shape))
        return pl.BlockSpec(block, lambda i: tuple(i if n == axis else 0 for n in range(len(shape))))

    large = [(output, 0), (grad_stream, 0), (own_w_in, 2), (own_w_out, 1)]
    (
        g_gain, g_conv_w, g_conv_b, g_w_xdt, g_w_xbc, g_w_dt, g_bias, g_a_log, g_skip, stats,
        output, grad_stream, own_w_in, own_w_out,
    ) = pl.pallas_call(
        unpack_kernel,
        out_shape=[jax.ShapeDtypeStruct(shape, F32) for shape in shapes]
        + [jax.ShapeDtypeStruct(array.shape, array.dtype) for array, _ in large],
        grid=(steps,),
        in_specs=[whole(array.shape) for array in (small, sums, parts)]
        + [sliced(array.shape, axis) for array, axis in large],
        out_specs=[whole(shape) for shape in shapes] + [sliced(array.shape, axis) for array, axis in large],
        compiler_params=pltpu.CompilerParams(dimension_semantics=("arbitrary",), vmem_limit_bytes=60 * 2**20),
        name="unpack",
    )(small, sums, parts, *[array for array, _ in large])
    return (
        output, grad_stream, g_gain[0], own_w_in, g_conv_w, g_conv_b[0], g_w_xdt, g_w_xbc, g_w_dt, g_bias,
        g_a_log, g_skip[0], own_w_out, stats[0],
    )


def per_device_by_token(
    stream,
    norm_gain,
    w_in,
    conv_w,
    conv_b,
    w_xdt,
    w_xbc,
    w_dt,
    dt_bias,
    a_log,
    d_skip,
    w_out,
    cotangent,
    seg_ids,
    modality,
):
    length = stream.shape[0]
    channels = conv_b.shape[0]
    model_width = norm_gain.shape[0]
    mod_count = w_in.shape[0]
    rim_len = CONV - 1
    ch_start = lax.axis_index("ch") * channels
    col_start = lax.axis_index("ch") * stream.shape[1]
    x_full, grad_full = (
        lax.all_gather(stream, "ch", axis=1, tiled=True),
        lax.all_gather(cotangent, "ch", axis=1, tiled=True),
    )
    w_in_full, w_xdt_full, w_dt_full, w_out_full = (
        lax.all_gather(w_in, "seq", axis=2, tiled=True),
        lax.all_gather(w_xdt, "seq", axis=1, tiled=True),
        lax.all_gather(w_dt, "seq", axis=1, tiled=True),
        lax.all_gather(w_out, "seq", axis=2, tiled=True),
    )
    mod_mask = modality[None, :] == jnp.arange(mod_count, dtype=jnp.int32)[:, None]
    mod_float = mod_mask.astype(jnp.float32)

    def by_mod(value):
        chosen = mod_mask.reshape(mod_mask.shape + (1,) * (value.ndim - 1))
        return jnp.where(chosen, value[None], jnp.zeros((), value.dtype))

    stream_f = x_full.astype(jnp.float32)
    inv_rms = lax.rsqrt(jnp.mean(stream_f * stream_f, axis=1, keepdims=True) + EPSILON)
    x_hat = stream_f * inv_rms
    normed = (x_hat * norm_gain[None, :]).astype(jnp.bfloat16)
    normed_split = by_mod(normed)
    projected = jnp.einsum(
        "mtd,mkde->tke", normed_split, w_in_full, preferred_element_type=jnp.float32
    )
    x_pre = projected[:, 0].astype(jnp.bfloat16)
    gate_in = projected[:, 1]
    rim_rows = passed_along(x_pre[length - rim_len :], "seq", 1)
    padded_seg = jnp.concatenate([jnp.full((rim_len,), -1, jnp.int32), seg_ids])
    seg_win = lax.dynamic_slice_in_dim(padded_seg, lax.axis_index("seq") * length, length + rim_len)
    seg_now = seg_win[rim_len:]
    extended = jnp.concatenate([rim_rows, x_pre], 0).astype(jnp.float32)
    tap_mask = [
        (seg_win[offset : offset + length] == seg_now).astype(jnp.float32)[:, None]
        for offset in range(CONV)
    ]
    conv_out = conv_b[None, :] + sum(
        (
            conv_w[offset][None, :] * extended[offset : offset + length] * tap_mask[offset]
            for offset in range(CONV)
        )
    )
    u_val = (conv_out * jax.nn.sigmoid(conv_out)).astype(jnp.bfloat16)
    u_split = by_mod(u_val)
    dt_part = jnp.einsum("mte,mre->tr", u_split, w_xdt_full, preferred_element_type=jnp.float32)
    bc_part = jnp.einsum("mte,mne->tn", u_split, w_xbc, preferred_element_type=jnp.float32)
    dt_sum, bc_sum = lax.psum((dt_part, bc_part), "ch")
    dt_low = dt_sum.astype(jnp.bfloat16)
    b_in = bc_sum[:, :STATE]
    c_out = bc_sum[:, STATE:]
    low_split = by_mod(dt_low)
    dt_raw = jnp.einsum(
        "mtr,mre->te", low_split, w_dt_full, preferred_element_type=jnp.float32
    ) + jnp.dot(mod_float.T, dt_bias, precision=PRECISE)
    dt_val = jax.nn.softplus(dt_raw)
    u_float = u_val.astype(jnp.float32)
    dt_u = dt_val * u_float
    neg_a = -jnp.exp(a_log)
    keep_mask = (seg_now == seg_win[rim_len - 1 : rim_len - 1 + length]).astype(jnp.float32)
    decay_all = jnp.exp(neg_a * jnp.sum(dt_val, axis=0)[None, :]) * jnp.prod(keep_mask)
    zero_state = jnp.zeros_like(neg_a)
    local_end, _, _ = run_forward(zero_state, dt_val, dt_u, b_in, c_out, keep_mask, neg_a)
    _, start_state = entering(
        (decay_all, local_end), "seq", chain_link, (jnp.ones_like(neg_a), zero_state), False
    )
    _, starts, y_ssm = run_forward(start_state, dt_val, dt_u, b_in, c_out, keep_mask, neg_a)
    y_val = y_ssm + d_skip[None, :] * u_float
    sig_gate = jax.nn.sigmoid(gate_in)
    gated = (y_val * (gate_in * sig_gate)).astype(jnp.bfloat16)
    gated_split = by_mod(gated)
    branch = lax.psum_scatter(
        jnp.einsum("mte,med->dt", gated_split, w_out_full, preferred_element_type=jnp.float32),
        "ch",
        scatter_dimension=0,
        tiled=True,
    ).T
    x_own = stream.astype(jnp.float32)
    mixed = x_own + branch
    output = mixed.astype(jnp.bfloat16)
    stats_part = jnp.stack(
        [jnp.sum(x_own * x_own), jnp.sum(branch * branch), jnp.sum(mixed * mixed)]
    )
    grad_split = by_mod(grad_full)
    d_gated = jnp.einsum("mtd,med->te", grad_split, w_out_full, preferred_element_type=jnp.float32)
    d_w_out = jnp.einsum("mte,td->med", gated_split, grad_full, preferred_element_type=jnp.float32)
    d_y = d_gated * gate_in * sig_gate
    d_gate = d_gated * y_val * silu_grad(gate_in)
    d_skip_part = jnp.sum(d_y * u_float, axis=0)
    local_back = local_adjoint(dt_val, c_out, keep_mask, d_y, neg_a)
    _, incoming = entering(
        (decay_all, local_back), "seq", chain_link, (jnp.ones_like(neg_a), zero_state), True
    )
    d_neg, d_dt_ssm, d_dtu, d_b, d_c = run_adjoint(
        incoming, starts, dt_val, dt_u, b_in, c_out, keep_mask, d_y, neg_a
    )
    d_a_log = d_neg * neg_a
    d_dt = d_dt_ssm + d_dtu * u_float
    d_u = d_y * d_skip[None, :] + d_dtu * dt_val
    d_raw = (d_dt * jax.nn.sigmoid(dt_raw)).astype(jnp.bfloat16)
    d_w_dt = jnp.einsum("mtr,te->mre", low_split, d_raw, preferred_element_type=jnp.float32)
    d_dt_bias = jnp.dot(mod_float, d_raw.astype(jnp.float32), precision=PRECISE)
    d_low_part = jnp.einsum(
        "mte,mre->tr", by_mod(d_raw), w_dt_full, preferred_element_type=jnp.float32
    )
    d_bc_part = jnp.concatenate([d_b, d_c], 1)
    d_low_sum, d_bc_sum = lax.psum((d_low_part, d_bc_part), "ch")
    d_low = d_low_sum.astype(jnp.bfloat16)
    d_bc = d_bc_sum.astype(jnp.bfloat16)
    d_w_xdt = jnp.einsum("mte,tr->mre", u_split, d_low, preferred_element_type=jnp.float32)
    d_w_xbc = jnp.einsum("mte,tn->mne", u_split, d_bc, preferred_element_type=jnp.float32)
    d_u = d_u + jnp.einsum(
        "mtr,mre->te", by_mod(d_low), w_xdt_full, preferred_element_type=jnp.float32
    )
    d_u = d_u + jnp.einsum("mtn,mne->te", by_mod(d_bc), w_xbc, preferred_element_type=jnp.float32)
    d_conv = d_u * silu_grad(conv_out)
    d_conv_b = jnp.sum(d_conv, axis=0)
    d_conv_w = jnp.stack(
        [
            jnp.sum(d_conv * extended[offset : offset + length] * tap_mask[offset], axis=0)
            for offset in range(CONV)
        ]
    )
    d_ext = sum(
        (
            jnp.pad(
                conv_w[offset][None, :] * d_conv * tap_mask[offset],
                ((offset, rim_len - offset), (0, 0)),
            )
            for offset in range(CONV)
        )
    )
    back_rim = passed_along(d_ext[:rim_len], "seq", -1)
    d_pre = d_ext[rim_len:] + jnp.pad(back_rim, ((length - rim_len, 0), (0, 0)))
    d_xz = jnp.stack([d_pre, d_gate], 1).astype(jnp.bfloat16)
    d_w_in = jnp.einsum("mtd,tke->mkde", normed_split, d_xz, preferred_element_type=jnp.float32)
    d_norm_part = jnp.einsum(
        "mtke,mkde->dt", by_mod(d_xz), w_in_full, preferred_element_type=jnp.float32
    )
    d_gain_part = jnp.einsum("dt,td->d", d_norm_part, x_hat, precision=PRECISE)
    d_norm = lax.psum(d_norm_part, "ch").T
    d_hat = d_norm * norm_gain[None, :]
    inner_dot = jnp.mean(d_hat * x_hat, axis=1, keepdims=True)
    d_x_full = inv_rms * (d_hat - x_hat * inner_dot)
    grad_stream = lax.dynamic_slice_in_dim(
        d_x_full, col_start, stream.shape[1], 1
    ) + cotangent.astype(jnp.float32)
    own_w_in, own_w_xdt, own_w_dt, own_w_out = (
        lax.psum_scatter(d_w_in, "seq", scatter_dimension=2, tiled=True),
        lax.psum_scatter(d_w_xdt, "seq", scatter_dimension=1, tiled=True),
        lax.psum_scatter(d_w_dt, "seq", scatter_dimension=1, tiled=True),
        lax.psum_scatter(d_w_out, "seq", scatter_dimension=2, tiled=True),
    )

    def spread(value):
        full_shape = value.shape[:-1] + (INNER,)
        return lax.dynamic_update_slice_in_dim(
            jnp.zeros(full_shape, jnp.float32), value, ch_start, value.ndim - 1
        )

    def own_slice(value):
        return lax.dynamic_slice_in_dim(value, ch_start, channels, value.ndim - 1)

    summed = lax.psum(
        (
            spread(d_conv_w),
            spread(d_conv_b),
            spread(d_w_xbc),
            spread(d_dt_bias),
            spread(d_a_log),
            spread(d_skip_part),
            d_gain_part,
            stats_part,
        ),
        ("seq", "ch"),
    )
    stats = jnp.sqrt(summed[7] / float(length * lax.axis_size("seq") * model_width))
    return (
        output,
        grad_stream,
        summed[6],
        own_w_in,
        own_slice(summed[0]),
        own_slice(summed[1]),
        own_w_xdt,
        own_slice(summed[2]),
        own_w_dt,
        own_slice(summed[3]),
        own_slice(summed[4]),
        own_slice(summed[5]),
        own_w_out,
        stats,
    )


def solution(mesh):
    in_specs = (
        P("seq", "ch"),
        P(),
        P(None, None, "seq", "ch"),
        P(None, "ch"),
        P("ch"),
        P(None, "seq", "ch"),
        P(None, None, "ch"),
        P(None, "seq", "ch"),
        P(None, "ch"),
        P(None, "ch"),
        P("ch"),
        P(None, "ch", "seq"),
        P("seq", "ch"),
        P(),
        P("seq"),
    )
    out_specs = (
        P("seq", "ch"),
        P("seq", "ch"),
        P(),
        P(None, None, "seq", "ch"),
        P(None, "ch"),
        P("ch"),
        P(None, "seq", "ch"),
        P(None, None, "ch"),
        P(None, "seq", "ch"),
        P(None, "ch"),
        P(None, "ch"),
        P("ch"),
        P(None, "ch", "seq"),
        P(),
    )
    seqs, chs = mesh.shape["seq"], mesh.shape["ch"]
    whole_lanes = INNER == seqs * chs * LANES and seqs == 2 * chs and chs == 4
    return jax.shard_map(
        per_device if whole_lanes else per_device_by_token, mesh=mesh, in_specs=in_specs, out_specs=out_specs, check_vma=False
    )
```

```python
from functools import partial

import jax
import jax.numpy as jnp
from jax import lax
from jax.experimental import pallas as pl
from jax.experimental.pallas import tpu as pltpu
from jax.sharding import PartitionSpec as P

INNER = 4096
STATE = 16
CONV = 4
BLK = 64
RANK = 128


EPSILON = 1e-05
PRECISE = lax.Precision.HIGHEST


def passed_along(value, axis, steps):
    count = lax.axis_size(axis)
    initial, last = (max(0, -steps), min(count, count - steps))
    return lax.ppermute(value, axis, [(source, source + steps) for source in range(initial, last)])


def entering(part, axis, combine, identity, reverse):
    count = lax.axis_size(axis)
    place = lax.axis_index(axis)
    ahead = count - 1 - place if reverse else place
    gathered = jax.tree.map(lambda a: lax.all_gather(a, axis), part)
    state = jax.tree.map(lambda a, e: jnp.zeros_like(a) + jnp.asarray(e, a.dtype), part, identity)

    def one(step, state):
        source = count - 1 - step if reverse else step
        return combine(
            state, jax.tree.map(lambda a: lax.dynamic_index_in_dim(a, source, 0, False), gathered)
        )

    return lax.fori_loop(0, ahead, one, state)


def silu_grad(value):
    sigma = jax.nn.sigmoid(value)
    return sigma * (1.0 + value * (1.0 - sigma))


def chain_link(earlier, latter):
    return (earlier[0] * latter[0], latter[0] * earlier[1] + latter[1])


def decay_terms(dt_blk, keep_blk, neg_a):
    return keep_blk[:, None, None] * jnp.exp(dt_blk[:, None, :] * neg_a[None])


def drive_terms(b_blk, dtu_blk):
    return b_blk[:, :, None] * dtu_blk[:, None, :]


def to_blocks(values):
    block_count = values[0].shape[0] // BLK
    return tuple((value.reshape((block_count, BLK) + value.shape[1:]) for value in values))


def run_forward(state_in, dt_val, dt_u, b_in, c_out, keep_mask, neg_a):

    def block_step(state_now, blk_rows):
        dt_blk, dtu_blk, b_blk, c_blk, keep_blk = blk_rows
        cum_a, cum_b = lax.associative_scan(
            chain_link, (decay_terms(dt_blk, keep_blk, neg_a), drive_terms(b_blk, dtu_blk))
        )
        states = cum_a * state_now[None] + cum_b
        y_blk = jnp.einsum("tn,tne->te", c_blk, states, precision=PRECISE)
        return (states[-1], (state_now, y_blk))

    state_end, (starts, y_ssm) = lax.scan(
        block_step, state_in, to_blocks((dt_val, dt_u, b_in, c_out, keep_mask))
    )
    return (state_end, starts, y_ssm.reshape(dt_val.shape))


def adjoint_states(decay, c_blk, dy_blk, incoming):
    source = c_blk[:, :, None] * dy_blk[:, None, :]
    shifted = jnp.concatenate([decay[1:], jnp.ones_like(decay[:1])], 0)
    prod_a, acc_g = lax.associative_scan(chain_link, (shifted, source), reverse=True)
    return prod_a * incoming[None] + acc_g


def local_adjoint(dt_val, c_out, keep_mask, d_y, neg_a):

    def block_step(incoming, blk_rows):
        dt_blk, c_blk, keep_blk, dy_blk = blk_rows
        decay = decay_terms(dt_blk, keep_blk, neg_a)
        adjoint = adjoint_states(decay, c_blk, dy_blk, incoming)
        return (decay[0] * adjoint[0], None)

    outgoing, _ = lax.scan(
        block_step, jnp.zeros_like(neg_a), to_blocks((dt_val, c_out, keep_mask, d_y)), reverse=True
    )
    return outgoing


def run_adjoint(incoming, starts, dt_val, dt_u, b_in, c_out, keep_mask, d_y, neg_a):

    def block_step(carried, blk_rows):
        later_in, d_neg = carried
        state_in, dt_blk, dtu_blk, b_blk, c_blk, keep_blk, dy_blk = blk_rows
        decay = decay_terms(dt_blk, keep_blk, neg_a)
        adjoint = adjoint_states(decay, c_blk, dy_blk, later_in)
        cum_a, cum_b = lax.associative_scan(chain_link, (decay, drive_terms(b_blk, dtu_blk)))
        states = cum_a * state_in[None] + cum_b
        before = jnp.concatenate([state_in[None], states[:-1]], 0)
        flow = adjoint * before * decay
        d_dt_blk = jnp.sum(flow * neg_a[None], axis=1)
        d_neg = d_neg + jnp.einsum("tne,te->ne", flow, dt_blk, precision=PRECISE)
        d_dtu_blk = jnp.einsum("tne,tn->te", adjoint, b_blk, precision=PRECISE)
        d_b_blk = jnp.einsum("tne,te->tn", adjoint, dtu_blk, precision=PRECISE)
        d_c_blk = jnp.einsum("tne,te->tn", states, dy_blk, precision=PRECISE)
        return ((decay[0] * adjoint[0], d_neg), (d_dt_blk, d_dtu_blk, d_b_blk, d_c_blk))

    blk_rows = (starts,) + to_blocks((dt_val, dt_u, b_in, c_out, keep_mask, d_y))
    (_, d_neg), outs = lax.scan(
        block_step, (incoming, jnp.zeros_like(neg_a)), blk_rows, reverse=True
    )
    length = dt_val.shape[0]
    return (d_neg,) + tuple((value.reshape((length,) + value.shape[2:]) for value in outs))


F32 = jnp.float32
BF16 = jnp.bfloat16
LANES = 128
ROWS = 256
CHUNK = 128
GROUP = 16
LOG2E = 1.4426950408889634
CUT = 1e4
CUTS = 8
LATE = 4
SKIP, CONV_B, CONV_W, BIAS = STATE, STATE + 1, STATE + 2, STATE + 2 + CONV


def dot(a, b, da, db):
    return lax.dot_general(a, b, (((da,), (db,)), ((), ())), preferred_element_type=F32)


def column(row):
    return jnp.transpose(jnp.broadcast_to(row, (LANES, row.shape[1])))


def silu_slope(value, sigma):
    return sigma * (1.0 + value * (1.0 - sigma))


def flat_mask(rows):
    t = lax.broadcasted_iota(jnp.int32, (rows, LANES), 0)
    lane = lax.broadcasted_iota(jnp.int32, (rows, LANES), 1)
    return lax.rem(t, 8) == lane // STATE


def two_parts(value):
    high = value.astype(BF16).astype(F32)
    return high, value - high


def stacked(value):
    return jnp.concatenate(two_parts(value), axis=0).astype(BF16)


def outer(flat, value, out):
    mask = flat_mask(8)
    for r in range(CHUNK // 8):
        bh, bl = two_parts(jnp.where(mask, flat[r : r + 1], 0.0))
        vh, vl = two_parts(value[8 * r : 8 * r + 8])
        left = jnp.concatenate([bh, bh, bl, bl], axis=0).astype(BF16)
        right = jnp.concatenate([vh, vl, vh, vl], axis=0).astype(BF16)
        out[8 * r : 8 * r + 8] = dot(left, right, 0, 0).reshape(8, STATE, LANES)


def block_at(i, size):
    return pl.ds(pl.multiple_of(i * size, size), size)


def token_at(i, size):
    return i * size + lax.broadcasted_iota(jnp.int32, (size, LANES), 0)


def decay_step(i, bound, dt):
    t = token_at(i, CHUNK)
    return jnp.where((t == 0) | (t == bound), CUT, dt)


class Front:
    def __init__(self, bound, x_all, gain, wi, rows, wx, wbc, mod, own, outs, scratch):
        self.bound, self.x_all, self.gain, self.wi, self.rows, self.wx, self.wbc = bound, x_all, gain, wi, rows, wx, wbc
        self.mod, self.own = mod, own
        self.normed, self.inv, self.xpre, self.conv, self.u, self.gate = outs
        self.ext, self.wide = scratch
        self.ext[0:8] = jnp.zeros((8, LANES), F32)

    def block(self, at, i):
        chs, part = at.chs, self.normed.shape[1]
        tokens = self.u.shape[0]
        span = block_at(i, ROWS)
        x = jnp.concatenate([self.x_all[i * chs + c] for c in range(chs)], axis=1).astype(F32)
        inv = lax.rsqrt(jnp.mean(x * x, axis=1, keepdims=True) + EPSILON)
        normed = (x * inv * self.gain[...]).astype(BF16)
        self.inv[span] = jnp.broadcast_to(inv, (ROWS, LANES))
        self.wide[...] = normed
        self.normed[span] = self.wide[:, lanes_at(at.s, part)]
        image = column(self.mod[i, 0:1]) > 0.5
        both = [dot(normed, jnp.concatenate([self.wi[m, 0], self.wi[m, 1]], axis=1), 1, 0) for m in range(2)]
        x_pre = jnp.where(image, both[1][:, :LANES], both[0][:, :LANES]).astype(BF16)
        self.gate[span] = jnp.where(image, both[1][:, LANES:], both[0][:, LANES:])
        self.xpre[span] = x_pre
        ext = self.ext
        ext[8:] = x_pre.astype(F32)
        t = token_at(i, ROWS)
        conv = None
        for j in range(CONV):
            lag = CONV - 1 - j
            term = self.rows[CONV_W + j : CONV_W + j + 1] * ext[8 - lag : 8 - lag + ROWS]
            if lag:
                term = jnp.where((t < lag) | ((t >= self.bound) & (t - lag < self.bound)), 0.0, term)
            conv = term if conv is None else conv + term
        conv = self.rows[CONV_B : CONV_B + 1] + conv
        self.conv[span] = conv
        ext[0:8] = ext[ROWS : ROWS + 8]
        u = (conv * jax.nn.sigmoid(conv)).astype(BF16)
        self.u[span] = u
        fold = tokens // 2 // ROWS
        part_of, place_in = i // fold, lax.rem(i, fold)
        self.own[part_of, block_at(place_in, ROWS)] = jnp.where(image, dot(u, self.wx[1], 1, 1), dot(u, self.wx[0], 1, 1))
        mask = flat_mask(ROWS)
        few = ROWS // 8
        for n in range(2):
            tiled = [
                jnp.concatenate([self.wbc[m, n * STATE : (n + 1) * STATE, lanes_at(at.s, LANES)]] * 8, axis=0)
                for m in range(2)
            ]
            wide = jnp.where(mask, jnp.where(image, dot(u, tiled[1], 1, 1), dot(u, tiled[0], 1, 1)), 0.0)
            start = pl.multiple_of(tokens // 2 + n * (tokens // 16) + place_in * few, few)
            self.own[part_of, pl.ds(start, few)] = jnp.sum(wide.reshape(few, 8, LANES), axis=1)


def waves(share, order, *numbers):
    def go():
        for d in numbers:
            for n in range(share.at.depth - 1):
                if 0 <= d - n < len(order):
                    share.serve(order[d - n], n)

    return go


def first_of_second(seg_ref):
    return jnp.sum(jnp.where(seg_ref[...] == 0, 1, 0))


def chunk_image(mod, i):
    fold = ROWS // CHUNK
    return column(mod[i // fold, 0:1, lanes_at(lax.rem(i, fold), CHUNK)]) > 0.5


def half_at(xdbl, i, size):
    tokens = xdbl.shape[1] // 5 * 4
    fold = tokens // size
    return tokens, i // fold, lax.rem(i, fold)


def flats_span(xdbl, i, n, size):
    tokens, half, place_in = half_at(xdbl, i, size)
    few = size // 8
    return half, pl.ds(pl.multiple_of(tokens + n * (tokens // 8) + place_in * few, few), few)


def low_span(xdbl, i, size):
    _, half, place_in = half_at(xdbl, i, size)
    return half, block_at(place_in, size)


def flats_at(xdbl, i, n):
    return xdbl[flats_span(xdbl, i, n, CHUNK)]


def forward_kernel(
    seqs, chs, x_ref, cot_ref, wi_ref, wo_ref, wx_ref, wdt_ref, mod_ref, seg_ref, gain_ref, wbc_ref,
    alog_ref, skip_ref, convb_ref, convw_ref, bias_ref,
    xdbl, u_all, conv_all, xpre_all, dy_all, dt_all, sig_all, gated_all, dgate_all, hs_out, normed_s, cot_s, inv_all,
    wx, wdt, mod, dskip, rows_ref, gathered, *rest,
):
    totals1, totals2, spread1, spread2, trades, shares, rest = split(rest, 9, 9, 3, 3, 15, 5, 15)
    x_all, cot_all, wi, wo, gate_all, y_all, ext, wide, h_s, dta_s, x_s, hbuf, mod_own, own_all, sems = rest
    at = Place(seqs, chs)
    bound = first_of_second(seg_ref)
    mod_own[...] = jnp.broadcast_to(mod_ref[...].astype(F32), mod_own.shape)
    mine = lanes_at(at.s, LANES)
    rows_ref[...] = jnp.concatenate(
        [alog_ref[:, mine], skip_ref[:, mine], convb_ref[:, mine], convw_ref[:, mine], bias_ref[:, mine]], axis=0
    )
    own, part, low = LANES, wi_ref.shape[2], wx_ref.shape[1]
    tokens = u_all.shape[0]
    sum1, sum2 = [Total(at, xdbl.at[n], own_all.at[n], *more) for n, more in enumerate((totals1, totals2))]
    stream = Spread(at, x_ref, x_all, *spread1)
    cot = Spread(at, cot_ref, cot_all, *spread2)
    lows = pl.ds(pl.multiple_of(at.s * low, 16), low)
    plans = [
        (lambda t: wi_ref.at[:, :, :, lanes_at(t, own)], wi.at[:, :, rows_at(at.s, part)]),
        (lambda t: wx_ref.at[:, :, lanes_at(t, own)], wx.at[:, lows]),
        (lambda t: mod_own, mod.at[at.s]),
        (lambda t: wdt_ref.at[:, :, lanes_at(t, own)], wdt.at[:, lows]),
        (lambda t: wo_ref.at[:, rows_at(t, own)], wo.at[:, :, lanes_at(at.s, part)]),
    ]
    trades = [Trade(at, src, dst, *trades[3 * n : 3 * n + 3]) for n, (src, dst) in enumerate(plans)]
    at.greet(at.others + [at.side, at.across])
    stream.post(0)
    stream.post(1)
    stream.post_near()
    for trade in trades[:4]:
        trade.start()
    for level in range(3):
        stream.relay(level)
    stream.finish()
    for trade in trades[:4]:
        trade.finish()
    front = Front(
        bound, x_all, gain_ref, wi, rows_ref, wx, wbc_ref, mod, own_all,
        (normed_s, inv_all, xpre_all, conv_all, u_all, gate_all), (ext, wide),
    )

    cot.post(0)
    cot.post_near()
    half = tokens // ROWS // 2
    events = {half + 1 + n: [partial(sum1.step, n)] for n in range(3)}
    events[half] = [partial(sum1.post, 0)]
    run(tokens // ROWS, partial(front.block, at), events)
    sum2.post(0)
    sum1.step(3)
    cot.post(1)
    sum2.step(0)
    sum1.step(4)
    sum2.step(1)
    sum1.step(5)
    sum2.step(2)
    sum1.step(6)
    cot.relay(0)
    sum2.step(3)
    trades[4].start()
    sum1.take(7)
    rate = -jnp.exp(rows_ref[0:STATE]) * LOG2E
    h_s[...] = jnp.zeros_like(h_s)
    first = pltpu.make_async_copy(h_s, hs_out.at[0], sems.at[2])
    first.start()
    first.wait()

    def out_copy(i, slot):
        start = i * CHUNK + 1
        return pltpu.make_async_copy(hbuf.at[slot], hs_out.at[pl.ds(start, CHUNK)], sems.at[slot])

    def scan_step(i):
        slot = lax.rem(i, 2)
        span = block_at(i, CHUNK)
        image = chunk_image(mod, i)
        low = xdbl[low_span(xdbl, i, CHUNK)].astype(BF16)
        raw = jnp.where(
            image,
            dot(low, wdt[1], 1, 0) + rows_ref[BIAS + 1 : BIAS + 2],
            dot(low, wdt[0], 1, 0) + rows_ref[BIAS : BIAS + 1],
        )
        dt = jnp.maximum(raw, 0.0) + jnp.log1p(jnp.exp(-jnp.abs(raw)))
        u = u_all[span].astype(F32)
        dt_all[span] = dt
        sig_all[span] = jax.nn.sigmoid(raw)
        dta_s[...] = decay_step(i, bound, dt)
        outer(flats_at(xdbl, i, 0), dt * u, x_s)

        @pl.when(i >= 2)
        def _():
            out_copy(i - 2, slot).wait()

        def group(g, h):
            base = pl.multiple_of(g * GROUP, GROUP)
            for k in range(GROUP):
                h = jnp.exp2(dta_s[pl.ds(base + k, 1)] * rate) * h + x_s[base + k]
                hbuf[slot, base + k] = h
            return h

        h_s[...] = lax.fori_loop(0, CHUNK // GROUP, group, h_s[...])
        out_copy(i, slot).start()
        c_all = flats_at(xdbl, i, 1)
        mask = flat_mask(8)
        parts = []
        for r in range(CHUNK // 8):
            left = stacked(jnp.where(mask, c_all[r : r + 1], 0.0))
            made = dot(left, hbuf[slot, 8 * r : 8 * r + 8].reshape(8 * STATE, LANES).astype(BF16), 1, 0)
            parts.append(made[0:8] + made[8:16])
        y = jnp.concatenate(parts, axis=0) + rows_ref[SKIP : SKIP + 1] * u
        y_all[span] = y
        gate = gate_all[span]
        gated_all[span] = (y * (gate * jax.nn.sigmoid(gate))).astype(BF16)

    chunks = tokens // CHUNK
    cuts = list(range(CUTS))
    gated = Share(at, gated_all, gathered, CUTS, cuts[-1:], *shares)
    gated_wave = partial(waves, gated, cuts)
    events = {j: [] for j in range(chunks)}
    for cut in cuts[:-1]:
        events[2 * cut + 2].append(partial(gated.post, cut))
    for d in range(LATE):
        events[2 * d + 15 - 2 * (LATE - 1)].append(gated_wave(d))
    for n in range(3):
        events[2 * n + 1].append(partial(sum2.step, 4 + n))
    events[7].append(partial(sum2.take, 7))
    events[2].append(partial(cot.relay, 1))
    events[6].append(partial(cot.relay, 2))
    run(chunks, scan_step, events)
    gated.post(cuts[-1])
    gated.home.start()
    cot.finish()
    trades[4].finish()
    folds = seqs // chs
    slices = []
    for n in range(seqs):
        src = cot_all.at[n * chs + at.s // folds, :, lanes_at(lax.rem(at.s, folds), part)]
        slices.append(pltpu.make_async_copy(src, cot_s.at[pl.ds(n * ROWS, ROWS)], sems.at[3 + n]))
        slices[-1].start()
    dskip[...] = jnp.zeros_like(dskip)

    def gate_step(i):
        span = block_at(i, ROWS)
        image = column(mod[i, 0:1]) > 0.5
        cots = jnp.concatenate([cot_all[i * chs + c] for c in range(chs)], axis=1)
        d_gated = jnp.where(image, dot(cots, wo[1], 1, 1), dot(cots, wo[0], 1, 1))
        gate = gate_all[span]
        sigma = jax.nn.sigmoid(gate)
        d_y = d_gated * gate * sigma
        dy_all[span] = d_y
        dgate_all[span] = (d_gated * y_all[span] * silu_slope(gate, sigma)).astype(BF16)
        dskip[...] += jnp.sum(d_y * u_all[span].astype(F32), axis=0, keepdims=True)

    run(tokens // ROWS, gate_step, {n: [gated_wave(LATE + n)] for n in range(10 - LATE)})
    for cut in cuts:
        gated.arrived(cut)
    gated.home.wait()
    gated.finish()
    for i in (chunks - 2, chunks - 1):
        out_copy(i, i % 2).wait()
    for copy in slices:
        copy.wait()
    sum1.finish()
    sum2.finish()


def adjoint_chunk(bound, i, state, xdbl, u_all, dy_all, dt_all, sig_all, mod, wdt, rows_ref, own, du_all, grads, scratch):
    ga_s, dn_s, dta_s, x_s, g_s, f_s = scratch
    dwdt, dbias = grads
    tokens = u_all.shape[0]
    span = block_at(i, CHUNK)
    dt = dt_all[span]
    u = u_all[span].astype(F32)
    d_y = dy_all[span]
    dta_s[...] = decay_step(i, bound, dt)
    neg_a = -jnp.exp(rows_ref[0:STATE])
    rate = neg_a * LOG2E
    outer(flats_at(xdbl, i, 1), d_y, x_s)
    start = pl.multiple_of(i * CHUNK, CHUNK)

    def group(step, carried):
        ga, dn = carried
        base = pl.multiple_of((CHUNK // GROUP - 1 - step) * GROUP, GROUP)
        for k in reversed(range(GROUP)):
            adjoint = x_s[base + k] + ga
            ga = jnp.exp2(dta_s[pl.ds(base + k, 1)] * rate) * adjoint
            slow = ga * state[base + k] * neg_a
            dn = dn + slow * dt_all[pl.ds(start + base + k, 1)]
            g_s[base + k] = adjoint.astype(BF16)
            f_s[base + k] = slow.astype(BF16)
        return ga, dn

    ga, dn = lax.fori_loop(0, CHUNK // GROUP, group, (ga_s[...], dn_s[...]))
    ga_s[...] = ga
    dn_s[...] = dn
    dtu = dt * u
    b_all = flats_at(xdbl, i, 0)
    mask = flat_mask(8)
    ones = jnp.where(flat_mask(16), 1.0, 0.0).astype(BF16)
    pu, pd, db, dc = [], [], [], []
    for r in range(CHUNK // 8):
        few = slice(8 * r, 8 * r + 8)
        adjoint = g_s[few].reshape(8 * STATE, LANES)
        slow = f_s[few].reshape(8 * STATE, LANES)
        h = state[8 * r + 1 : 8 * r + 9].reshape(8 * STATE, LANES).astype(BF16)
        made = dot(stacked(jnp.where(mask, b_all[r : r + 1], 0.0)), adjoint, 1, 0)
        pu.append(made[0:8] + made[8:16])
        pd.append(dot(ones, slow, 1, 0)[0:8])
        for out, value, other in ((db, dtu, adjoint), (dc, d_y, h)):
            made = dot(stacked(value[few]), other, 1, 1)
            out.append(jnp.sum(jnp.where(mask, made[0:8] + made[8:16], 0.0), axis=0, keepdims=True))
    d_dtu = jnp.concatenate(pu, axis=0)
    d_dt = jnp.concatenate(pd, axis=0) + d_dtu * u
    for n, part in enumerate((db, dc)):
        own[flats_span(own, i, n, CHUNK)] = jnp.concatenate(part, axis=0)
    du_all[span] = d_y * rows_ref[SKIP : SKIP + 1] + d_dtu * dt
    d_raw = (d_dt * sig_all[span]).astype(BF16)
    image = chunk_image(mod, i)
    low = xdbl[low_span(xdbl, i, CHUNK)].astype(BF16)
    own[low_span(own, i, CHUNK)] = jnp.where(image, dot(d_raw, wdt[1], 1, 1), dot(d_raw, wdt[0], 1, 1))
    raw_f = d_raw.astype(F32)
    for m in range(2):
        mine = jnp.where(image == (m == 1), raw_f, 0.0)
        dwdt[m] += dot(low, mine.astype(BF16), 0, 0)
        dbias[m : m + 1] += jnp.sum(mine, axis=0, keepdims=True)


def rear_block(bound, i, at, dx, du_all, u_all, conv_all, xpre_all, mod, wx, wbc, rows_ref, dpre_all, grads, scratch):
    dwx, dwbc, dconv = grads
    ext, ahead = scratch
    tokens = u_all.shape[0]
    span = block_at(i, ROWS)
    few = ROWS // 8
    image = column(mod[i, 0:1]) > 0.5
    low = dx[low_span(dx, i, ROWS)].astype(BF16)
    mask = flat_mask(ROWS)
    lane = lax.broadcasted_iota(jnp.int32, (LANES, 2 * STATE), 0)
    state = lax.broadcasted_iota(jnp.int32, (LANES, 2 * STATE), 1)
    d_bc = None
    for n in range(2):
        fold = jnp.where(lax.rem(lane, STATE) + n * STATE == state, 1.0, 0.0).astype(BF16)
        flat = dx[flats_span(dx, i, n, ROWS)]
        wide = jnp.broadcast_to(flat[:, None, :], (few, 8, LANES)).reshape(ROWS, LANES)
        part = dot(jnp.where(mask, wide, 0.0).astype(BF16), fold, 1, 0)
        d_bc = part if d_bc is None else d_bc + part
    d_bc = d_bc.astype(BF16)
    u = u_all[span]
    extra = [dot(low, wx[m], 1, 0) + dot(d_bc, wbc[m, :, lanes_at(at.s, LANES)], 1, 0) for m in range(2)]
    d_u = du_all[span] + jnp.where(image, extra[1], extra[0])
    u_f = u.astype(F32)
    for m in range(2):
        mine = jnp.where(image == (m == 1), u_f, 0.0).astype(BF16)
        dwx[m] += dot(low, mine, 0, 0)
        dwbc[m] += dot(d_bc, mine, 0, 0)
    conv = conv_all[span]
    d_conv = d_u * silu_slope(conv, jax.nn.sigmoid(conv))
    before = lax.rem(i * ROWS + tokens - 16, tokens)
    ext[0:8] = xpre_all[pl.ds(pl.multiple_of(before, 16), 16)].astype(F32)[8:16]
    ext[8:] = xpre_all[span].astype(F32)
    ahead[ROWS : ROWS + 8] = ahead[0:8]
    ahead[0:ROWS] = d_conv
    t = token_at(i, ROWS)
    d_pre = None
    for tap in range(CONV):
        lag = CONV - 1 - tap
        seen = ext[8 - lag : 8 - lag + ROWS] * d_conv
        term = rows_ref[CONV_W + tap : CONV_W + tap + 1] * ahead[lag : lag + ROWS]
        if lag:
            seen = jnp.where((t < lag) | ((t >= bound) & (t - lag < bound)), 0.0, seen)
            term = jnp.where((t < bound) & (t + lag >= bound), 0.0, term)
        dconv[tap : tap + 1] += jnp.sum(seen, axis=0, keepdims=True)
        d_pre = term if d_pre is None else d_pre + term
    dconv[CONV : CONV + 1] += jnp.sum(d_conv, axis=0, keepdims=True)
    dpre_all[span] = d_pre.astype(BF16)


def grown(image, width):
    return jnp.concatenate([image] * (width // LANES), axis=1)


def out_block(i, gated, cot_s, mod, wo, branch, dwo):
    span = block_at(i, ROWS)
    wide = jnp.concatenate([gated[n, span] for n in range(gated.shape[0])], axis=1)
    cot = cot_s[span].astype(F32)
    image = grown(column(mod[i, 0:1]) > 0.5, cot.shape[1])
    branch[span] = jnp.where(image, dot(wide, wo[1], 1, 0), dot(wide, wo[0], 1, 0))
    for m in range(2):
        dwo[m] += dot(wide, jnp.where(image == (m == 1), cot, 0.0).astype(BF16), 0, 0)


def in_block(i, k, first, dz_all, normed_s, mod, wi, d_norm, dwi):
    span = block_at(i, ROWS)
    dz = jnp.concatenate([dz_all[n, span] for n in range(dz_all.shape[0])], axis=1)
    normed = normed_s[span].astype(F32)
    image = grown(column(mod[i, 0:1]) > 0.5, normed.shape[1])
    total = jnp.where(image, dot(dz, wi[1, k], 1, 1), dot(dz, wi[0, k], 1, 1))
    d_norm[span] = total if first else d_norm[span] + total
    for m in range(2):
        dwi[m, k] += dot(jnp.where(image == (m == 1), normed, 0.0).astype(BF16), dz, 0, 0)


def backward_kernel(
    seqs, chs, seg_ref, xdbl, u_all, conv_hbm, xpre_hbm, dy_all, dt_all, sig_all, gated_hbm, dgate_own, hs,
    normed_hbm, cot_hbm, inv_hbm, wx, wdt, mod, dskip, wbc, rows_ref, wi_hbm, wo_hbm, gain_ref, x_ref, own_cot,
    out_ref, grad_ref, sums_ref, dwi_out, dwo_out, small_ref, parts_ref, *rest,
):
    totals1, totals2, branches, norms, shares, trades, rest = split(rest, 9, 9, 9, 9, 15, 3, len(rest) - 54)
    (
        dx, du_all, dpre_own, gated_all, dgate_all, dpre_all, conv_all, xpre_all, normed_s, cot_s, wi, wo, inv,
        branch, d_norm, hbuf, ga_s, dn_s, dta_s, x_s, g_s, f_s, ext, ahead, dwdx, dwbc, dbias, dconv,
        small_own, small_all, dots, r3, pay, r4, hsem, lsem, dsend, drecv, gsend, grecv, psend, precv, dwi, dwo, own_all, osem,
    ) = rest
    at = Place(seqs, chs)
    bound = first_of_second(seg_ref)
    tokens, own, rows = u_all.shape[0], LANES, x_ref.shape[0]
    chunks, blocks = tokens // CHUNK, tokens // ROWS

    def state_copy(i, slot):
        return pltpu.make_async_copy(hs.at[pl.ds(i * CHUNK, CHUNK + 1)], hbuf.at[slot], hsem.at[slot])

    state_copy(chunks - 1, 0).start()
    late = [
        (conv_hbm, conv_all), (xpre_hbm, xpre_all), (normed_hbm, normed_s), (cot_hbm, cot_s), (wi_hbm, wi),
        (wo_hbm, wo), (gated_hbm, gated_all), (inv_hbm.at[block_at(at.s, rows)], inv),
    ]
    late = [pltpu.make_async_copy(src, dst, lsem.at[n]) for n, (src, dst) in enumerate(late)]
    for copy in late:
        copy.start()
    sum1, sum2 = [Total(at, dx.at[n], own_all.at[n], *more) for n, more in enumerate((totals1, totals2))]
    ups, downs = list(range(CUTS)), list(reversed(range(CUTS)))
    d_gate = Share(at, dgate_own, dgate_all, CUTS, ups[-1:], *shares[0:5])
    d_pre = Share(at, dpre_own, dpre_all, CUTS, downs[-1:], *shares[5:10])
    small = Share(at, small_own, small_all, 1, [], *shares[10:15])

    wave = waves

    def post(share, *cuts):
        def go():
            for cut in cuts:
                share.post(cut)

        return go

    at.greet(at.mates + at.others + Regroup.sources(at))
    post(d_gate, *ups)()
    d_gate.home.start()
    for ref in (ga_s, dn_s, dwdx, dwbc, dbias, dconv, ahead, dwi, dwo):
        ref[...] = jnp.zeros_like(ref)

    def adjoint_step(j):
        i = chunks - 1 - j
        slot = lax.rem(j, 2)
        state_copy(i, slot).wait()

        @pl.when(j < chunks - 1)
        def _():
            state_copy(i - 1, 1 - slot).start()

        adjoint_chunk(
            bound, i, hbuf.at[slot], xdbl, u_all, dy_all, dt_all, sig_all, mod, wdt, rows_ref, own_all, du_all,
            (dwdx.at[1], dbias), (ga_s, dn_s, dta_s, x_s, g_s, f_s),
        )

    events = {j: [] for j in range(chunks)}
    for d in range(7):
        events[2 * d + 3].append(wave(d_gate, ups, d))
    half = chunks // 2
    events[half].append(partial(sum2.post, 0))
    for n, j in enumerate((half + 1, half + 3, half + 6)):
        events[j].append(partial(sum2.step, n))
    run(chunks, adjoint_step, events)
    sum1.post(0)
    for copy in late:
        copy.wait()
    branch_sum = Regroup(at, branch, *branches)
    norm_sum = Regroup(at, d_norm, *norms)

    def rear_step(j):
        rear_block(
            bound, blocks - 1 - j, at, dx, du_all, u_all, conv_all, xpre_all, mod, wx, wbc, rows_ref, dpre_own,
            (dwdx.at[0], dwbc, dconv), (ext, ahead),
        )
        d_pre.post(blocks - 1 - j)

    def rear_late(j):
        rear_step(blocks // 2 + j)

    def out_step(i):
        out_block(i, gated_all, cot_s, mod, wo, branch, dwo)

    def first_step(i):
        in_block(i, 1, True, dgate_all, normed_s, mod, wi, d_norm, dwi)

    quarters = blocks // 2

    def outs(q):
        run(2, lambda n: out_step(2 * q + n), {})
        branch_sum.one(q)

    sum2.step(3)
    sum1.step(0)
    wave(d_gate, ups, 7)()
    outs(0)
    sum2.step(4)
    sum1.step(1)
    outs(1)
    sum2.step(5)
    sum1.step(2)
    wave(d_gate, ups, 8)()
    outs(2)
    sum2.step(6)
    sum1.step(3)
    outs(3)
    sum2.take(7)
    run(blocks // 2, rear_step, {3: [partial(sum1.step, 4)]})
    sum1.step(5)
    wave(d_gate, ups, 9)()
    for q in range(quarters):
        branch_sum.two(q)
    sum1.step(6)
    wave(d_pre, downs, 0)()
    for cut in range(CUTS):
        d_gate.arrived(cut)
    d_gate.home.wait()
    run(blocks // 2, first_step, {2: [wave(d_pre, downs, 1)]})
    sum1.take(7)
    run(blocks // 2, rear_late, {0: [wave(d_pre, downs, 2)], 2: [wave(d_pre, downs, 3)]})
    d_pre.home.start()
    small_own[...] = jnp.concatenate(
        [dn_s[...], dconv[...], dbias[...], dskip[...], jnp.zeros((5, own), F32), dwbc[0], dwbc[1]], axis=0
    )
    low = parts_ref.shape[2]
    parts = Trade(
        at, lambda t: dwdx.at[:, :, rows_at(t, low)], parts_ref.at[:, :, :, lanes_at(at.s, own)], *trades
    )
    written = [pltpu.make_async_copy(dwo, dwo_out, osem.at[2])]
    for k in range(2):
        written.append(pltpu.make_async_copy(dwi.at[:, k], dwi_out.at[:, k], osem.at[k]))
    written[0].start()
    for q in range(quarters):
        branch_sum.three(q)
    run(blocks // 2, lambda j: first_step(blocks // 2 + j), {0: [wave(d_pre, downs, 4)], 2: [wave(d_pre, downs, 5)]})
    small.post(0)
    small.home.start()
    parts.start()
    written[2].start()
    d_pre.home.wait()

    def second_step(j):
        i = blocks - 1 - j
        in_block(i, 0, False, dpre_all, normed_s, mod, wi, d_norm, dwi)
        q = i // 2

        @pl.when(lax.rem(j, 2) == 1)
        def _():
            norm_sum.one(q)

        @pl.when((lax.rem(j, 2) == 0) & (j > 1))
        def _():
            norm_sum.two(q + 1)

        @pl.when((lax.rem(j, 2) == 1) & (j > 2))
        def _():
            norm_sum.three(q + 1)

    events = {j: [wave(d_pre, downs, j + 6), partial(d_pre.arrived, downs[j])] for j in range(blocks)}
    for n in range(3):
        events[2 * n + 1].append(partial(small.serve, 0, n))
    run(blocks, second_step, events)
    written[1].start()
    added = branch_sum.result()
    xs = x_ref[...].astype(F32)
    mixed = xs + added
    out_ref[...] = mixed.astype(BF16)
    norm_sum.two(0)
    norm_sum.three(0)
    inv_own = inv[...][:, 0:1]
    x_hat = xs * inv_own
    width = chs * x_ref.shape[1]
    gain = gain_ref[:, lanes_at(at.c, x_ref.shape[1])]
    total_norm = norm_sum.result()
    d_hat = total_norm * gain
    dot_part = jnp.sum(d_hat * x_hat, axis=1, keepdims=True)
    dots[...] = jnp.transpose(jnp.broadcast_to(dot_part, (rows, LANES)))[0:8]
    third = [remote(dots, r3.at[k], dsend.at[k], drecv.at[k], mate) for k, mate in enumerate(at.mates)]
    for copy in third:
        copy.start()
    rows_of = [total_norm * x_hat, xs * xs, added * added, mixed * mixed]
    pay[...] = jnp.concatenate(
        [jnp.sum(v, axis=0, keepdims=True) for v in rows_of] + [jnp.zeros((4, x_ref.shape[1]), F32)], axis=0
    )
    fourth = [remote(pay, r4.at[k], gsend.at[k], grecv.at[k], other) for k, other in enumerate(at.others)]
    for copy in fourth:
        copy.start()
    dot_sum = dots[...]
    for k, copy in enumerate(third):
        copy.wait_recv()
        dot_sum = dot_sum + r3[k]
    inner = column(dot_sum[0:1])[:, 0:1] / width
    grad_ref[...] = own_cot[...].astype(F32) + inv_own * (d_hat - x_hat * inner)
    joint = pay[...]
    for k, copy in enumerate(fourth):
        copy.wait_recv()
        joint = joint + r4[k]
    sums_ref[at.c] = joint
    spot = sums_ref.at[at.c]
    fifth = [remote(spot, spot, psend.at[k], precv.at[k], mate) for k, mate in enumerate(at.mates)]
    for copy in fifth:
        copy.start()
    for copy in fifth:
        copy.wait_recv()
    for copy in written:
        copy.wait()
    small.arrived(0)
    small.home.wait()
    parts.finish()
    for n in range(seqs):
        small_ref[:, n * own : (n + 1) * own] = small_all[n]
    for share in (d_gate, d_pre, small):
        share.finish()
    for copy in third + fourth + fifth:
        copy.wait_send()
    branch_sum.finish()
    norm_sum.finish()
    sum1.finish()
    sum2.finish()


def unpack_kernel(
    small_ref, sums_ref, parts_ref, in0, in1, in2, in3,
    gain, conv_w, conv_b, w_xdt, w_xbc, w_dt, bias, a_log, skip, stats, out0, out1, out2, out3,
):
    for src, dst in ((in0, out0), (in1, out1), (in2, out2), (in3, out3)):
        dst[...] = src[...]

    @pl.when(pl.program_id(0) == 0)
    def _():
        a_log[...] = small_ref[0:STATE]
        conv_w[...] = small_ref[STATE : STATE + CONV]
        conv_b[...] = small_ref[STATE + CONV : STATE + CONV + 1]
        bias[...] = small_ref[STATE + 8 : STATE + 10]
        skip[...] = small_ref[STATE + 10 : STATE + 11]
        for m in range(2):
            w_xbc[m] = small_ref[32 + 2 * STATE * m : 32 + 2 * STATE * (m + 1)]
        w_xdt[...] = parts_ref[0]
        w_dt[...] = parts_ref[1]
        cols = sums_ref.shape[2]
        total = sums_ref[0]
        for c in range(sums_ref.shape[0]):
            gain[:, c * cols : (c + 1) * cols] = sums_ref[c, 0:1]
            if c:
                total = total + sums_ref[c]
        size = float(gain.shape[1] * sums_ref.shape[0] * cols)
        mean = jnp.sum(total, axis=1, keepdims=True)[1:4] / size
        stats[...] = jnp.sqrt(jnp.transpose(jnp.broadcast_to(mean, (3, LANES)))[0:1, 0:3])

MESH = pl.DeviceIdType.MESH


def remote(src, dst, send, recv, peer):
    return pltpu.make_async_remote_copy(
        src_ref=src, dst_ref=dst, send_sem=send, recv_sem=recv,
        device_id={"seq": peer[0], "ch": peer[1]}, device_id_type=MESH,
    )


def rows_at(start, size):
    return pl.ds(pl.multiple_of(start * size, 8), size)


def lanes_at(start, size):
    return pl.ds(pl.multiple_of(start * size, LANES), size)


class Place:
    def __init__(self, seqs, chs):
        self.seqs, self.chs, self.depth = seqs, chs, seqs // 2
        self.s, self.c = lax.axis_index("seq"), lax.axis_index("ch")
        self.z, self.x = self.s // 2, lax.rem(self.s, 2)
        self.y, self.o = self.c // 2, lax.rem(self.c, 2)
        self.side = (self.s, self.y * 2 + 1 - self.o)
        self.across = (self.s, (1 - self.y) * 2 + self.o)
        self.beside = (self.z * 2 + 1 - self.x, self.c)
        self.deep = [(lax.rem(self.z + k, self.depth) * 2 + self.x, self.c) for k in range(1, self.depth)]
        self.others = [(lax.rem(self.s + k, seqs), self.c) for k in range(1, seqs)]
        self.mates = [(self.s, lax.rem(self.c + k, chs)) for k in range(1, chs)]

    def greet(self, peers):
        barrier = pltpu.get_barrier_semaphore()
        for seq, ch in peers:
            pl.semaphore_signal(barrier, inc=1, device_id={"seq": seq, "ch": ch}, device_id_type=MESH)
        pl.semaphore_wait(barrier, len(peers))


class Spread:
    ORDERS = ((0, 1, 2, 3), (0, 2, 1, 3))
    ORIGIN = (0, 0, 0, 0)

    @staticmethod
    def semaphores(seqs):
        dma = pltpu.SemaphoreType.DMA
        return [dma((2, 4 * seqs)), dma((2, 4 * seqs)), dma((1,))]

    def __init__(self, at, src, out, send, recv, local):
        self.at, self.src, self.out, self.send, self.recv = at, src, out, send, recv
        self.half = src.shape[0] // 2
        self.home = pltpu.make_async_copy(src, out.at[at.s * at.chs + at.c], local.at[0])

    def index(self, role):
        return ((role[0] * 2 + role[1]) * 2 + role[2]) * 2 + role[3]

    def piece(self, cut, role):
        at = self.at
        dz, dx, dy, do = role
        src = lax.rem(at.z + at.depth - dz, at.depth) * 2 + (1 - at.x if dx else at.x)
        col = (1 - at.y if dy else at.y) * 2 + (1 - at.o if do else at.o)
        return self.out.at[src * at.chs + col, pl.ds(cut * self.half, self.half)]

    def hop(self, cut, role, axis, step=1):
        at = self.at
        peer = (at.deep[step - 1], at.beside, at.across, at.side)[axis]
        src = self.piece(cut, role)
        if role == self.ORIGIN:
            src = self.src.at[pl.ds(cut * self.half, self.half)]
        index = self.index(tuple(step if i == axis else v for i, v in enumerate(role)))
        return remote(src, self.piece(cut, role), self.send.at[cut, index], self.recv.at[cut, index], peer)

    def roles(self, cut, level):
        order = self.ORDERS[cut]
        for step in range(self.at.depth):
            for extra in range(max(level, 1)):
                role = [step, 0, 0, 0]
                if level:
                    role[order[level]] = 1
                if extra:
                    role[order[1]] = 1
                if tuple(role) != self.ORIGIN:
                    yield tuple(role)

    def arrived(self, cut, role):
        spot, index = self.piece(cut, role), self.index(role)
        remote(spot, spot, self.send.at[cut, index], self.recv.at[cut, index], self.at.side).wait_recv()

    def post(self, cut):
        for step in range(1, self.at.depth):
            self.hop(cut, self.ORIGIN, 0, step).start()

    def post_near(self):
        for cut in range(2):
            for axis in self.ORDERS[cut][1:]:
                self.hop(cut, self.ORIGIN, axis).start()
        self.home.start()

    def relay(self, level):
        for cut in range(2):
            for role in self.roles(cut, level):
                self.arrived(cut, role)
                for axis in self.ORDERS[cut][level + 1 :]:
                    self.hop(cut, role, axis).start()

    def finish(self):
        for cut in range(2):
            for step in range(self.at.depth):
                for dx in range(2):
                    for dy in range(2):
                        self.arrived(cut, (step, dx, dy, 1))
        self.home.wait()
        for cut in range(2):
            order = self.ORDERS[cut]
            for step in range(1, self.at.depth):
                self.hop(cut, self.ORIGIN, 0, step).wait_send()
            for axis in order[1:]:
                self.hop(cut, self.ORIGIN, axis).wait_send()
            for level in range(3):
                for role in self.roles(cut, level):
                    for axis in order[level + 1 :]:
                        self.hop(cut, role, axis).wait_send()


class Trade:
    @staticmethod
    def semaphores(seqs):
        dma = pltpu.SemaphoreType.DMA
        return [dma((seqs - 1,)), dma((seqs - 1,)), dma((1,))]

    def __init__(self, at, src_for, dst, send, recv, local):
        self.copies = [
            remote(src_for(peer[0]), dst, send.at[k], recv.at[k], peer) for k, peer in enumerate(at.others)
        ]
        self.home = pltpu.make_async_copy(src_for(at.s), dst, local.at[0])

    def start(self):
        for copy in self.copies:
            copy.start()
        self.home.start()

    def finish(self):
        for copy in self.copies:
            copy.wait_recv()
        self.home.wait()
        for copy in self.copies:
            copy.wait_send()


class Share:
    @staticmethod
    def semaphores(seqs, cuts):
        dma, depth = pltpu.SemaphoreType.DMA, seqs // 2
        return [dma((cuts, 4, depth)), dma((cuts, 2, depth)), dma((cuts, depth)), dma((cuts, depth)), dma((1,))]

    def __init__(self, at, src, out, cuts, turned, send, recv, hop_s, hop_r, local, base=0, rows=None):
        self.at, self.src, self.out, self.cuts, self.turned = at, src, out, cuts, turned
        rows = rows or src.shape[0]
        self.size, self.base = rows // cuts, base
        self.z = (send, recv)
        self.x = (hop_s, hop_r)
        span = pl.ds(base, rows)
        self.home = pltpu.make_async_copy(src.at[span], out.at[at.s, span], local.at[0])
        first, last = (at.depth - 1 - at.z) // (at.depth - 1), at.z // (at.depth - 1)
        self.order = (1 + 2 * first, 3 - first - last, 2 - first + last)

    def piece(self, cut, side, r):
        at = self.at
        owner = lax.rem(at.z + at.depth - r, at.depth) * 2 + (1 - at.x if side else at.x)
        return self.out.at[owner, pl.ds(self.base + cut * self.size, self.size)]

    def origin(self, cut):
        return self.src.at[pl.ds(self.base + cut * self.size, self.size)]

    def along(self, cut, side, r, way):
        at = self.at
        own = isinstance(r, int) and r == 0
        if way == 0:
            there = at.z < at.depth - 1 if own else (at.z >= r) & (at.z < at.depth - 1)
            role, peer = r + 1, at.z + 1
        else:
            there = at.z > 0 if own else (at.z < r) & (at.z > 0)
            role, peer = (at.depth - 1 if own else r - 1), at.z - 1
        spot = self.piece(cut, side, r)
        src = self.origin(cut) if own and not side else spot
        copy = remote(
            src, spot, self.z[0].at[cut, 2 * side + way, r], self.z[1].at[cut, side, role], (peer * 2 + at.x, at.c)
        )
        return there, copy

    def pass_on(self, cut, side, r):
        for way in range(2):
            there, copy = self.along(cut, side, r, way)
            pl.when(there)(copy.start)

    def beside(self, cut, r):
        spot = self.piece(cut, 0, r)
        src = self.origin(cut) if isinstance(r, int) and r == 0 else spot
        return remote(src, spot, self.x[0].at[cut, r], self.x[1].at[cut, r], self.at.beside)

    def is_turned(self, cut):
        return cut in self.turned

    def post(self, cut):
        self.pass_on(cut, 0, 0)
        self.beside(cut, 0).start()

    def wait_z(self, cut, side, r):
        spot = self.piece(cut, side, r)
        remote(spot, spot, self.z[0].at[cut, 0, 0], self.z[1].at[cut, side, r], self.at.beside).wait_recv()

    def wait_x(self, cut, r):
        spot = self.piece(cut, 1, r)
        remote(spot, spot, self.x[0].at[cut, r], self.x[1].at[cut, r], self.at.beside).wait_recv()

    def serve(self, cut, n):
        r = self.order[n]
        if not self.is_turned(cut):
            self.wait_z(cut, 0, r)
            self.pass_on(cut, 0, r)
            self.beside(cut, r).start()
            return
        if n == 0:
            self.wait_x(cut, 0)
            self.pass_on(cut, 1, 0)
        for side in range(2):
            self.wait_z(cut, side, r)
            self.pass_on(cut, side, r)

    def arrived(self, cut):
        if not self.is_turned(cut):
            for r in range(self.at.depth):
                self.wait_x(cut, r)

    def finish(self):
        for cut in range(self.cuts):
            turned = self.is_turned(cut)
            for side in range(2 if turned else 1):
                for r in range(self.at.depth):
                    for way in range(2):
                        there, copy = self.along(cut, side, r, way)
                        pl.when(there)(copy.wait_send)
            for r in range(1 if turned else self.at.depth):
                self.beside(cut, r).wait_send()


class Total:
    @staticmethod
    def scratch(seqs, rows):
        depth, dma = seqs // 2, pltpu.SemaphoreType.DMA

        def vmem(*shape):
            return pltpu.VMEM(shape + (LANES,), F32)

        return [
            vmem(rows // 2), vmem(2, rows // 8), vmem(2, rows // 16), vmem(depth - 1, rows // 8 // depth),
            vmem(rows // 2), vmem(2, rows // 8), vmem(2, rows // 16), dma((8, 2, depth)), dma((8, 2, depth)),
        ]

    def __init__(self, at, out, own, r0, r1, r2, r3, a1, a2, a3, send, recv):
        self.at, self.out, self.own = at, out, own
        self.r0, self.r1, self.r2, self.r3, self.a1, self.a2, self.a3 = r0, r1, r2, r3, a1, a2, a3
        self.send, self.recv = send, recv
        self.rows = own.shape[0]
        self.bits = ((at.y, at.x), (at.x, at.y))
        self.peers = ((at.across, at.beside), (at.beside, at.across))

    def halved(self, n, g):
        rows = self.rows
        src = self.a1.at[pl.ds(g * (rows // 4), rows // 4)] if n == 1 else self.a2.at[g]
        size = (self.r1, self.r2)[n - 1].shape[1]
        return src, self.bits[g][n - 1], size

    def spot(self, g, level):
        at, rows = self.at, self.rows
        start = at.o * (rows // 2)
        if level > 0:
            start = start + g * (rows // 4) + self.bits[g][0] * (rows // 8)
        if level > 1:
            start = start + self.bits[g][1] * (rows // 16)
        size = (rows // 2, rows // 8, rows // 16)[level]
        return pl.ds(pl.multiple_of(start, 8), size)

    def band(self, z):
        fold = self.at.depth // 2
        return z // fold, rows_at(lax.rem(z, fold), self.r3.shape[1])

    def band_spot(self):
        at, rows = self.at, self.rows
        g, fold = at.z // (at.depth // 2), at.depth // 2
        start = at.o * (rows // 2) + g * (rows // 4) + lax.rem(at.z, fold) * self.r3.shape[1]
        start = start + (at.y + g * (at.x - at.y)) * (rows // 8) + (at.x + g * (at.y - at.x)) * (rows // 16)
        return pl.ds(pl.multiple_of(start, 8), self.r3.shape[1])

    def transfers(self, n):
        at, rows = self.at, self.rows
        plan = []
        for g in range(1 if n in (0, 3, 4, 7) else 2):
            if n == 0:
                plan.append((self.own.at[rows_at(1 - at.o, rows // 2)], self.r0, g, 0, at.side))
            elif n < 3:
                src, bit, size = self.halved(n, g)
                plan.append((src.at[rows_at(1 - bit, size)], (self.r1, self.r2)[n - 1].at[g], g, 0, self.peers[g][n - 1]))
            elif n == 3:
                for k, peer in enumerate(at.deep):
                    there = lax.rem(at.z + 1 + k, at.depth)
                    plan.append((self.a3.at[self.band(there)], self.r3.at[k], g, k, peer))
            else:
                spot = self.out.at[self.band_spot() if n == 4 else self.spot(g, 7 - n)]
                peers = at.deep if n == 4 else [at.side if n == 7 else self.peers[g][6 - n]]
                for k, peer in enumerate(peers):
                    plan.append((spot, spot, g, k, peer))
        return [remote(src, dst, self.send.at[n, g, k], self.recv.at[n, g, k], peer) for src, dst, g, k, peer in plan]

    def post(self, n):
        for copy in self.transfers(n):
            copy.start()

    def take(self, n):
        at = self.at
        for copy in self.transfers(n):
            copy.wait_recv()
        if n == 0:
            self.a1[...] = self.own[rows_at(at.o, self.rows // 2)] + self.r0[...]
        elif n < 3:
            for g in range(2):
                src, bit, size = self.halved(n, g)
                (self.a2, self.a3)[n - 1][g] = src[rows_at(bit, size)] + (self.r1, self.r2)[n - 1][g]
        elif n == 3:
            total = self.a3[self.band(at.z)]
            for k in range(at.depth - 1):
                total = total + self.r3[k]
            self.out[self.band_spot()] = total

    def step(self, n):
        self.take(n)
        self.post(n + 1)

    def finish(self):
        for n in range(8):
            for copy in self.transfers(n):
                copy.wait_send()


class Regroup:
    @staticmethod
    def scratch(seqs, chs, tokens, part):
        folds, vmem, dma = seqs // chs, pltpu.VMEM, pltpu.SemaphoreType.DMA
        n, rows = seqs // 2, tokens // seqs
        half = rows // 2
        return [
            vmem((n, rows, part), F32), vmem((n, rows, part), F32), vmem((n, half, part), BF16),
            vmem((n, half, part), BF16), vmem((n, half, part), BF16), vmem((folds, 2, half, part), BF16),
            dma((n, 3)), dma((n, 2)), dma((folds, 2)),
        ]

    @staticmethod
    def sources(at):
        folds = at.seqs // at.chs
        return [(at.c * folds + f, y * 2 + lax.rem(at.s, 2)) for f in range(folds) for y in range(2)]

    def __init__(self, at, src, r0, a1, sb, r1, fb, r2, send, recv, last):
        self.at, self.src = at, src
        self.r0, self.a1, self.sb, self.r1, self.fb, self.r2 = r0, a1, sb, r1, fb, r2
        self.send, self.recv, self.last = send, recv, last
        self.quarters, self.rows, self.half = r0.shape[0], r0.shape[1], r1.shape[1]
        self.folds = at.seqs // at.chs
        self.home, self.slot = at.s // self.folds, lax.rem(at.s, self.folds)

    def first(self, q):
        at = self.at
        src = self.src.at[rows_at(2 * q + 1 - at.o, self.rows)]
        return remote(src, self.r0.at[q], self.send.at[q, 0], self.recv.at[q, 0], at.side)

    def second(self, q):
        return remote(self.sb.at[q], self.r1.at[q], self.send.at[q, 1], self.recv.at[q, 1], self.at.across)

    def third(self, q):
        at = self.at
        dst, sem = self.r2.at[self.slot, at.y], self.last.at[self.slot, at.y]
        away = jnp.logical_or(2 * q + at.o != at.s, self.home != at.c)
        there = remote(self.fb.at[q], dst, self.send.at[q, 2], sem, (2 * q + at.o, self.home))
        return away, there, pltpu.make_async_copy(self.fb.at[q], dst, sem)

    def one(self, q):
        self.first(q).start()

    def two(self, q):
        at = self.at
        self.first(q).wait_recv()
        self.a1[q] = self.src[rows_at(2 * q + at.o, self.rows)] + self.r0[q]
        self.sb[q] = self.a1[q, rows_at(1 - at.y, self.half)].astype(BF16)
        self.second(q).start()

    def three(self, q):
        at = self.at
        self.second(q).wait_recv()
        self.fb[q] = (self.a1[q, rows_at(at.y, self.half)] + self.r1[q].astype(F32)).astype(BF16)
        away, there, here = self.third(q)
        pl.when(away)(there.start)
        pl.when(jnp.logical_not(away))(here.start)

    def result(self):
        for f in range(self.folds):
            for y in range(2):
                spot = self.r2.at[f, y]
                remote(self.fb.at[0], spot, self.send.at[0, 2], self.last.at[f, y], self.at.side).wait_recv()
        rows = [jnp.concatenate([self.r2[f, 0], self.r2[f, 1]], axis=0) for f in range(self.folds)]
        return jnp.concatenate(rows, axis=1).astype(F32)

    def finish(self):
        for q in range(self.quarters):
            self.first(q).wait_send()
            self.second(q).wait_send()
            away, there, _ = self.third(q)
            pl.when(away)(there.wait_send)


def run(count, body, events):
    def step(j, carry):
        for when, things in events.items():

            @pl.when(j == when)
            def _():
                for thing in things:
                    thing()

        body(j)
        return carry

    lax.fori_loop(0, count, step, 0)


def split(refs, *counts):
    out, start = [], 0
    for count in counts:
        out.append(refs[start : start + count])
        start += count
    return out

ANY = pl.BlockSpec(memory_space=pl.ANY)
WHOLE = pl.BlockSpec(memory_space=pltpu.VMEM)


def comm(kernel, ins, outs, scratch, ident, name, moved):
    return pl.pallas_call(
        kernel,
        out_shape=[jax.ShapeDtypeStruct(shape, dtype) for shape, dtype, _ in outs],
        in_specs=[spec for _, spec in ins],
        out_specs=[spec for _, _, spec in outs],
        scratch_shapes=scratch,
        compiler_params=pltpu.CompilerParams(
            collective_id=ident, has_side_effects=True, vmem_limit_bytes=60 * 2**20
        ),
        cost_estimate=pl.CostEstimate(flops=0, bytes_accessed=moved, transcendentals=0),
        name=name,
    )(*[array for array, _ in ins])


def per_device(
    stream, norm_gain, w_in, conv_w, conv_b, w_xdt, w_xbc, w_dt, dt_bias, a_log, d_skip, w_out,
    cotangent, seg_ids, modality,
):
    seqs, chs = lax.axis_size("seq"), lax.axis_size("ch")
    s = lax.axis_index("seq")
    rows, cols = stream.shape
    tokens, width = seg_ids.shape[0], norm_gain.shape[0]
    channels = conv_b.shape[0]
    own = channels // seqs
    part = width // seqs
    flat = tokens * STATE // LANES
    dma, vmem = pltpu.SemaphoreType.DMA, pltpu.VMEM
    segs = seg_ids.reshape(tokens // LANES, LANES)
    gain = norm_gain[None]
    xdbl, u, conv, x_pre, d_y, dt, sig, _, d_gate, hs, normed, cot, inv, wx, wdt, mod, d_skip_own, own_rows, gathered = comm(
        partial(forward_kernel, seqs, chs),
        [
            (stream, ANY), (cotangent, ANY), (w_in, ANY), (w_out, ANY), (w_xdt, ANY), (w_dt, ANY),
            (modality[None], WHOLE), (segs, WHOLE), (gain, WHOLE), (w_xbc, WHOLE), (a_log, WHOLE),
            (d_skip[None], WHOLE), (conv_b[None], WHOLE), (conv_w, WHOLE), (dt_bias, WHOLE),
        ],
        [
            ((2, tokens // 2 + flat, LANES), F32, WHOLE),
            ((tokens, own), BF16, WHOLE),
            ((tokens, own), F32, WHOLE),
            ((tokens, own), BF16, WHOLE),
            ((tokens, own), F32, WHOLE),
            ((tokens, own), F32, WHOLE),
            ((tokens, own), F32, WHOLE),
            ((tokens, own), BF16, WHOLE),
            ((tokens, own), BF16, WHOLE),
            ((tokens + 1, STATE, own), F32, ANY),
            ((tokens, part), BF16, WHOLE),
            ((tokens, part), BF16, ANY),
            ((tokens, LANES), F32, WHOLE),
            ((2, RANK, own), BF16, WHOLE),
            ((2, RANK, own), BF16, WHOLE),
            ((seqs, 8, rows), F32, WHOLE),
            ((1, own), F32, WHOLE),
            ((STATE + 8, own), F32, WHOLE),
            ((seqs, tokens, own), BF16, ANY),
        ],
        2 * Total.scratch(seqs, tokens // 2 + flat) + 2 * Spread.semaphores(seqs) + 5 * Trade.semaphores(seqs)
        + Share.semaphores(seqs, CUTS)
        + [
            vmem((seqs * chs, rows, cols), BF16), vmem((seqs * chs, rows, cols), BF16),
            vmem((2, 2, width, own), BF16), vmem((2, own, width), BF16),
            vmem((tokens, own), F32), vmem((tokens, own), F32), vmem((ROWS + 8, own), F32), vmem((ROWS, width), BF16),
            vmem((STATE, own), F32), vmem((CHUNK, own), F32), vmem((CHUNK, STATE, own), F32),
            vmem((2, CHUNK, STATE, own), F32), vmem((8, rows), F32), vmem((2, tokens // 2 + flat, LANES), F32),
            dma((3 + seqs,)),
        ],
        1, "forward", 64 << 20,
    )
    output, grad_stream, sums, own_w_in, own_w_out, small, parts = comm(
        partial(backward_kernel, seqs, chs),
        [
            (segs, WHOLE), (xdbl, WHOLE), (u, WHOLE), (conv, ANY), (x_pre, ANY), (d_y, WHOLE), (dt, WHOLE),
            (sig, WHOLE), (gathered, ANY), (d_gate, WHOLE), (hs, ANY), (normed, ANY), (cot, ANY), (inv, ANY),
            (wx, WHOLE), (wdt, WHOLE), (mod, WHOLE), (d_skip_own, WHOLE), (w_xbc, WHOLE), (own_rows, WHOLE),
            (w_in, ANY), (w_out, ANY), (gain, WHOLE), (stream, WHOLE), (cotangent, WHOLE),
        ],
        [
            ((rows, cols), BF16, WHOLE),
            ((rows, cols), F32, WHOLE),
            ((chs, 8, cols), F32, WHOLE),
            (w_in.shape, F32, ANY),
            (w_out.shape, F32, ANY),
            ((96, channels), F32, WHOLE),
            ((2, 2, RANK // seqs, channels), F32, ANY),
        ],
        2 * Total.scratch(seqs, tokens // 2 + flat) + 2 * Regroup.scratch(seqs, chs, tokens, part)
        + 2 * Share.semaphores(seqs, CUTS) + Share.semaphores(seqs, 1) + Trade.semaphores(seqs)
        + [
            vmem((2, tokens // 2 + flat, LANES), F32), vmem((tokens, own), F32), vmem((tokens, own), BF16),
            vmem((seqs, tokens, own), BF16), vmem((seqs, tokens, own), BF16), vmem((seqs, tokens, own), BF16),
            vmem((tokens, own), F32), vmem((tokens, own), BF16), vmem((tokens, part), BF16), vmem((tokens, part), BF16),
            vmem(w_in.shape, BF16), vmem(w_out.shape, BF16), vmem((rows, LANES), F32),
            vmem((tokens, part), F32), vmem((tokens, part), F32), vmem((2, CHUNK + 1, STATE, own), F32),
            vmem((STATE, own), F32), vmem((STATE, own), F32), vmem((CHUNK, own), F32), vmem((CHUNK, STATE, own), F32),
            vmem((CHUNK, STATE, own), BF16), vmem((CHUNK, STATE, own), BF16),
            vmem((ROWS + 8, own), F32), vmem((ROWS + 8, own), F32), vmem((2, 2, RANK, own), F32),
            vmem((2, 2 * STATE, own), F32), vmem((2, own), F32), vmem((8, own), F32),
            vmem((96, own), F32), vmem((seqs, 96, own), F32), vmem((8, rows), F32), vmem((chs - 1, 8, rows), F32),
            vmem((8, cols), F32), vmem((seqs - 1, 8, cols), F32),
            dma((2,)), dma((8,)), dma((chs - 1,)), dma((chs - 1,)), dma((seqs - 1,)), dma((seqs - 1,)),
            dma((chs - 1,)), dma((chs - 1,)), vmem(w_in.shape, F32), vmem(w_out.shape, F32),
            vmem((2, tokens // 2 + flat, LANES), F32), dma((3,)),
        ],
        2, "backward", 64 << 20,
    )
    shapes = [
        (1, width), conv_w.shape, (1, channels), parts.shape[1:], w_xbc.shape, parts.shape[1:], dt_bias.shape,
        a_log.shape, (1, channels), (1, 3),
    ]
    steps = 2

    def whole(shape):
        zeros = (0,) * len(shape)
        return pl.BlockSpec(shape, lambda i: zeros)

    def sliced(shape, axis):
        block = tuple(size // steps if n == axis else size for n, size in enumerate(shape))
        return pl.BlockSpec(block, lambda i: tuple(i if n == axis else 0 for n in range(len(shape))))

    large = [(output, 0), (grad_stream, 0), (own_w_in, 2), (own_w_out, 1)]
    (
        g_gain, g_conv_w, g_conv_b, g_w_xdt, g_w_xbc, g_w_dt, g_bias, g_a_log, g_skip, stats,
        output, grad_stream, own_w_in, own_w_out,
    ) = pl.pallas_call(
        unpack_kernel,
        out_shape=[jax.ShapeDtypeStruct(shape, F32) for shape in shapes]
        + [jax.ShapeDtypeStruct(array.shape, array.dtype) for array, _ in large],
        grid=(steps,),
        in_specs=[whole(array.shape) for array in (small, sums, parts)]
        + [sliced(array.shape, axis) for array, axis in large],
        out_specs=[whole(shape) for shape in shapes] + [sliced(array.shape, axis) for array, axis in large],
        compiler_params=pltpu.CompilerParams(dimension_semantics=("arbitrary",), vmem_limit_bytes=60 * 2**20),
        name="unpack",
    )(small, sums, parts, *[array for array, _ in large])
    return (
        output, grad_stream, g_gain[0], own_w_in, g_conv_w, g_conv_b[0], g_w_xdt, g_w_xbc, g_w_dt, g_bias,
        g_a_log, g_skip[0], own_w_out, stats[0],
    )


def per_device_by_token(
    stream,
    norm_gain,
    w_in,
    conv_w,
    conv_b,
    w_xdt,
    w_xbc,
    w_dt,
    dt_bias,
    a_log,
    d_skip,
    w_out,
    cotangent,
    seg_ids,
    modality,
):
    length = stream.shape[0]
    channels = conv_b.shape[0]
    model_width = norm_gain.shape[0]
    mod_count = w_in.shape[0]
    rim_len = CONV - 1
    ch_start = lax.axis_index("ch") * channels
    col_start = lax.axis_index("ch") * stream.shape[1]
    x_full, grad_full = (
        lax.all_gather(stream, "ch", axis=1, tiled=True),
        lax.all_gather(cotangent, "ch", axis=1, tiled=True),
    )
    w_in_full, w_xdt_full, w_dt_full, w_out_full = (
        lax.all_gather(w_in, "seq", axis=2, tiled=True),
        lax.all_gather(w_xdt, "seq", axis=1, tiled=True),
        lax.all_gather(w_dt, "seq", axis=1, tiled=True),
        lax.all_gather(w_out, "seq", axis=2, tiled=True),
    )
    mod_mask = modality[None, :] == jnp.arange(mod_count, dtype=jnp.int32)[:, None]
    mod_float = mod_mask.astype(jnp.float32)

    def by_mod(value):
        chosen = mod_mask.reshape(mod_mask.shape + (1,) * (value.ndim - 1))
        return jnp.where(chosen, value[None], jnp.zeros((), value.dtype))

    stream_f = x_full.astype(jnp.float32)
    inv_rms = lax.rsqrt(jnp.mean(stream_f * stream_f, axis=1, keepdims=True) + EPSILON)
    x_hat = stream_f * inv_rms
    normed = (x_hat * norm_gain[None, :]).astype(jnp.bfloat16)
    normed_split = by_mod(normed)
    projected = jnp.einsum(
        "mtd,mkde->tke", normed_split, w_in_full, preferred_element_type=jnp.float32
    )
    x_pre = projected[:, 0].astype(jnp.bfloat16)
    gate_in = projected[:, 1]
    rim_rows = passed_along(x_pre[length - rim_len :], "seq", 1)
    padded_seg = jnp.concatenate([jnp.full((rim_len,), -1, jnp.int32), seg_ids])
    seg_win = lax.dynamic_slice_in_dim(padded_seg, lax.axis_index("seq") * length, length + rim_len)
    seg_now = seg_win[rim_len:]
    extended = jnp.concatenate([rim_rows, x_pre], 0).astype(jnp.float32)
    tap_mask = [
        (seg_win[offset : offset + length] == seg_now).astype(jnp.float32)[:, None]
        for offset in range(CONV)
    ]
    conv_out = conv_b[None, :] + sum(
        (
            conv_w[offset][None, :] * extended[offset : offset + length] * tap_mask[offset]
            for offset in range(CONV)
        )
    )
    u_val = (conv_out * jax.nn.sigmoid(conv_out)).astype(jnp.bfloat16)
    u_split = by_mod(u_val)
    dt_part = jnp.einsum("mte,mre->tr", u_split, w_xdt_full, preferred_element_type=jnp.float32)
    bc_part = jnp.einsum("mte,mne->tn", u_split, w_xbc, preferred_element_type=jnp.float32)
    dt_sum, bc_sum = lax.psum((dt_part, bc_part), "ch")
    dt_low = dt_sum.astype(jnp.bfloat16)
    b_in = bc_sum[:, :STATE]
    c_out = bc_sum[:, STATE:]
    low_split = by_mod(dt_low)
    dt_raw = jnp.einsum(
        "mtr,mre->te", low_split, w_dt_full, preferred_element_type=jnp.float32
    ) + jnp.dot(mod_float.T, dt_bias, precision=PRECISE)
    dt_val = jax.nn.softplus(dt_raw)
    u_float = u_val.astype(jnp.float32)
    dt_u = dt_val * u_float
    neg_a = -jnp.exp(a_log)
    keep_mask = (seg_now == seg_win[rim_len - 1 : rim_len - 1 + length]).astype(jnp.float32)
    decay_all = jnp.exp(neg_a * jnp.sum(dt_val, axis=0)[None, :]) * jnp.prod(keep_mask)
    zero_state = jnp.zeros_like(neg_a)
    local_end, _, _ = run_forward(zero_state, dt_val, dt_u, b_in, c_out, keep_mask, neg_a)
    _, start_state = entering(
        (decay_all, local_end), "seq", chain_link, (jnp.ones_like(neg_a), zero_state), False
    )
    _, starts, y_ssm = run_forward(start_state, dt_val, dt_u, b_in, c_out, keep_mask, neg_a)
    y_val = y_ssm + d_skip[None, :] * u_float
    sig_gate = jax.nn.sigmoid(gate_in)
    gated = (y_val * (gate_in * sig_gate)).astype(jnp.bfloat16)
    gated_split = by_mod(gated)
    branch = lax.psum_scatter(
        jnp.einsum("mte,med->dt", gated_split, w_out_full, preferred_element_type=jnp.float32),
        "ch",
        scatter_dimension=0,
        tiled=True,
    ).T
    x_own = stream.astype(jnp.float32)
    mixed = x_own + branch
    output = mixed.astype(jnp.bfloat16)
    stats_part = jnp.stack(
        [jnp.sum(x_own * x_own), jnp.sum(branch * branch), jnp.sum(mixed * mixed)]
    )
    grad_split = by_mod(grad_full)
    d_gated = jnp.einsum("mtd,med->te", grad_split, w_out_full, preferred_element_type=jnp.float32)
    d_w_out = jnp.einsum("mte,td->med", gated_split, grad_full, preferred_element_type=jnp.float32)
    d_y = d_gated * gate_in * sig_gate
    d_gate = d_gated * y_val * silu_grad(gate_in)
    d_skip_part = jnp.sum(d_y * u_float, axis=0)
    local_back = local_adjoint(dt_val, c_out, keep_mask, d_y, neg_a)
    _, incoming = entering(
        (decay_all, local_back), "seq", chain_link, (jnp.ones_like(neg_a), zero_state), True
    )
    d_neg, d_dt_ssm, d_dtu, d_b, d_c = run_adjoint(
        incoming, starts, dt_val, dt_u, b_in, c_out, keep_mask, d_y, neg_a
    )
    d_a_log = d_neg * neg_a
    d_dt = d_dt_ssm + d_dtu * u_float
    d_u = d_y * d_skip[None, :] + d_dtu * dt_val
    d_raw = (d_dt * jax.nn.sigmoid(dt_raw)).astype(jnp.bfloat16)
    d_w_dt = jnp.einsum("mtr,te->mre", low_split, d_raw, preferred_element_type=jnp.float32)
    d_dt_bias = jnp.dot(mod_float, d_raw.astype(jnp.float32), precision=PRECISE)
    d_low_part = jnp.einsum(
        "mte,mre->tr", by_mod(d_raw), w_dt_full, preferred_element_type=jnp.float32
    )
    d_bc_part = jnp.concatenate([d_b, d_c], 1)
    d_low_sum, d_bc_sum = lax.psum((d_low_part, d_bc_part), "ch")
    d_low = d_low_sum.astype(jnp.bfloat16)
    d_bc = d_bc_sum.astype(jnp.bfloat16)
    d_w_xdt = jnp.einsum("mte,tr->mre", u_split, d_low, preferred_element_type=jnp.float32)
    d_w_xbc = jnp.einsum("mte,tn->mne", u_split, d_bc, preferred_element_type=jnp.float32)
    d_u = d_u + jnp.einsum(
        "mtr,mre->te", by_mod(d_low), w_xdt_full, preferred_element_type=jnp.float32
    )
    d_u = d_u + jnp.einsum("mtn,mne->te", by_mod(d_bc), w_xbc, preferred_element_type=jnp.float32)
    d_conv = d_u * silu_grad(conv_out)
    d_conv_b = jnp.sum(d_conv, axis=0)
    d_conv_w = jnp.stack(
        [
            jnp.sum(d_conv * extended[offset : offset + length] * tap_mask[offset], axis=0)
            for offset in range(CONV)
        ]
    )
    d_ext = sum(
        (
            jnp.pad(
                conv_w[offset][None, :] * d_conv * tap_mask[offset],
                ((offset, rim_len - offset), (0, 0)),
            )
            for offset in range(CONV)
        )
    )
    back_rim = passed_along(d_ext[:rim_len], "seq", -1)
    d_pre = d_ext[rim_len:] + jnp.pad(back_rim, ((length - rim_len, 0), (0, 0)))
    d_xz = jnp.stack([d_pre, d_gate], 1).astype(jnp.bfloat16)
    d_w_in = jnp.einsum("mtd,tke->mkde", normed_split, d_xz, preferred_element_type=jnp.float32)
    d_norm_part = jnp.einsum(
        "mtke,mkde->dt", by_mod(d_xz), w_in_full, preferred_element_type=jnp.float32
    )
    d_gain_part = jnp.einsum("dt,td->d", d_norm_part, x_hat, precision=PRECISE)
    d_norm = lax.psum(d_norm_part, "ch").T
    d_hat = d_norm * norm_gain[None, :]
    inner_dot = jnp.mean(d_hat * x_hat, axis=1, keepdims=True)
    d_x_full = inv_rms * (d_hat - x_hat * inner_dot)
    grad_stream = lax.dynamic_slice_in_dim(
        d_x_full, col_start, stream.shape[1], 1
    ) + cotangent.astype(jnp.float32)
    own_w_in, own_w_xdt, own_w_dt, own_w_out = (
        lax.psum_scatter(d_w_in, "seq", scatter_dimension=2, tiled=True),
        lax.psum_scatter(d_w_xdt, "seq", scatter_dimension=1, tiled=True),
        lax.psum_scatter(d_w_dt, "seq", scatter_dimension=1, tiled=True),
        lax.psum_scatter(d_w_out, "seq", scatter_dimension=2, tiled=True),
    )

    def spread(value):
        full_shape = value.shape[:-1] + (INNER,)
        return lax.dynamic_update_slice_in_dim(
            jnp.zeros(full_shape, jnp.float32), value, ch_start, value.ndim - 1
        )

    def own_slice(value):
        return lax.dynamic_slice_in_dim(value, ch_start, channels, value.ndim - 1)

    summed = lax.psum(
        (
            spread(d_conv_w),
            spread(d_conv_b),
            spread(d_w_xbc),
            spread(d_dt_bias),
            spread(d_a_log),
            spread(d_skip_part),
            d_gain_part,
            stats_part,
        ),
        ("seq", "ch"),
    )
    stats = jnp.sqrt(summed[7] / float(length * lax.axis_size("seq") * model_width))
    return (
        output,
        grad_stream,
        summed[6],
        own_w_in,
        own_slice(summed[0]),
        own_slice(summed[1]),
        own_w_xdt,
        own_slice(summed[2]),
        own_w_dt,
        own_slice(summed[3]),
        own_slice(summed[4]),
        own_slice(summed[5]),
        own_w_out,
        stats,
    )


def solution(mesh):
    in_specs = (
        P("seq", "ch"),
        P(),
        P(None, None, "seq", "ch"),
        P(None, "ch"),
        P("ch"),
        P(None, "seq", "ch"),
        P(None, None, "ch"),
        P(None, "seq", "ch"),
        P(None, "ch"),
        P(None, "ch"),
        P("ch"),
        P(None, "ch", "seq"),
        P("seq", "ch"),
        P(),
        P("seq"),
    )
    out_specs = (
        P("seq", "ch"),
        P("seq", "ch"),
        P(),
        P(None, None, "seq", "ch"),
        P(None, "ch"),
        P("ch"),
        P(None, "seq", "ch"),
        P(None, None, "ch"),
        P(None, "seq", "ch"),
        P(None, "ch"),
        P(None, "ch"),
        P("ch"),
        P(None, "ch", "seq"),
        P(),
    )
    seqs, chs = mesh.shape["seq"], mesh.shape["ch"]
    whole_lanes = INNER == seqs * chs * LANES and seqs == 2 * chs and chs == 4
    return jax.shard_map(
        per_device if whole_lanes else per_device_by_token, mesh=mesh, in_specs=in_specs, out_specs=out_specs, check_vma=False
    )
```
